32 devices in a mesh: dp: 4 (over z), seq: 2 (over y), mp: 4 (over x, core).
Axes of the slice: x: 2, y: 2, z: 4, core: 2. Of those that a mesh axis runs over, the one named last changes fastest.
Arguments:
- hidden_in: bfloat16 [4, 1024, 768], P('dp', 'seq', 'mp'), may hold values from -6 to 6
- cotangent: bfloat16 [4, 1024, 768], P('dp', 'seq', 'mp'), may hold values from -6 to 6
- attention_gain: float32 [768], replicated, may hold values from 0.1 to 1.9
- feedforward_gain: float32 [768], replicated, may hold values from 0.1 to 1.9
- qkv_weight: bfloat16 [768, 3, 768], P(None, None, 'mp'), may hold values from -0.21875 to 0.21875
- attention_out: bfloat16 [768, 768], P('mp'), may hold values from -0.75 to 0.75
- geglu_in: bfloat16 [768, 2, 1152], P(None, None, 'mp'), may hold values from -0.21875 to 0.21875
- geglu_out: bfloat16 [1152, 768], P('mp'), may hold values from -0.1875 to 0.1875
Outputs:
- layer_out: float32 [4, 1024, 768], P('dp', 'seq', 'mp')
- grad_input: float32 [4, 1024, 768], P('dp', 'seq', 'mp')
- grad_qkv: float32 [768, 3, 768], P(None, None, 'mp')
- grad_attention_out: float32 [768, 768], P('mp')
- grad_geglu_in: float32 [768, 2, 1152], P(None, None, 'mp')
- grad_geglu_out: float32 [1152, 768], P('mp')
- grad_attention_gain: float32 [768], P('mp')
- grad_feedforward_gain: float32 [768], P('mp')
The draws below stay inside these ranges and needn't reach their ends.
All inputs are finite; a program needn't handle non-finite values.
Results may differ from the reference program's by a relative error of at most 0.018.
Values may be sent and summed in bfloat16 or wider, within the bound.
No kernel may reach another device: no remote copies, remote signals or barrier semaphores. Data moves between devices by JAX's collectives and lax.ppermute only.
A program may use at most 64 MiB of HBM per device.

```python
import math
import jax
import jax.numpy as jnp
from jax import lax

D = 768
HEADS = 12
HEAD = 64
FF = 1152
HALF = 64
TB = 512
SEQS = 4
LEN = 1024


def steps_of(own_key, extent, split, low, high):
    def one(axis_at, parts):
        steps = jax.random.uniform(jax.random.fold_in(jax.random.fold_in(own_key, 6), axis_at), (parts,), jnp.float32, low / len(split), high / len(split))
        return jnp.repeat(jnp.exp(steps), extent[axis_at] // parts).reshape((-1,) + (1,) * (len(extent) - axis_at - 1))

    loudness = one(*split[0])
    for cut in split[1:]:
        loudness = loudness * one(*cut)
    return loudness


def gaussian(rng, shape, spread, bound, pieces=(), held_as=jnp.bfloat16):
    values = jax.random.normal(rng, shape, jnp.float32) * spread
    if len(pieces) > 0:
        values = steps_of(rng, shape, pieces, -0.22, 0.18) * values
    return jnp.clip(values, min=-bound, max=bound).astype(held_as)


def setup_inputs(seed: int = 0) -> dict:
    streams_of = jax.random.split(jax.random.key(seed), 9)
    hidden_in = gaussian(streams_of[0], (SEQS, LEN, D), 1.0, 6.0, ((0, 4), (1, 2), (2, 4)))
    cotangent = gaussian(streams_of[1], (SEQS, LEN, D), 1.0, 6.0, ((0, 4), (1, 2), (2, 4)))
    attention_gain = jnp.clip(1.0 + 0.18 * jax.random.normal(streams_of[2], (D,), jnp.float32), 0.1, 1.9)
    feedforward_gain = jnp.clip(1.0 + 0.18 * jax.random.normal(streams_of[3], (D,), jnp.float32), 0.1, 1.9)
    qkv_weight = gaussian(streams_of[4], (D, 3, HEADS * HEAD), D ** -0.5, 0.21875, ((2, 4),))
    attention_out = gaussian(streams_of[5], (HEADS * HEAD, D), (HEADS * HEAD // 12) ** -0.5, 0.75, ((0, 4),))
    geglu_in = gaussian(streams_of[6], (D, 2, FF), D ** -0.5, 0.21875, ((2, 4),))
    geglu_out = gaussian(streams_of[7], (FF, D), FF ** -0.5, 0.1875, ((0, 4),))
    return dict(hidden_in=hidden_in, cotangent=cotangent, attention_gain=attention_gain, feedforward_gain=feedforward_gain, qkv_weight=qkv_weight, attention_out=attention_out, geglu_in=geglu_in, geglu_out=geglu_out)


def normalize(rows):
    center = rows - lax.optimization_barrier(jnp.mean(rows, axis=-1, keepdims=True))
    inverse = lax.rsqrt(lax.optimization_barrier(jnp.mean(center * center, axis=-1, keepdims=True)) + 1e-05)
    return (center * inverse, inverse)

def norm_back(dhat, normed, inverse):
    first = lax.optimization_barrier(jnp.mean(dhat, axis=-1, keepdims=True))
    second = lax.optimization_barrier(jnp.mean(dhat * normed, axis=-1, keepdims=True))
    return inverse * (dhat - first - normed * second)

def frequencies(positions):
    inverse_freq = jnp.exp(jnp.arange(HEAD // 2).astype(jnp.float32) * (-2.0 * math.log(10000.0) / HEAD))
    angles = positions[:, None] * inverse_freq[None, :]
    angles = jnp.concatenate([angles, angles], axis=-1)
    return (jnp.cos(angles), jnp.sin(angles))

def rotate(tensor, cosine, sine):
    halfway = HEAD // 2
    turned = jnp.concatenate([-tensor[..., halfway:], tensor[..., :halfway]], axis=-1)
    return tensor * cosine[:, None, :] + turned * sine[:, None, :]

def gelu_exact(value):
    return 0.5 * value * (1.0 + lax.erf(value * 0.7071067811865476))

def gelu_slope(value):
    return 0.5 * (1.0 + lax.erf(value * 0.7071067811865476)) + value * jnp.exp(-0.5 * value * value) * 0.3989422804014327

def block_scores(queries, keys_wide, query_pos, key_pos, length):
    scores = jnp.einsum('qhd,khd->hqk', queries.astype(jnp.float32), keys_wide.astype(jnp.float32)) * HEAD ** (-0.5)
    allowed = (jnp.abs(query_pos[:, None] - key_pos[None, :]) <= HALF) & (key_pos >= 0)[None, :] & (key_pos < length)[None, :]
    return jnp.where(allowed[None], scores, -1e+30)

def one_sequence(inputs, upstream, attention_gain, feedforward_gain, qkv_weight, attention_out, geglu_in, geglu_out):
    length = inputs.shape[0]
    columns = HEADS * HEAD
    blocks = length // TB
    span = TB + 2 * HALF
    inputs_f = inputs.astype(jnp.float32)
    normed_one, inverse_one = normalize(inputs_f)
    fed_one = (normed_one * attention_gain).astype(jnp.bfloat16)
    flat_qkv = qkv_weight.reshape(D, 3 * columns)
    projected = jnp.dot(fed_one, flat_qkv, preferred_element_type=jnp.float32).reshape(length, 3, HEADS, HEAD)
    cosine, sine = frequencies(jnp.arange(length, dtype=jnp.int32).astype(jnp.float32))
    queries = rotate(projected[:, 0], cosine, sine).astype(jnp.bfloat16)
    keys = rotate(projected[:, 1], cosine, sine).astype(jnp.bfloat16)
    values = projected[:, 2].astype(jnp.bfloat16)
    keys_pad = jnp.pad(keys, ((HALF, HALF), (0, 0), (0, 0)))
    values_pad = jnp.pad(values, ((HALF, HALF), (0, 0), (0, 0)))

    def positions(index):
        start = (index * TB).astype(jnp.int32)
        query_pos = start + jnp.arange(TB, dtype=jnp.int32)
        key_pos = start - HALF + jnp.arange(span, dtype=jnp.int32)
        return (start, query_pos, key_pos)

    def forward_block(carry, index):
        start, query_pos, key_pos = positions(index)
        query_blk = lax.dynamic_slice_in_dim(queries, start, TB, 0)
        key_blk = lax.dynamic_slice_in_dim(keys_pad, start, span, 0)
        value_blk = lax.dynamic_slice_in_dim(values_pad, start, span, 0)
        scores = block_scores(query_blk, key_blk, query_pos, key_pos, length)
        top = lax.optimization_barrier(jnp.max(scores, axis=-1, keepdims=True))
        log_total = top + jnp.log(lax.optimization_barrier(jnp.sum(jnp.exp(scores - top), axis=-1, keepdims=True)))
        weights = jnp.exp(scores - log_total).astype(jnp.bfloat16)
        mixed = jnp.einsum('hqk,khd->qhd', weights.astype(jnp.float32), value_blk.astype(jnp.float32)).astype(jnp.bfloat16)
        return (carry, (mixed, log_total))
    indices = jnp.arange(blocks, dtype=jnp.int32)
    unused, (mixed_all, totals) = lax.scan(forward_block, jnp.float32(0.0), indices)
    mixed = mixed_all.reshape(length, HEADS, HEAD)
    joined = mixed.reshape(length, columns)
    middle = inputs_f + jnp.dot(joined, attention_out, preferred_element_type=jnp.float32)
    normed_two, inverse_two = normalize(middle)
    fed_two = (normed_two * feedforward_gain).astype(jnp.bfloat16)
    flat_in = geglu_in.reshape(D, 2 * FF)
    lifted = jnp.dot(fed_two, flat_in, preferred_element_type=jnp.float32)
    linear = lifted[:, :FF]
    gating = lifted[:, FF:]
    activated = gelu_exact(linear)
    product = (activated * gating).astype(jnp.bfloat16)
    layer_out = middle + jnp.dot(product, geglu_out, preferred_element_type=jnp.float32)
    grad_geglu_out = jnp.dot(product.T, upstream, preferred_element_type=jnp.float32)
    grad_product = jnp.dot(upstream, geglu_out.T, preferred_element_type=jnp.float32)
    grad_linear = grad_product * gating * gelu_slope(linear)
    grad_gating = grad_product * activated
    grad_lifted = jnp.concatenate([grad_linear, grad_gating], axis=1).astype(jnp.bfloat16)
    grad_geglu_in = jnp.dot(fed_two.T, grad_lifted, preferred_element_type=jnp.float32).reshape(D, 2, FF)
    grad_fed_two = jnp.dot(grad_lifted, flat_in.T, preferred_element_type=jnp.float32)
    grad_ff_gain = lax.optimization_barrier(jnp.sum(grad_fed_two * normed_two, axis=0))
    grad_middle = upstream.astype(jnp.float32) + norm_back(grad_fed_two * feedforward_gain, normed_two, inverse_two)
    grad_middle_low = grad_middle.astype(jnp.bfloat16)
    grad_attention_out = jnp.dot(joined.T, grad_middle_low, preferred_element_type=jnp.float32)
    grad_mixed = jnp.dot(grad_middle_low, attention_out.T, preferred_element_type=jnp.float32).astype(jnp.bfloat16).reshape(length, HEADS, HEAD)

    def backward_block(carry, index):
        key_grads, value_grads = carry
        start, query_pos, key_pos = positions(index)
        query_blk = lax.dynamic_slice_in_dim(queries, start, TB, 0)
        key_blk = lax.dynamic_slice_in_dim(keys_pad, start, span, 0)
        value_blk = lax.dynamic_slice_in_dim(values_pad, start, span, 0)
        mixed_blk = lax.dynamic_slice_in_dim(mixed, start, TB, 0)
        grad_blk = lax.dynamic_slice_in_dim(grad_mixed, start, TB, 0)
        log_total = totals[index]
        scores = block_scores(query_blk, key_blk, query_pos, key_pos, length)
        probs = jnp.exp(scores - log_total)
        weights = probs.astype(jnp.bfloat16)
        delta = lax.optimization_barrier(jnp.sum(grad_blk.astype(jnp.float32) * mixed_blk.astype(jnp.float32), axis=-1)).T
        value_part = jnp.einsum('hqk,qhd->khd', weights.astype(jnp.float32), grad_blk.astype(jnp.float32))
        grad_probs = jnp.einsum('qhd,khd->hqk', grad_blk.astype(jnp.float32), value_blk.astype(jnp.float32))
        grad_scores = (probs * (grad_probs - delta[:, :, None]) * HEAD ** (-0.5)).astype(jnp.bfloat16)
        query_part = jnp.einsum('hqk,khd->qhd', grad_scores.astype(jnp.float32), key_blk.astype(jnp.float32))
        key_part = jnp.einsum('hqk,qhd->khd', grad_scores.astype(jnp.float32), query_blk.astype(jnp.float32))
        old_keys = lax.dynamic_slice_in_dim(key_grads, start, span, 0)
        old_values = lax.dynamic_slice_in_dim(value_grads, start, span, 0)
        key_grads = lax.dynamic_update_slice_in_dim(key_grads, old_keys + key_part, start, 0)
        value_grads = lax.dynamic_update_slice_in_dim(value_grads, old_values + value_part, start, 0)
        return ((key_grads, value_grads), query_part)
    empty = jnp.zeros((length + 2 * HALF, HEADS, HEAD), jnp.float32)
    (key_grads, value_grads), query_grads = lax.scan(backward_block, (empty, empty), indices)
    grad_queries = rotate(query_grads.reshape(length, HEADS, HEAD), cosine, -sine)
    grad_keys = rotate(key_grads[HALF:HALF + length], cosine, -sine)
    grad_values = value_grads[HALF:HALF + length]
    grad_projected = jnp.stack([grad_queries, grad_keys, grad_values], axis=1).reshape(length, 3 * columns).astype(jnp.bfloat16)
    grad_qkv = jnp.dot(fed_one.T, grad_projected, preferred_element_type=jnp.float32).reshape(D, 3, columns)
    grad_fed_one = jnp.dot(grad_projected, flat_qkv.T, preferred_element_type=jnp.float32)
    grad_attn_gain = lax.optimization_barrier(jnp.sum(grad_fed_one * normed_one, axis=0))
    grad_input = grad_middle + norm_back(grad_fed_one * attention_gain, normed_one, inverse_one)
    grads = (grad_qkv, grad_attention_out, grad_geglu_in, grad_geglu_out, grad_attn_gain, grad_ff_gain)
    return (layer_out, grad_input, grads)

def reference(hidden_in, cotangent, attention_gain, feedforward_gain, qkv_weight, attention_out, geglu_in, geglu_out):

    def per_sequence(carry, pair):
        inputs, upstream = pair
        layer_out, grad_input, grads = one_sequence(inputs, upstream, attention_gain, feedforward_gain, qkv_weight, attention_out, geglu_in, geglu_out)
        carry = tuple((total + piece for total, piece in zip(carry, grads)))
        return (carry, (layer_out, grad_input))
    initial = (jnp.zeros((D, 3, HEADS * HEAD), jnp.float32), jnp.zeros((HEADS * HEAD, D), jnp.float32), jnp.zeros((D, 2, FF), jnp.float32), jnp.zeros((FF, D), jnp.float32), jnp.zeros((D,), jnp.float32), jnp.zeros((D,), jnp.float32))
    sums, (outputs, input_grads) = lax.scan(per_sequence, initial, (hidden_in, cotangent))
    return (outputs, input_grads, sums[0], sums[1], sums[2], sums[3], sums[4], sums[5])
```

```python
import functools
import math

import jax
import jax.numpy as jnp
from jax import lax
from jax.experimental import pallas as pl
from jax.experimental.pallas import tpu as pltpu
from jax.sharding import PartitionSpec as P

HEAD = 64
HALF = 64
TILE = 2 * HALF
STEP = 64
F32 = jnp.float32
BF16 = jnp.bfloat16


def call(kernel, outs, scratch, *args):
    return pl.pallas_call(
        kernel,
        out_shape=tuple(jax.ShapeDtypeStruct(s, t) for s, t in outs),
        scratch_shapes=[pltpu.VMEM(s, t) for s, t in scratch],
        compiler_params=pltpu.CompilerParams(vmem_limit_bytes=56 * 1024 * 1024),
    )(*args)


def nn(a, b):
    return lax.dot_general(a, b, (((1,), (0,)), ((), ())), preferred_element_type=F32)


def tn(a, b):
    return lax.dot_general(a, b, (((0,), (0,)), ((), ())), preferred_element_type=F32)


def nt(a, b):
    return lax.dot_general(a, b, (((1,), (1,)), ((), ())), preferred_element_type=F32)


def row_loop(rows, step, fn, init):
    def one(i, carry):
        return fn(pl.multiple_of(i * step, step), carry)

    return lax.fori_loop(0, rows // step, one, init)


def fold(x):
    return jnp.sum(x.reshape(x.shape[0] // 8, 8, x.shape[1]), axis=0)


def allowed_of(first, tile, total):
    shape = (2 * TILE, TILE)
    key = lax.broadcasted_iota(jnp.int32, shape, 0)
    query = lax.broadcasted_iota(jnp.int32, shape, 1)
    gap = key - query
    position = key + (first + tile * TILE - HALF)
    return (gap >= 0) & (gap <= TILE) & (position >= 0) & (position < total)


def gather_rows(pieces, target, lanes):
    me = lax.axis_index("mp")
    share = pieces[0].shape[0]
    for k, piece in enumerate(pieces):
        start = pl.multiple_of(jnp.bitwise_xor(me, k) * share, share)
        target[pl.ds(start, share), lanes] = piece[...]


def split_half(source, keep, send, index):
    rows = keep.shape[0]

    def one(r, carry):
        mine = pl.multiple_of(index * rows + r, 16)
        other = pl.multiple_of((1 - index) * rows + r, 16)
        keep[pl.ds(r, 16), :] = source[pl.ds(mine, 16), :]
        send[pl.ds(r, 16), :] = source[pl.ds(other, 16), :].astype(send.dtype)
        return carry

    row_loop(rows, 16, one, 0)


def split_shards(source, keep, send, core):
    share = keep.shape[1]
    for x in range(2):
        mine = pl.multiple_of((2 * x + core) * share, share)
        other = pl.multiple_of((2 * x + 1 - core) * share, share)
        keep[x] = source[pl.ds(mine, share), :]
        send[x] = source[pl.ds(other, share), :].astype(send.dtype)


def attention_kernel(
    p0, p1, p2, p3, h0, h1, h2, h3, gain, w, wo, cos, sin,
    xall, stats, fed, q, kw, vw, totals, mixed, keep, send,
    proj, terms,
):
    width, tokens = xall.shape
    length = q.shape[1]
    columns = q.shape[0]
    heads = columns // HEAD
    core = lax.axis_index("mp") % 2
    first = lax.axis_index("seq") * length
    total = lax.axis_size("seq") * length
    gather_rows((p0, p1, p2, p3), xall, slice(0, length))
    gather_rows((h0, h1, h2, h3), xall, slice(length, tokens))

    def add(r, acc):
        return acc + fold(xall[pl.ds(r, STEP), :].astype(F32))

    zero = jnp.zeros((8, tokens), F32)
    mean = jnp.sum(row_loop(width, STEP, add, zero), axis=0, keepdims=True) / width

    def add_square(r, acc):
        center = xall[pl.ds(r, STEP), :].astype(F32) - mean
        return acc + fold(center * center)

    var = jnp.sum(row_loop(width, STEP, add_square, zero), axis=0, keepdims=True) / width
    inverse = lax.rsqrt(var + 1e-05)
    stats[0:1, :] = mean
    stats[1:2, :] = inverse
    stats[2:8, :] = jnp.zeros((6, tokens), F32)

    def feed(r, carry):
        normed = (xall[pl.ds(r, STEP), :].astype(F32) - mean) * inverse
        fed[pl.ds(r, STEP), :] = (normed * gain[pl.ds(r, STEP), :]).astype(BF16)
        return carry

    row_loop(width, STEP, feed, 0)
    proj[...] = nn(w[...], fed[...])
    half = HEAD // 2

    def rope(row, lanes):
        a = proj[pl.ds(row, half), lanes]
        b = proj[pl.ds(row + half, half), lanes]
        c = cos[:, lanes]
        s = sin[:, lanes]
        return a * c - b * s, b * c + a * s

    def one_head(h, carry):
        row = pl.multiple_of(h * HEAD, HEAD)
        own = slice(0, length)
        every = slice(0, tokens)
        upper, lower = rope(row, own)
        q[pl.ds(row, half), :] = upper.astype(BF16)
        q[pl.ds(row + half, half), :] = lower.astype(BF16)
        upper, lower = rope(columns + row, every)
        kw[pl.ds(row, half), :] = pltpu.roll(upper, HALF, 1).astype(BF16)
        kw[pl.ds(row + half, half), :] = pltpu.roll(lower, HALF, 1).astype(BF16)
        value = proj[pl.ds(2 * columns + row, HEAD), :]
        vw[pl.ds(row, HEAD), :] = pltpu.roll(value, HALF, 1).astype(BF16)
        for j in range(length // TILE):
            wide = slice(j * TILE, (j + 2) * TILE)
            mine = slice(j * TILE, (j + 1) * TILE)
            scores = tn(kw[pl.ds(row, HEAD), wide], q[pl.ds(row, HEAD), mine]) * HEAD**-0.5
            scores = jnp.where(allowed_of(first, j, total), scores, -1e30)
            top = jnp.max(scores, axis=0, keepdims=True)
            log_total = top + jnp.log(jnp.sum(jnp.exp(scores - top), axis=0, keepdims=True))
            weights = jnp.exp(scores - log_total).astype(BF16)
            totals[h, 0:1, mine] = log_total
            mixed[pl.ds(row, HEAD), mine] = nn(vw[pl.ds(row, HEAD), wide], weights).astype(BF16)
        return carry

    lax.fori_loop(0, heads, one_head, 0)
    terms[...] = tn(wo[...], mixed[...])
    split_half(terms, keep, send, core)


def geglu_kernel(
    xall, mine, other, u0, u1, u2, u3, gain, win, gout,
    middle_own, normed, inverse_out, fed, upstream, product, lifted_grad, keep, send,
    middle, lifted, grad_product, terms,
):
    width, length = normed.shape
    share = middle_own.shape[0]
    units = product.shape[0]
    rows = mine.shape[0]
    me = lax.axis_index("mp")
    core = me % 2
    gather_rows((u0, u1, u2, u3), upstream, slice(0, length))
    own = slice(0, length)

    def add(r, acc):
        for part, index in ((mine, core), (other, 1 - core)):
            at = pl.multiple_of(index * rows + r, STEP)
            value = xall[pl.ds(at, STEP), own].astype(F32) + part[pl.ds(r, STEP), :].astype(F32)
            middle[pl.ds(at, STEP), :] = value
            acc = acc + fold(value)
        return acc

    zero = jnp.zeros((8, length), F32)
    mean = jnp.sum(row_loop(rows, STEP, add, zero), axis=0, keepdims=True) / width

    def add_square(r, acc):
        center = middle[pl.ds(r, STEP), :] - mean
        return acc + fold(center * center)

    var = jnp.sum(row_loop(width, STEP, add_square, zero), axis=0, keepdims=True) / width
    inverse = lax.rsqrt(var + 1e-05)
    inverse_out[...] = jnp.broadcast_to(inverse, inverse_out.shape)

    def feed(r, carry):
        value = (middle[pl.ds(r, STEP), :] - mean) * inverse
        normed[pl.ds(r, STEP), :] = value
        fed[pl.ds(r, STEP), :] = (value * gain[pl.ds(r, STEP), :]).astype(BF16)
        return carry

    row_loop(width, STEP, feed, 0)
    middle_own[...] = middle[pl.ds(pl.multiple_of(me * share, share), share), :]
    lifted[...] = nn(win[...], fed[...])
    grad_product[...] = nn(gout[...], upstream[...])

    def unit(r, carry):
        at = pl.ds(r, 32)
        gate = pl.ds(pl.multiple_of(units + r, 32), 32)
        linear = lifted[at, :]
        gating = lifted[gate, :]
        grad = grad_product[at, :]
        area = 0.5 * (1.0 + lax.erf(linear * 0.7071067811865476))
        activated = linear * area
        slope = area + linear * jnp.exp(-0.5 * linear * linear) * 0.3989422804014327
        product[at, :] = (activated * gating).astype(BF16)
        lifted_grad[at, :] = (grad * gating * slope).astype(BF16)
        lifted_grad[gate, :] = (grad * activated).astype(BF16)
        return carry

    row_loop(units, 32, unit, 0)
    terms[...] = tn(win[...], lifted_grad[...])
    split_half(terms, keep, send, core)


def geglu_weights_kernel(product, lifted_grad, fed, upstream, gout, *rest, cuts):
    outs, (terms, stack) = rest[:-2], rest[-2:]
    core = lax.axis_index("mp") % 2
    terms[...] = tn(gout[...], product[...])
    split_shards(terms, outs[0], outs[1], core)
    count = lifted_grad.shape[0]
    units = product.shape[0]
    stack[0:count, :] = nt(lifted_grad[...], fed[...])
    stack[count : count + units, :] = nt(product[...], upstream[...])
    if stack.shape[0] > count + units:
        stack[count + units :, :] = jnp.zeros((stack.shape[0] - count - units, stack.shape[1]), F32)
    emit_units(stack, outs[2:], cuts)


def emit_units(stack, outs, cuts):
    if cuts is None:
        outs[0][...] = stack[...]
        return
    seq = lax.axis_index("seq")
    start = 0
    for i, rows in enumerate(cuts):
        split_half(stack.at[pl.ds(start, rows), :], outs[2 * i], outs[2 * i + 1], seq)
        start += rows


def attention_back_kernel(
    mine, other, normed, inverse, gain, upstream, wo, q, kw, vw, totals, mixed, cos, sin, fed, *rest,
    cuts,
):
    outs, (full, low, mixed_grad, dk, dv, stack) = rest[:-6], rest[-6:]
    middle_grad_own, gain_grad, proj_grad = outs[:3]
    width, length = normed.shape
    columns = q.shape[0]
    heads = columns // HEAD
    tokens = kw.shape[1]
    rows = mine.shape[0]
    share = middle_grad_own.shape[0]
    me = lax.axis_index("mp")
    core = me % 2
    first = lax.axis_index("seq") * length
    total = lax.axis_size("seq") * length
    inv = inverse[0:1, :]

    def add(r, acc):
        a, b = acc
        for part, index in ((mine, core), (other, 1 - core)):
            at = pl.multiple_of(index * rows + r, STEP)
            grad = part[pl.ds(r, STEP), :].astype(F32)
            full[pl.ds(at, STEP), :] = grad
            hat = grad * gain[pl.ds(at, STEP), :]
            a = a + fold(hat)
            b = b + fold(hat * normed[pl.ds(at, STEP), :])
        return a, b

    zero = jnp.zeros((8, length), F32)
    a, b = row_loop(rows, STEP, add, (zero, zero))
    one = jnp.sum(a, axis=0, keepdims=True) / width
    two = jnp.sum(b, axis=0, keepdims=True) / width
    start = pl.multiple_of(me * share, share)
    weighted = full[pl.ds(start, share), :] * normed[pl.ds(start, share), :]
    lanes = weighted[:, 0:128]
    for j in range(1, length // 128):
        lanes = lanes + weighted[:, j * 128 : (j + 1) * 128]
    gain_grad[...] = lanes

    def back(r, carry):
        at = pl.ds(r, STEP)
        hat = full[at, :] * gain[at, :]
        value = upstream[at, :].astype(F32) + inv * (hat - one - normed[at, :] * two)
        full[at, :] = value
        low[at, :] = value.astype(BF16)
        return carry

    row_loop(width, STEP, back, 0)
    middle_grad_own[...] = full[pl.ds(start, share), :]
    mixed_grad[...] = nn(wo[...], low[...]).astype(BF16)
    dk[...] = jnp.zeros(dk.shape, F32)
    dv[...] = jnp.zeros(dv.shape, F32)
    half = HEAD // 2
    every = slice(0, tokens)

    def unrope(a, b, lanes):
        c = cos[:, lanes]
        s = sin[:, lanes]
        return a * c + b * s, b * c - a * s

    def one_head(h, carry):
        row = pl.multiple_of(h * HEAD, HEAD)
        head = pl.ds(row, HEAD)
        for j in range(length // TILE):
            wide = slice(j * TILE, (j + 2) * TILE)
            here = slice(j * TILE, (j + 1) * TILE)
            keys = kw[head, wide]
            query = q[head, here]
            grad = mixed_grad[head, here]
            scores = tn(keys, query) * HEAD**-0.5
            scores = jnp.where(allowed_of(first, j, total), scores, -1e30)
            probs = jnp.exp(scores - totals[h, 0:1, here])
            both = grad.astype(F32) * mixed[head, here].astype(F32)
            delta = jnp.sum(both, axis=0, keepdims=True)
            dv[head, wide] += nt(grad, probs.astype(BF16))
            grad_probs = tn(vw[head, wide], grad)
            grad_scores = (probs * (grad_probs - delta) * HEAD**-0.5).astype(BF16)
            dk[head, wide] += nt(query, grad_scores)
            dq = nn(keys, grad_scores)
            upper, lower = unrope(dq[:half], dq[half:], here)
            proj_grad[pl.ds(row, half), here] = upper.astype(BF16)
            proj_grad[pl.ds(row + half, half), here] = lower.astype(BF16)
        proj_grad[head, length:tokens] = jnp.zeros((HEAD, tokens - length), BF16)
        keys_grad = pltpu.roll(dk[head, :], tokens - HALF, 1)
        upper, lower = unrope(keys_grad[:half], keys_grad[half:], every)
        at = pl.multiple_of(columns + row, HEAD)
        proj_grad[pl.ds(at, half), :] = upper.astype(BF16)
        proj_grad[pl.ds(at + half, half), :] = lower.astype(BF16)
        at = pl.multiple_of(2 * columns + row, HEAD)
        proj_grad[pl.ds(at, HEAD), :] = pltpu.roll(dv[head, :], tokens - HALF, 1).astype(BF16)
        return carry

    lax.fori_loop(0, heads, one_head, 0)
    stack[0:columns, :] = nt(proj_grad[2 * columns : 3 * columns, :], fed[...])
    stack[columns : 2 * columns, :] = nt(mixed[...], low[...])
    stack[2 * columns : 4 * columns, :] = nt(proj_grad[0 : 2 * columns, :], fed[...])
    emit_units(stack, outs[3:], cuts)


def input_terms_kernel(proj_grad, w, gain, xall, stats, keep, send, sums, terms):
    width, tokens = terms.shape
    core = lax.axis_index("mp") % 2
    terms[...] = tn(w[...], proj_grad[...])
    mean = stats[0:1, :]
    inverse = stats[1:2, :]

    def add(r, acc):
        a, b = acc
        at = pl.ds(r, STEP)
        hat = terms[at, :] * gain[at, :]
        normed = (xall[at, :].astype(F32) - mean) * inverse
        return a + fold(hat), b + fold(hat * normed)

    zero = jnp.zeros((8, tokens), F32)
    a, b = row_loop(width, STEP, add, (zero, zero))
    sums[0:1, :] = jnp.sum(a, axis=0, keepdims=True) / width
    sums[1:2, :] = jnp.sum(b, axis=0, keepdims=True) / width
    sums[2:8, :] = jnp.zeros((6, tokens), F32)
    split_shards(terms, keep, send, core)


def quarters_kernel(keep, got, own, *sends):
    rows = own.shape[0]
    me = lax.axis_index("dp")
    for k, out in enumerate((own,) + sends):
        at = pl.ds(pl.multiple_of(jnp.bitwise_xor(me, k) * rows, 16), rows)
        out[...] = (keep[at, :] + got[at, :].astype(F32)).astype(out.dtype)


def join_kernel(*refs):
    pieces, out = refs[:-1], refs[-1]
    rows = pieces[0].shape[0]
    me = lax.axis_index("dp")
    for k, piece in enumerate(pieces):
        out[pl.ds(pl.multiple_of(jnp.bitwise_xor(me, k) * rows, 16), rows), :] = piece[...]


def place_kernel(*refs, cuts, outs):
    count = len(cuts)
    halves, targets, stack = refs[: 2 * count], refs[2 * count : -1], refs[-1]
    seq = lax.axis_index("seq")
    start = 0
    for i, rows in enumerate(cuts):
        size = rows // 2
        mine = pl.ds(pl.multiple_of(start + seq * size, 16), size)
        other = pl.ds(pl.multiple_of(start + (1 - seq) * size, 16), size)
        stack[mine, :] = halves[2 * i][...].astype(F32)
        stack[other, :] = halves[2 * i + 1][...].astype(F32)
        start += rows
    for target, spans in zip(targets, outs):
        at = 0
        for begin, size in spans:
            target[at : at + size, :] = stack[begin : begin + size, :]
            at += size


def flip(x, axis, bit):
    count = lax.axis_size(axis)
    return lax.ppermute(x, axis, [(i, i ^ bit) for i in range(count)])


def gather_mp(shard):
    across = flip(shard, "mp", 2)
    return shard, flip(shard, "mp", 1), across, flip(across, "mp", 1)


def sum_halves(keep, send):
    half = (keep + flip(send, "mp", 1).astype(F32)).astype(BF16)
    total = (half.astype(F32) + flip(half, "mp", 2).astype(F32)).astype(BF16)
    return total, flip(total, "mp", 1)


def scatter_shards(keep, send):
    x = lax.axis_index("mp") // 2
    half = keep + flip(send, "mp", 1).astype(F32)
    away = jnp.where(x == 0, half[1], half[0]).astype(BF16)
    return jnp.where(x == 0, half[0], half[1]) + flip(away, "mp", 2).astype(F32)


def reduce_unit(keep, send):
    rows, width = keep.shape
    count = lax.axis_size("dp")
    part = rows // count
    got = flip(send, "seq", 1)
    outs = [((part, width), F32)] + [((part, width), BF16)] * (count - 1)
    quarters = call(quarters_kernel, outs, [], keep, got)
    total = quarters[0]
    for k in range(1, count):
        total = total + flip(quarters[k], "dp", k).astype(F32)
    total = total.astype(BF16)
    pieces = [total] + [flip(total, "dp", k) for k in range(1, count)]
    (half,) = call(join_kernel, [((rows, width), BF16)], [], *pieces)
    return half, flip(half, "seq", 1)


def reduce_stack(parts, cuts, spans, width):
    sizes = [(sum(size for _, size in span), width) for span in spans]
    if cuts is None:
        total = lax.psum(parts[0], ("dp", "seq"))
        return [jnp.concatenate([total[b : b + n] for b, n in span]) for span in spans]
    halves = []
    for i in range(len(cuts)):
        halves.extend(reduce_unit(parts[2 * i], parts[2 * i + 1]))
    kernel = functools.partial(place_kernel, cuts=cuts, outs=spans)
    return call(
        kernel, [(size, F32) for size in sizes], [((sum(cuts), width), F32)], *halves
    )


def unit_shapes(cuts, rows, width):
    if cuts is None:
        return [((rows, width), F32)]
    shapes = []
    for size in cuts:
        shapes += [((size // 2, width), F32), ((size // 2, width), BF16)]
    return shapes


def body(
    hidden_in,
    cotangent,
    attention_gain,
    feedforward_gain,
    qkv_weight,
    attention_out,
    geglu_in,
    geglu_out,
):
    length, share = hidden_in.shape[1:]
    width = qkv_weight.shape[0]
    columns = qkv_weight.shape[2]
    units = geglu_out.shape[0]
    heads = columns // HEAD
    tokens = length + TILE
    half = width // 2
    dp, seqs = lax.axis_size("dp"), lax.axis_size("seq")
    staged = seqs == 2 and dp & (dp - 1) == 0
    grain = 2 * dp * 16
    x_own = hidden_in[0].T
    u_own = cotangent[0].T
    w = jnp.transpose(qkv_weight, (1, 2, 0)).reshape(3 * columns, width)
    win = jnp.transpose(geglu_in, (1, 2, 0)).reshape(2 * units, width)
    gain_one = attention_gain[:, None]
    gain_two = feedforward_gain[:, None]

    forward = [(i, i + 1) for i in range(seqs - 1)]
    backward = [(i + 1, i) for i in range(seqs - 1)]
    before = lax.ppermute(x_own[:, length - HALF :], "seq", forward)
    after = lax.ppermute(x_own[:, :HALF], "seq", backward)
    halo = jnp.concatenate([after, before], axis=1)
    x_parts = gather_mp(x_own)
    h_parts = gather_mp(halo)
    u_parts = gather_mp(u_own)

    base = (lax.axis_index("seq") * length).astype(jnp.int32)
    spot = jnp.arange(tokens, dtype=jnp.int32)
    spot = jnp.where(spot < length + HALF, spot, spot - tokens) + base
    rates = jnp.exp(jnp.arange(HEAD // 2).astype(F32) * (-2.0 * math.log(10000.0) / HEAD))
    angles = rates[:, None] * spot.astype(F32)[None, :]
    cos, sin = jnp.cos(angles), jnp.sin(angles)

    xall, stats, fed, q, kw, vw, totals, mixed, keep, send = call(
        attention_kernel,
        [
            ((width, tokens), BF16),
            ((8, tokens), F32),
            ((width, tokens), BF16),
            ((columns, length), BF16),
            ((columns, tokens), BF16),
            ((columns, tokens), BF16),
            ((heads, 8, length), F32),
            ((columns, length), BF16),
            ((half, length), F32),
            ((half, length), BF16),
        ],
        [((3 * columns, tokens), F32), ((width, length), F32)],
        *x_parts, *h_parts, gain_one, w, attention_out, cos, sin,
    )
    mine, other = sum_halves(keep, send)
    middle_own, normed, inverse, fed_two, upstream, product, lifted_grad, keep, send = call(
        geglu_kernel,
        [
            ((share, length), F32),
            ((width, length), F32),
            ((8, length), F32),
            ((width, length), BF16),
            ((width, length), BF16),
            ((units, length), BF16),
            ((2 * units, length), BF16),
            ((half, length), F32),
            ((half, length), BF16),
        ],
        [
            ((width, length), F32),
            ((2 * units, length), F32),
            ((units, length), F32),
            ((width, length), F32),
        ],
        xall, mine, other, *u_parts, gain_two, win, geglu_out,
    )
    mine, other = sum_halves(keep, send)

    rows = 3 * units
    padded = -(-rows // grain) * grain if staged else rows
    large = -(-padded // (2 * grain)) * grain
    geglu_cuts = (large, padded - large) if staged else None
    shard_shapes = [((2, share, length), F32), ((2, share, length), BF16)]
    outs = call(
        functools.partial(geglu_weights_kernel, cuts=geglu_cuts),
        shard_shapes + unit_shapes(geglu_cuts, padded, width),
        [((width, length), F32), ((padded, width), F32)],
        product, lifted_grad, fed_two, upstream, geglu_out,
    )
    layer_out = middle_own + scatter_shards(outs[0], outs[1])
    grad_in, grad_out = reduce_stack(
        outs[2:], geglu_cuts, (((0, 2 * units),), ((2 * units, units),)), width
    )

    back_cuts = (2 * columns, 2 * columns) if staged and 2 * columns % grain == 0 else None
    outs = call(
        functools.partial(attention_back_kernel, cuts=back_cuts),
        [((share, length), F32), ((share, 128), F32), ((3 * columns, tokens), BF16)]
        + unit_shapes(back_cuts, 4 * columns, width),
        [
            ((width, length), F32),
            ((width, length), BF16),
            ((columns, length), BF16),
            ((columns, tokens), F32),
            ((columns, tokens), F32),
            ((4 * columns, width), F32),
        ],
        mine, other, normed, inverse, gain_two, upstream, attention_out,
        q, kw, vw, totals, mixed, cos, sin, fed,
    )
    middle_grad, gain_two_lanes, proj_grad = outs[:3]
    grad_qkv, grad_attention_out = reduce_stack(
        outs[3:],
        back_cuts,
        (((2 * columns, 2 * columns), (0, columns)), ((columns, columns),)),
        width,
    )

    keep, send, sums = call(
        input_terms_kernel,
        [((2, share, tokens), F32), ((2, share, tokens), BF16), ((8, tokens), F32)],
        [((width, tokens), F32)],
        proj_grad, w, gain_one, xall, stats,
    )
    grad_one = scatter_shards(keep, send)
    sums = sums + flip(sums, "mp", 1)
    sums = sums + flip(sums, "mp", 2)
    offset = lax.axis_index("mp") * share
    x_all_own = lax.dynamic_slice_in_dim(xall, offset, share, 0).astype(F32)
    normed_own = (x_all_own - stats[0:1]) * stats[1:2]
    gain_one_grad = jnp.sum(grad_one * normed_own, axis=1)
    gain_two_grad = jnp.sum(gain_two_lanes, axis=1)
    gains = lax.psum(jnp.stack([gain_one_grad, gain_two_grad]), ("dp", "seq"))
    both = jnp.concatenate([grad_one, sums], axis=0)
    low_add = lax.ppermute(both[:, length : length + HALF], "seq", forward)
    high_add = lax.ppermute(both[:, length + HALF :], "seq", backward)
    both = jnp.concatenate(
        [
            both[:, :HALF] + low_add,
            both[:, HALF : length - HALF],
            both[:, length - HALF : length] + high_add,
        ],
        axis=1,
    )
    hat = both[:share] * lax.dynamic_slice_in_dim(gain_one, offset, share, 0)
    grad_input = middle_grad + stats[1:2, :length] * (
        hat - both[share : share + 1] - normed_own[:, :length] * both[share + 1 : share + 2]
    )
    return (
        layer_out.T[None],
        grad_input.T[None],
        jnp.transpose(grad_qkv.reshape(3, columns, width), (2, 0, 1)),
        grad_attention_out,
        jnp.transpose(grad_in.reshape(2, units, width), (2, 0, 1)),
        grad_out,
        gains[0],
        gains[1],
    )


def solution(mesh):
    in_specs = (
        P("dp", "seq", "mp"),
        P("dp", "seq", "mp"),
        P(),
        P(),
        P(None, None, "mp"),
        P("mp", None),
        P(None, None, "mp"),
        P("mp", None),
    )
    out_specs = (
        P("dp", "seq", "mp"),
        P("dp", "seq", "mp"),
        P(None, None, "mp"),
        P("mp", None),
        P(None, None, "mp"),
        P("mp", None),
        P("mp"),
        P("mp"),
    )
    return jax.shard_map(body, mesh=mesh, in_specs=in_specs, out_specs=out_specs, check_vma=False)
```

```python
import functools
import math

import jax
import jax.numpy as jnp
from jax import lax
from jax.experimental import pallas as pl
from jax.experimental.pallas import tpu as pltpu
from jax.sharding import PartitionSpec as P

HEAD = 64
HALF = 64
TILE = 2 * HALF
STEP = 64
F32 = jnp.float32
BF16 = jnp.bfloat16


def room(shape, dtype):
    lanes = -(-shape[-1] // 128) * 128
    return math.prod(shape[:-1]) * lanes * jnp.dtype(dtype).itemsize


def call(kernel, outs, scratch, *args):
    arrays = list(outs) + list(scratch) + [(a.shape, a.dtype) for a in args]
    grant = sum(room(s, t) for s, t in arrays) + 4 * 1024 * 1024
    return pl.pallas_call(
        kernel,
        out_shape=tuple(jax.ShapeDtypeStruct(s, t) for s, t in outs),
        scratch_shapes=[pltpu.VMEM(s, t) for s, t in scratch],
        compiler_params=pltpu.CompilerParams(vmem_limit_bytes=grant),
    )(*args)


def nn(a, b):
    return lax.dot_general(a, b, (((1,), (0,)), ((), ())), preferred_element_type=F32)


def tn(a, b):
    return lax.dot_general(a, b, (((0,), (0,)), ((), ())), preferred_element_type=F32)


def nt(a, b):
    return lax.dot_general(a, b, (((1,), (1,)), ((), ())), preferred_element_type=F32)


def row_loop(rows, step, fn, init):
    def one(i, carry):
        return fn(pl.multiple_of(i * step, step), carry)

    return lax.fori_loop(0, rows // step, one, init)


def fold(x):
    return jnp.sum(x.reshape(x.shape[0] // 8, 8, x.shape[1]), axis=0)


def allowed_of(first, tile, total):
    shape = (2 * TILE, TILE)
    key = lax.broadcasted_iota(jnp.int32, shape, 0)
    query = lax.broadcasted_iota(jnp.int32, shape, 1)
    gap = key - query
    position = key + (first + tile * TILE - HALF)
    return (gap >= 0) & (gap <= TILE) & (position >= 0) & (position < total)


def gather_rows(pieces, target, lanes):
    me = lax.axis_index("mp")
    share = pieces[0].shape[0]
    for k, piece in enumerate(pieces):
        start = pl.multiple_of(jnp.bitwise_xor(me, k) * share, share)
        target[pl.ds(start, share), lanes] = piece[...]


def split_half(source, keep, send, index):
    rows = keep.shape[0]

    def one(r, carry):
        mine = pl.multiple_of(index * rows + r, 16)
        other = pl.multiple_of((1 - index) * rows + r, 16)
        keep[pl.ds(r, 16), :] = source[pl.ds(mine, 16), :]
        send[pl.ds(r, 16), :] = source[pl.ds(other, 16), :].astype(send.dtype)
        return carry

    row_loop(rows, 16, one, 0)


def split_shards(source, keep, send, core):
    share = keep.shape[1]
    for x in range(2):
        mine = pl.multiple_of((2 * x + core) * share, share)
        other = pl.multiple_of((2 * x + 1 - core) * share, share)
        keep[x] = source[pl.ds(mine, share), :]
        send[x] = source[pl.ds(other, share), :].astype(send.dtype)


def attention_kernel(
    p0, p1, p2, p3, h0, h1, h2, h3, gain, w, wo, cos, sin,
    xall, stats, fed, q, kw, vw, totals, mixed, keep, send,
    proj, terms,
):
    width, tokens = xall.shape
    length = q.shape[1]
    columns = q.shape[0]
    heads = columns // HEAD
    core = lax.axis_index("mp") % 2
    first = lax.axis_index("seq") * length
    total = lax.axis_size("seq") * length
    gather_rows((p0, p1, p2, p3), xall, slice(0, length))
    gather_rows((h0, h1, h2, h3), xall, slice(length, tokens))

    def add(r, acc):
        return acc + fold(xall[pl.ds(r, STEP), :].astype(F32))

    zero = jnp.zeros((8, tokens), F32)
    mean = jnp.sum(row_loop(width, STEP, add, zero), axis=0, keepdims=True) / width

    def add_square(r, acc):
        center = xall[pl.ds(r, STEP), :].astype(F32) - mean
        return acc + fold(center * center)

    var = jnp.sum(row_loop(width, STEP, add_square, zero), axis=0, keepdims=True) / width
    inverse = lax.rsqrt(var + 1e-05)
    stats[0:1, :] = mean
    stats[1:2, :] = inverse
    stats[2:8, :] = jnp.zeros((6, tokens), F32)

    def feed(r, carry):
        normed = (xall[pl.ds(r, STEP), :].astype(F32) - mean) * inverse
        fed[pl.ds(r, STEP), :] = (normed * gain[pl.ds(r, STEP), 0:1]).astype(BF16)
        return carry

    row_loop(width, STEP, feed, 0)
    proj[...] = nn(w[...], fed[...])
    half = HEAD // 2

    def rope(row, lanes):
        a = proj[pl.ds(row, half), lanes]
        b = proj[pl.ds(row + half, half), lanes]
        c = cos[:, lanes]
        s = sin[:, lanes]
        return a * c - b * s, b * c + a * s

    def one_head(h, carry):
        row = pl.multiple_of(h * HEAD, HEAD)
        own = slice(0, length)
        every = slice(0, tokens)
        upper, lower = rope(row, own)
        q[pl.ds(row, half), :] = upper.astype(BF16)
        q[pl.ds(row + half, half), :] = lower.astype(BF16)
        upper, lower = rope(columns + row, every)
        kw[pl.ds(row, half), :] = pltpu.roll(upper, HALF, 1).astype(BF16)
        kw[pl.ds(row + half, half), :] = pltpu.roll(lower, HALF, 1).astype(BF16)
        value = proj[pl.ds(2 * columns + row, HEAD), :]
        vw[pl.ds(row, HEAD), :] = pltpu.roll(value, HALF, 1).astype(BF16)
        for j in range(length // TILE):
            wide = slice(j * TILE, (j + 2) * TILE)
            mine = slice(j * TILE, (j + 1) * TILE)
            scores = tn(kw[pl.ds(row, HEAD), wide], q[pl.ds(row, HEAD), mine]) * HEAD**-0.5
            scores = jnp.where(allowed_of(first, j, total), scores, -1e30)
            top = jnp.max(scores, axis=0, keepdims=True)
            log_total = top + jnp.log(jnp.sum(jnp.exp(scores - top), axis=0, keepdims=True))
            weights = jnp.exp(scores - log_total).astype(BF16)
            totals[h, 0:1, mine] = log_total
            mixed[pl.ds(row, HEAD), mine] = nn(vw[pl.ds(row, HEAD), wide], weights).astype(BF16)
        return carry

    lax.fori_loop(0, heads, one_head, 0)
    terms[...] = tn(wo[...], mixed[...])
    split_half(terms, keep, send, core)


def geglu_kernel(
    xall, mine, other, u0, u1, u2, u3, gain, win, gout,
    middle_own, normed, inverse_out, fed, upstream, product, lifted_grad, keep, send,
    middle, lifted, grad_product, terms,
):
    width, length = normed.shape
    share = middle_own.shape[0]
    units = product.shape[0]
    rows = mine.shape[0]
    me = lax.axis_index("mp")
    core = me % 2
    gather_rows((u0, u1, u2, u3), upstream, slice(0, length))
    own = slice(0, length)

    def add(r, acc):
        for part, index in ((mine, core), (other, 1 - core)):
            at = pl.multiple_of(index * rows + r, STEP)
            value = xall[pl.ds(at, STEP), own].astype(F32) + part[pl.ds(r, STEP), :].astype(F32)
            middle[pl.ds(at, STEP), :] = value
            acc = acc + fold(value)
        return acc

    zero = jnp.zeros((8, length), F32)
    mean = jnp.sum(row_loop(rows, STEP, add, zero), axis=0, keepdims=True) / width

    def add_square(r, acc):
        center = middle[pl.ds(r, STEP), :] - mean
        return acc + fold(center * center)

    var = jnp.sum(row_loop(width, STEP, add_square, zero), axis=0, keepdims=True) / width
    inverse = lax.rsqrt(var + 1e-05)
    inverse_out[...] = jnp.broadcast_to(inverse, inverse_out.shape)

    def feed(r, carry):
        value = (middle[pl.ds(r, STEP), :] - mean) * inverse
        normed[pl.ds(r, STEP), :] = value
        fed[pl.ds(r, STEP), :] = (value * gain[pl.ds(r, STEP), 1:2]).astype(BF16)
        return carry

    row_loop(width, STEP, feed, 0)
    middle_own[...] = middle[pl.ds(pl.multiple_of(me * share, share), share), :]
    lifted[...] = nn(win[...], fed[...])
    grad_product[...] = nn(gout[...], upstream[...])

    def unit(r, carry):
        at = pl.ds(r, 32)
        gate = pl.ds(pl.multiple_of(units + r, 32), 32)
        linear = lifted[at, :]
        gating = lifted[gate, :]
        grad = grad_product[at, :]
        area = 0.5 * (1.0 + lax.erf(linear * 0.7071067811865476))
        activated = linear * area
        slope = area + linear * jnp.exp(-0.5 * linear * linear) * 0.3989422804014327
        product[at, :] = (activated * gating).astype(BF16)
        lifted_grad[at, :] = (grad * gating * slope).astype(BF16)
        lifted_grad[gate, :] = (grad * activated).astype(BF16)
        return carry

    row_loop(units, 32, unit, 0)
    terms[...] = tn(win[...], lifted_grad[...])
    split_half(terms, keep, send, core)


def geglu_weights_kernel(product, lifted_grad, fed, upstream, gout, *rest, cuts):
    outs, (terms, stack) = rest[:-2], rest[-2:]
    core = lax.axis_index("mp") % 2
    terms[...] = tn(gout[...], product[...])
    split_shards(terms, outs[0], outs[1], core)
    count = lifted_grad.shape[0]
    units = product.shape[0]
    stack[0:count, :] = nt(lifted_grad[...], fed[...])
    stack[count : count + units, :] = nt(product[...], upstream[...])
    if stack.shape[0] > count + units:
        stack[count + units :, :] = jnp.zeros((stack.shape[0] - count - units, stack.shape[1]), F32)
    emit_units(stack, outs[2:], cuts)


def emit_units(stack, outs, cuts):
    if cuts is None:
        outs[0][...] = stack[...]
        return
    start = 0
    for i, (rows, order) in enumerate(cuts):
        index = lax.axis_index(order[0]) % 2
        split_half(stack.at[pl.ds(start, rows), :], outs[2 * i], outs[2 * i + 1], index)
        start += rows


def attention_back_kernel(
    mine, other, normed, inverse, gain, upstream, wo, q, kw, vw, totals, mixed, cos, sin, fed, *rest,
    cuts,
):
    outs, (full, low, mixed_grad, dk, dv, stack) = rest[:-6], rest[-6:]
    middle_grad_own, gain_grad, proj_grad = outs[:3]
    width, length = normed.shape
    columns = q.shape[0]
    heads = columns // HEAD
    tokens = kw.shape[1]
    rows = mine.shape[0]
    share = middle_grad_own.shape[0]
    me = lax.axis_index("mp")
    core = me % 2
    first = lax.axis_index("seq") * length
    total = lax.axis_size("seq") * length
    inv = inverse[0:1, :]

    def add(r, acc):
        a, b = acc
        for part, index in ((mine, core), (other, 1 - core)):
            at = pl.multiple_of(index * rows + r, STEP)
            grad = part[pl.ds(r, STEP), :].astype(F32)
            full[pl.ds(at, STEP), :] = grad
            hat = grad * gain[pl.ds(at, STEP), 1:2]
            a = a + fold(hat)
            b = b + fold(hat * normed[pl.ds(at, STEP), :])
        return a, b

    zero = jnp.zeros((8, length), F32)
    a, b = row_loop(rows, STEP, add, (zero, zero))
    one = jnp.sum(a, axis=0, keepdims=True) / width
    two = jnp.sum(b, axis=0, keepdims=True) / width
    start = pl.multiple_of(me * share, share)
    weighted = full[pl.ds(start, share), :] * normed[pl.ds(start, share), :]
    lanes = weighted[:, 0:128]
    for j in range(1, length // 128):
        lanes = lanes + weighted[:, j * 128 : (j + 1) * 128]
    gain_grad[...] = lanes

    def back(r, carry):
        at = pl.ds(r, STEP)
        hat = full[at, :] * gain[at, 1:2]
        value = upstream[at, :].astype(F32) + inv * (hat - one - normed[at, :] * two)
        full[at, :] = value
        low[at, :] = value.astype(BF16)
        return carry

    row_loop(width, STEP, back, 0)
    middle_grad_own[...] = full[pl.ds(start, share), :]
    mixed_grad[...] = nn(wo[...], low[...]).astype(BF16)
    dk[...] = jnp.zeros(dk.shape, F32)
    dv[...] = jnp.zeros(dv.shape, F32)
    half = HEAD // 2
    every = slice(0, tokens)

    def unrope(a, b, lanes):
        c = cos[:, lanes]
        s = sin[:, lanes]
        return a * c + b * s, b * c - a * s

    def one_head(h, carry):
        row = pl.multiple_of(h * HEAD, HEAD)
        head = pl.ds(row, HEAD)
        for j in range(length // TILE):
            wide = slice(j * TILE, (j + 2) * TILE)
            here = slice(j * TILE, (j + 1) * TILE)
            keys = kw[head, wide]
            query = q[head, here]
            grad = mixed_grad[head, here]
            scores = tn(keys, query) * HEAD**-0.5
            scores = jnp.where(allowed_of(first, j, total), scores, -1e30)
            probs = jnp.exp(scores - totals[h, 0:1, here])
            both = grad.astype(F32) * mixed[head, here].astype(F32)
            delta = jnp.sum(both, axis=0, keepdims=True)
            dv[head, wide] += nt(grad, probs.astype(BF16))
            grad_probs = tn(vw[head, wide], grad)
            grad_scores = (probs * (grad_probs - delta) * HEAD**-0.5).astype(BF16)
            dk[head, wide] += nt(query, grad_scores)
            dq = nn(keys, grad_scores)
            upper, lower = unrope(dq[:half], dq[half:], here)
            proj_grad[pl.ds(row, half), here] = upper.astype(BF16)
            proj_grad[pl.ds(row + half, half), here] = lower.astype(BF16)
        proj_grad[head, length:tokens] = jnp.zeros((HEAD, tokens - length), BF16)
        keys_grad = pltpu.roll(dk[head, :], tokens - HALF, 1)
        upper, lower = unrope(keys_grad[:half], keys_grad[half:], every)
        at = pl.multiple_of(columns + row, HEAD)
        proj_grad[pl.ds(at, half), :] = upper.astype(BF16)
        proj_grad[pl.ds(at + half, half), :] = lower.astype(BF16)
        at = pl.multiple_of(2 * columns + row, HEAD)
        proj_grad[pl.ds(at, HEAD), :] = pltpu.roll(dv[head, :], tokens - HALF, 1).astype(BF16)
        return carry

    lax.fori_loop(0, heads, one_head, 0)
    stack[0:columns, :] = nt(proj_grad[2 * columns : 3 * columns, :], fed[...])
    stack[columns : 2 * columns, :] = nt(mixed[...], low[...])
    stack[2 * columns : 4 * columns, :] = nt(proj_grad[0 : 2 * columns, :], fed[...])
    emit_units(stack, outs[3:], cuts)


def input_terms_kernel(proj_grad, w, gain, xall, stats, keep, send, sums, terms):
    width, tokens = terms.shape
    core = lax.axis_index("mp") % 2
    terms[...] = tn(w[...], proj_grad[...])
    mean = stats[0:1, :]
    inverse = stats[1:2, :]

    def add(r, acc):
        a, b = acc
        at = pl.ds(r, STEP)
        hat = terms[at, :] * gain[at, 0:1]
        normed = (xall[at, :].astype(F32) - mean) * inverse
        return a + fold(hat), b + fold(hat * normed)

    zero = jnp.zeros((8, tokens), F32)
    a, b = row_loop(width, STEP, add, (zero, zero))
    sums[0:1, :] = jnp.sum(a, axis=0, keepdims=True) / width
    sums[1:2, :] = jnp.sum(b, axis=0, keepdims=True) / width
    sums[2:8, :] = jnp.zeros((6, tokens), F32)
    split_shards(terms, keep, send, core)


def halves_kernel(keep, got, out_keep, out_send, *, axis):
    rows = out_keep.shape[0]
    index = lax.axis_index(axis) % 2

    def one(r, carry):
        mine = pl.ds(pl.multiple_of(index * rows + r, 16), 16)
        other = pl.ds(pl.multiple_of((1 - index) * rows + r, 16), 16)
        at = pl.ds(r, 16)
        out_keep[at, :] = keep[mine, :] + got[mine, :].astype(F32)
        out_send[at, :] = (keep[other, :] + got[other, :].astype(F32)).astype(BF16)
        return carry

    row_loop(rows, 16, one, 0)


def place_kernel(*refs, cuts, outs):
    count = len(cuts)
    pieces, targets, stack = refs[: 4 * count], refs[4 * count : -1], refs[-1]
    start = 0
    for i, (rows, order) in enumerate(cuts):
        size = rows // 4
        one, two = (lax.axis_index(axis) % 2 for axis in order)
        for k in range(4):
            far = one if k < 2 else 1 - one
            near = two if k % 2 == 0 else 1 - two
            at = pl.multiple_of(start + (2 * far + near) * size, 16)
            stack[pl.ds(at, size), :] = pieces[4 * i + k][...].astype(F32)
        start += rows
    for target, spans in zip(targets, outs):
        at = 0
        for begin, size in spans:
            target[at : at + size, :] = stack[begin : begin + size, :]
            at += size


def flip(x, axis, bit):
    count = lax.axis_size(axis)
    return lax.ppermute(x, axis, [(i, i ^ bit) for i in range(count)])


def gather_mp(shard):
    across = flip(shard, "mp", 2)
    return shard, flip(shard, "mp", 1), across, flip(across, "mp", 1)


def sum_halves(keep, send):
    half = (keep + flip(send, "mp", 1).astype(F32)).astype(BF16)
    total = (half.astype(F32) + flip(half, "mp", 2).astype(F32)).astype(BF16)
    return total, flip(total, "mp", 1)


def scatter_shards(keep, send):
    x = lax.axis_index("mp") // 2
    half = keep + flip(send, "mp", 1).astype(F32)
    away = jnp.where(x == 0, half[1], half[0]).astype(BF16)
    return jnp.where(x == 0, half[0], half[1]) + flip(away, "mp", 2).astype(F32)


def to_neighbours(low, high):
    count = lax.axis_size("seq")
    if count == 2:
        last = lax.axis_index("seq") == 1
        got = flip(jnp.where(last, low, high), "seq", 1)
        zero = jnp.zeros_like(got)
        return jnp.where(last, zero, got), jnp.where(last, got, zero)
    after = lax.ppermute(low, "seq", [(i + 1, i) for i in range(count - 1)])
    before = lax.ppermute(high, "seq", [(i, i + 1) for i in range(count - 1)])
    return after, before


def staged():
    return lax.axis_size("seq") == 2 and lax.axis_size("dp") == 4


def sum_blocks(x):
    if not staged():
        return lax.psum(x, ("dp", "seq"))
    x = x + flip(x, "seq", 1)
    x = x + flip(x, "dp", 1)
    return x + flip(x, "dp", 2)


def reduce_unit(keep, send, order):
    one, two = order
    rows, width = keep.shape
    got = flip(send, one, 1)
    keep, send = call(
        functools.partial(halves_kernel, axis=two),
        [((rows // 2, width), F32), ((rows // 2, width), BF16)],
        [],
        keep,
        got,
    )
    part = (keep + flip(send, two, 1).astype(F32)).astype(BF16)
    total = (part.astype(F32) + flip(part, "dp", 2).astype(F32)).astype(BF16)
    beside = flip(total, two, 1)
    return total, beside, flip(total, one, 1), flip(beside, one, 1)


def reduce_stack(parts, cuts, spans, width):
    sizes = [(sum(size for _, size in span), width) for span in spans]
    if cuts is None:
        total = lax.psum(parts[0], ("dp", "seq"))
        return [jnp.concatenate([total[b : b + n] for b, n in span]) for span in spans]
    pieces = []
    for i, (_, order) in enumerate(cuts):
        pieces.extend(reduce_unit(parts[2 * i], parts[2 * i + 1], order))
    kernel = functools.partial(place_kernel, cuts=cuts, outs=spans)
    scratch = [((sum(rows for rows, _ in cuts), width), F32)]
    return call(kernel, [(size, F32) for size in sizes], scratch, *pieces)


def unit_shapes(cuts, rows, width):
    if cuts is None:
        return [((rows, width), F32)]
    shapes = []
    for size, _ in cuts:
        shapes += [((size // 2, width), F32), ((size // 2, width), BF16)]
    return shapes


def body(
    hidden_in,
    cotangent,
    attention_gain,
    feedforward_gain,
    qkv_weight,
    attention_out,
    geglu_in,
    geglu_out,
):
    length, share = hidden_in.shape[1:]
    width = qkv_weight.shape[0]
    columns = qkv_weight.shape[2]
    units = geglu_out.shape[0]
    heads = columns // HEAD
    tokens = length + TILE
    half = width // 2
    orders = (("seq", "dp"), ("dp", "seq"))
    grain = 4 * 16
    x_own = hidden_in[0].T
    u_own = cotangent[0].T
    w = jnp.transpose(qkv_weight, (1, 2, 0)).reshape(3 * columns, width)
    win = jnp.transpose(geglu_in, (1, 2, 0)).reshape(2 * units, width)
    gains = jnp.stack([attention_gain, feedforward_gain], axis=1)

    x_parts = gather_mp(x_own)
    after, before = to_neighbours(x_own[:, :HALF], x_own[:, length - HALF :])
    halo = jnp.concatenate([after, before], axis=1)
    h_parts = gather_mp(halo)
    u_parts = gather_mp(u_own)

    base = (lax.axis_index("seq") * length).astype(jnp.int32)
    spot = jnp.arange(tokens, dtype=jnp.int32)
    spot = jnp.where(spot < length + HALF, spot, spot - tokens) + base
    rates = jnp.exp(jnp.arange(HEAD // 2).astype(F32) * (-2.0 * math.log(10000.0) / HEAD))
    angles = rates[:, None] * spot.astype(F32)[None, :]
    cos, sin = jnp.cos(angles), jnp.sin(angles)

    xall, stats, fed, q, kw, vw, totals, mixed, keep, send = call(
        attention_kernel,
        [
            ((width, tokens), BF16),
            ((8, tokens), F32),
            ((width, tokens), BF16),
            ((columns, length), BF16),
            ((columns, tokens), BF16),
            ((columns, tokens), BF16),
            ((heads, 8, length), F32),
            ((columns, length), BF16),
            ((half, length), F32),
            ((half, length), BF16),
        ],
        [((3 * columns, tokens), F32), ((width, length), F32)],
        *x_parts, *h_parts, gains, w, attention_out, cos, sin,
    )
    mine, other = sum_halves(keep, send)
    middle_own, normed, inverse, fed_two, upstream, product, lifted_grad, keep, send = call(
        geglu_kernel,
        [
            ((share, length), F32),
            ((width, length), F32),
            ((8, length), F32),
            ((width, length), BF16),
            ((width, length), BF16),
            ((units, length), BF16),
            ((2 * units, length), BF16),
            ((half, length), F32),
            ((half, length), BF16),
        ],
        [
            ((width, length), F32),
            ((2 * units, length), F32),
            ((units, length), F32),
            ((width, length), F32),
        ],
        xall, mine, other, *u_parts, gains, win, geglu_out,
    )
    mine, other = sum_halves(keep, send)

    rows = 3 * units
    padded = -(-rows // (2 * grain)) * (2 * grain) if staged() else rows
    geglu_cuts = tuple((padded // 2, order) for order in orders) if staged() else None
    shard_shapes = [((2, share, length), F32), ((2, share, length), BF16)]
    outs = call(
        functools.partial(geglu_weights_kernel, cuts=geglu_cuts),
        shard_shapes + unit_shapes(geglu_cuts, padded, width),
        [((width, length), F32), ((padded, width), F32)],
        product, lifted_grad, fed_two, upstream, geglu_out,
    )
    layer_out = middle_own + scatter_shards(outs[0], outs[1])
    grad_in, grad_out = reduce_stack(
        outs[2:], geglu_cuts, (((0, 2 * units),), ((2 * units, units),)), width
    )

    back_cuts = None
    if staged() and 2 * columns % grain == 0:
        back_cuts = tuple((2 * columns, order) for order in orders)
    outs = call(
        functools.partial(attention_back_kernel, cuts=back_cuts),
        [((share, length), F32), ((share, 128), F32), ((3 * columns, tokens), BF16)]
        + unit_shapes(back_cuts, 4 * columns, width),
        [
            ((width, length), F32),
            ((width, length), BF16),
            ((columns, length), BF16),
            ((columns, tokens), F32),
            ((columns, tokens), F32),
            ((4 * columns, width), F32),
        ],
        mine, other, normed, inverse, gains, upstream, attention_out,
        q, kw, vw, totals, mixed, cos, sin, fed,
    )
    middle_grad, gain_two_lanes, proj_grad = outs[:3]
    grad_qkv, grad_attention_out = reduce_stack(
        outs[3:],
        back_cuts,
        (((2 * columns, 2 * columns), (0, columns)), ((columns, columns),)),
        width,
    )

    keep, send, sums = call(
        input_terms_kernel,
        [((2, share, tokens), F32), ((2, share, tokens), BF16), ((8, tokens), F32)],
        [((width, tokens), F32)],
        proj_grad, w, gains, xall, stats,
    )
    grad_one = scatter_shards(keep, send)
    sums = sums + flip(sums, "mp", 1)
    sums = sums + flip(sums, "mp", 2)
    offset = lax.axis_index("mp") * share
    x_all_own = lax.dynamic_slice_in_dim(xall, offset, share, 0).astype(F32)
    normed_own = (x_all_own - stats[0:1]) * stats[1:2]
    gain_one_grad = jnp.sum(grad_one * normed_own, axis=1)
    gain_two_grad = jnp.sum(gain_two_lanes, axis=1)
    gains = sum_blocks(jnp.stack([gain_one_grad, gain_two_grad]))
    both = jnp.concatenate([grad_one, sums], axis=0)
    high_add, low_add = to_neighbours(both[:, length + HALF :], both[:, length : length + HALF])
    both = jnp.concatenate(
        [
            both[:, :HALF] + low_add,
            both[:, HALF : length - HALF],
            both[:, length - HALF : length] + high_add,
        ],
        axis=1,
    )
    hat = both[:share] * lax.dynamic_slice_in_dim(attention_gain, offset, share, 0)[:, None]
    grad_input = middle_grad + stats[1:2, :length] * (
        hat - both[share : share + 1] - normed_own[:, :length] * both[share + 1 : share + 2]
    )
    return (
        layer_out.T[None],
        grad_input.T[None],
        jnp.transpose(grad_qkv.reshape(3, columns, width), (2, 0, 1)),
        grad_attention_out,
        jnp.transpose(grad_in.reshape(2, units, width), (2, 0, 1)),
        grad_out,
        gains[0],
        gains[1],
    )


def solution(mesh):
    in_specs = (
        P("dp", "seq", "mp"),
        P("dp", "seq", "mp"),
        P(),
        P(),
        P(None, None, "mp"),
        P("mp", None),
        P(None, None, "mp"),
        P("mp", None),
    )
    out_specs = (
        P("dp", "seq", "mp"),
        P("dp", "seq", "mp"),
        P(None, None, "mp"),
        P("mp", None),
        P(None, None, "mp"),
        P("mp", None),
        P("mp"),
        P("mp"),
    )
    return jax.shard_map(body, mesh=mesh, in_specs=in_specs, out_specs=out_specs, check_vma=False)
```

```python
import functools
import math

import jax
import jax.numpy as jnp
from jax import lax
from jax.experimental import pallas as pl
from jax.experimental.pallas import tpu as pltpu
from jax.sharding import PartitionSpec as P


HEAD = 64
HALF = 64
TILE = 2 * HALF
STEP = 64
GRANT = 8 * 1024 * 1024
F32 = jnp.float32
BF16 = jnp.bfloat16


def room(shape, dtype):
    lanes = -(-shape[-1] // 128) * 128
    return math.prod(shape[:-1]) * lanes * jnp.dtype(dtype).itemsize


def call(kernel, outs, scratch, *args, loads=0):
    grant = sum(room(s, t) for s, t in scratch) + GRANT
    extra = [pltpu.SemaphoreType.DMA((loads,))] if loads else []
    spaces = [pltpu.VMEM] * (len(args) - loads) + [pltpu.HBM] * loads
    run = pl.pallas_call(
        kernel,
        out_shape=tuple(jax.ShapeDtypeStruct(s, t) for s, t in outs),
        in_specs=[pl.BlockSpec(memory_space=space) for space in spaces],
        scratch_shapes=[pltpu.VMEM(s, t) for s, t in scratch] + extra,
        compiler_params=pltpu.CompilerParams(vmem_limit_bytes=grant),
    )
    if loads:
        far = [pltpu.with_memory_space_constraint(a, pltpu.HBM) for a in args[-loads:]]
        args = args[:-loads] + tuple(far)
    return run(*args)


def nn(a, b):
    return lax.dot_general(a, b, (((1,), (0,)), ((), ())), preferred_element_type=F32)


def tn(a, b):
    return lax.dot_general(a, b, (((0,), (0,)), ((), ())), preferred_element_type=F32)


def nt(a, b):
    return lax.dot_general(a, b, (((1,), (1,)), ((), ())), preferred_element_type=F32)


def row_loop(rows, step, fn, init):
    def one(i, carry):
        return fn(pl.multiple_of(i * step, step), carry)

    return lax.fori_loop(0, rows // step, one, init)


def fold(x):
    return jnp.sum(x.reshape(x.shape[0] // 8, 8, x.shape[1]), axis=0)


def allowed_of(first, tile, total):
    shape = (2 * TILE, TILE)
    key = lax.broadcasted_iota(jnp.int32, shape, 0)
    query = lax.broadcasted_iota(jnp.int32, shape, 1)
    gap = key - query
    position = key + (first + tile * TILE - HALF)
    return (gap >= 0) & (gap <= TILE) & (position >= 0) & (position < total)


def gather_rows(pieces, target, lanes):
    me = lax.axis_index("mp")
    share = pieces[0].shape[0]
    for k, piece in enumerate(pieces):
        start = pl.multiple_of(jnp.bitwise_xor(me, k) * share, share)
        target[pl.ds(start, share), lanes] = piece[...]


def split_half(source, keep, send, index):
    rows = keep.shape[0]

    def one(r, carry):
        mine = pl.multiple_of(index * rows + r, 16)
        other = pl.multiple_of((1 - index) * rows + r, 16)
        keep[pl.ds(r, 16), :] = source[pl.ds(mine, 16), :]
        send[pl.ds(r, 16), :] = source[pl.ds(other, 16), :].astype(send.dtype)
        return carry

    row_loop(rows, 16, one, 0)


def attention_kernel(
    p1, p2, p3, h0, h1, h2, h3, gain, cos, sin, p0_far, w_far, wo_far,
    xall, stats, fed, q, kw, vw, totals, mixed, keep, send,
    proj, terms, p0, w, wo, sems,
):
    copies = [
        pltpu.make_async_copy(p0_far, p0, sems.at[0]),
        pltpu.make_async_copy(w_far, w, sems.at[1]),
        pltpu.make_async_copy(wo_far, wo, sems.at[2]),
    ]
    for copy in copies:
        copy.start()
    width, tokens = xall.shape
    length = q.shape[1]
    columns = q.shape[0]
    heads = columns // HEAD
    core = lax.axis_index("mp") % 2
    first = lax.axis_index("seq") * length
    total = lax.axis_size("seq") * length
    gather_rows((h0, h1, h2, h3), xall, slice(length, tokens))
    copies[0].wait()
    gather_rows((p0, p1, p2, p3), xall, slice(0, length))

    def add(r, acc):
        return acc + fold(xall[pl.ds(r, STEP), :].astype(F32))

    zero = jnp.zeros((8, tokens), F32)
    mean = jnp.sum(row_loop(width, STEP, add, zero), axis=0, keepdims=True) / width

    def add_square(r, acc):
        center = xall[pl.ds(r, STEP), :].astype(F32) - mean
        return acc + fold(center * center)

    var = jnp.sum(row_loop(width, STEP, add_square, zero), axis=0, keepdims=True) / width
    inverse = lax.rsqrt(var + 1e-05)
    stats[0:1, :] = mean
    stats[1:2, :] = inverse
    stats[2:8, :] = jnp.zeros((6, tokens), F32)

    def feed(r, carry):
        normed = (xall[pl.ds(r, STEP), :].astype(F32) - mean) * inverse
        fed[pl.ds(r, STEP), :] = (normed * gain[pl.ds(r, STEP), 0:1]).astype(BF16)
        return carry

    row_loop(width, STEP, feed, 0)
    copies[1].wait()
    proj[...] = nn(w[...], fed[...])
    half = HEAD // 2

    def rope(row, lanes):
        a = proj[pl.ds(row, half), lanes]
        b = proj[pl.ds(row + half, half), lanes]
        c = cos[:, lanes]
        s = sin[:, lanes]
        return a * c - b * s, b * c + a * s

    def one_head(h, carry):
        row = pl.multiple_of(h * HEAD, HEAD)
        own = slice(0, length)
        every = slice(0, tokens)
        upper, lower = rope(row, own)
        q[pl.ds(row, half), :] = upper.astype(BF16)
        q[pl.ds(row + half, half), :] = lower.astype(BF16)
        upper, lower = rope(columns + row, every)
        kw[pl.ds(row, half), :] = pltpu.roll(upper, HALF, 1).astype(BF16)
        kw[pl.ds(row + half, half), :] = pltpu.roll(lower, HALF, 1).astype(BF16)
        value = proj[pl.ds(2 * columns + row, HEAD), :]
        vw[pl.ds(row, HEAD), :] = pltpu.roll(value, HALF, 1).astype(BF16)
        for j in range(length // TILE):
            wide = slice(j * TILE, (j + 2) * TILE)
            mine = slice(j * TILE, (j + 1) * TILE)
            scores = tn(kw[pl.ds(row, HEAD), wide], q[pl.ds(row, HEAD), mine]) * HEAD**-0.5
            scores = jnp.where(allowed_of(first, j, total), scores, -1e30)
            top = jnp.max(scores, axis=0, keepdims=True)
            log_total = top + jnp.log(jnp.sum(jnp.exp(scores - top), axis=0, keepdims=True))
            weights = jnp.exp(scores - log_total).astype(BF16)
            totals[h, 0:1, mine] = log_total
            mixed[pl.ds(row, HEAD), mine] = nn(vw[pl.ds(row, HEAD), wide], weights).astype(BF16)
        return carry

    lax.fori_loop(0, heads, one_head, 0)
    copies[2].wait()
    terms[...] = tn(wo[...], mixed[...])
    split_half(terms, keep, send, core)


def geglu_kernel(
    xall, mine, other, u0, u1, u2, u3, gain, win, gout,
    middle_own, normed, inverse_out, fed, upstream, product, lifted_grad, keep, send,
    middle, lifted, grad_product, terms,
):
    width, length = normed.shape
    share = middle_own.shape[0]
    units = product.shape[0]
    rows = mine.shape[0]
    me = lax.axis_index("mp")
    core = me % 2
    gather_rows((u0, u1, u2, u3), upstream, slice(0, length))
    own = slice(0, length)

    def add(r, acc):
        for part, index in ((mine, core), (other, 1 - core)):
            at = pl.multiple_of(index * rows + r, STEP)
            value = xall[pl.ds(at, STEP), own].astype(F32) + part[pl.ds(r, STEP), :].astype(F32)
            middle[pl.ds(at, STEP), :] = value
            acc = acc + fold(value)
        return acc

    zero = jnp.zeros((8, length), F32)
    mean = jnp.sum(row_loop(rows, STEP, add, zero), axis=0, keepdims=True) / width

    def add_square(r, acc):
        center = middle[pl.ds(r, STEP), :] - mean
        return acc + fold(center * center)

    var = jnp.sum(row_loop(width, STEP, add_square, zero), axis=0, keepdims=True) / width
    inverse = lax.rsqrt(var + 1e-05)
    inverse_out[...] = jnp.broadcast_to(inverse, inverse_out.shape)

    def feed(r, carry):
        value = (middle[pl.ds(r, STEP), :] - mean) * inverse
        normed[pl.ds(r, STEP), :] = value
        fed[pl.ds(r, STEP), :] = (value * gain[pl.ds(r, STEP), 1:2]).astype(BF16)
        return carry

    row_loop(width, STEP, feed, 0)
    middle_own[...] = middle[pl.ds(pl.multiple_of(me * share, share), share), :]
    lifted[...] = nn(win[...], fed[...])
    grad_product[...] = nn(gout[...], upstream[...])

    def unit(r, carry):
        at = pl.ds(r, 32)
        gate = pl.ds(pl.multiple_of(units + r, 32), 32)
        linear = lifted[at, :]
        gating = lifted[gate, :]
        grad = grad_product[at, :]
        area = 0.5 * (1.0 + lax.erf(linear * 0.7071067811865476))
        activated = linear * area
        slope = area + linear * jnp.exp(-0.5 * linear * linear) * 0.3989422804014327
        product[at, :] = (activated * gating).astype(BF16)
        lifted_grad[at, :] = (grad * gating * slope).astype(BF16)
        lifted_grad[gate, :] = (grad * activated).astype(BF16)
        return carry

    row_loop(units, 32, unit, 0)
    terms[...] = tn(win[...], lifted_grad[...])
    split_half(terms, keep, send, core)


def geglu_weights_kernel(product, lifted_grad, fed, upstream, *rest, cuts):
    outs, stack = rest[:-1], rest[-1]
    count = lifted_grad.shape[0]
    units = product.shape[0]
    stack[0:count, :] = nt(lifted_grad[...], fed[...])
    stack[count : count + units, :] = nt(product[...], upstream[...])
    if stack.shape[0] > count + units:
        stack[count + units :, :] = jnp.zeros((stack.shape[0] - count - units, stack.shape[1]), F32)
    emit_units(stack, outs, cuts)


def emit_units(stack, outs, cuts):
    if cuts is None:
        outs[0][...] = stack[...]
        return
    start = 0
    for i, (rows, order) in enumerate(cuts):
        index = lax.axis_index(order[0]) % 2
        split_half(stack.at[pl.ds(start, rows), :], outs[2 * i], outs[2 * i + 1], index)
        start += rows


def attention_back_kernel(
    mine, other, normed, inverse, gain, upstream, wo, q, kw, vw, totals, mixed, cos, sin, fed, *rest,
    cuts,
):
    outs, (full, low, mixed_grad, dk, dv, stack) = rest[:-6], rest[-6:]
    middle_grad_own, gain_grad, proj_grad = outs[:3]
    width, length = normed.shape
    columns = q.shape[0]
    heads = columns // HEAD
    tokens = kw.shape[1]
    rows = mine.shape[0]
    share = middle_grad_own.shape[0]
    me = lax.axis_index("mp")
    core = me % 2
    first = lax.axis_index("seq") * length
    total = lax.axis_size("seq") * length
    inv = inverse[0:1, :]

    def add(r, acc):
        a, b = acc
        for part, index in ((mine, core), (other, 1 - core)):
            at = pl.multiple_of(index * rows + r, STEP)
            grad = part[pl.ds(r, STEP), :].astype(F32)
            full[pl.ds(at, STEP), :] = grad
            hat = grad * gain[pl.ds(at, STEP), 1:2]
            a = a + fold(hat)
            b = b + fold(hat * normed[pl.ds(at, STEP), :])
        return a, b

    zero = jnp.zeros((8, length), F32)
    a, b = row_loop(rows, STEP, add, (zero, zero))
    one = jnp.sum(a, axis=0, keepdims=True) / width
    two = jnp.sum(b, axis=0, keepdims=True) / width
    start = pl.multiple_of(me * share, share)
    weighted = full[pl.ds(start, share), :] * normed[pl.ds(start, share), :]
    lanes = weighted[:, 0:128]
    for j in range(1, length // 128):
        lanes = lanes + weighted[:, j * 128 : (j + 1) * 128]
    gain_grad[...] = lanes

    def back(r, carry):
        at = pl.ds(r, STEP)
        hat = full[at, :] * gain[at, 1:2]
        value = upstream[at, :].astype(F32) + inv * (hat - one - normed[at, :] * two)
        full[at, :] = value
        low[at, :] = value.astype(BF16)
        return carry

    row_loop(width, STEP, back, 0)
    middle_grad_own[...] = full[pl.ds(start, share), :]
    mixed_grad[...] = nn(wo[...], low[...]).astype(BF16)
    dk[...] = jnp.zeros(dk.shape, F32)
    dv[...] = jnp.zeros(dv.shape, F32)
    half = HEAD // 2
    every = slice(0, tokens)

    def unrope(a, b, lanes):
        c = cos[:, lanes]
        s = sin[:, lanes]
        return a * c + b * s, b * c - a * s

    def one_head(h, carry):
        row = pl.multiple_of(h * HEAD, HEAD)
        head = pl.ds(row, HEAD)
        for j in range(length // TILE):
            wide = slice(j * TILE, (j + 2) * TILE)
            here = slice(j * TILE, (j + 1) * TILE)
            keys = kw[head, wide]
            query = q[head, here]
            grad = mixed_grad[head, here]
            scores = tn(keys, query) * HEAD**-0.5
            scores = jnp.where(allowed_of(first, j, total), scores, -1e30)
            probs = jnp.exp(scores - totals[h, 0:1, here])
            both = grad.astype(F32) * mixed[head, here].astype(F32)
            delta = jnp.sum(both, axis=0, keepdims=True)
            dv[head, wide] += nt(grad, probs.astype(BF16))
            grad_probs = tn(vw[head, wide], grad)
            grad_scores = (probs * (grad_probs - delta) * HEAD**-0.5).astype(BF16)
            dk[head, wide] += nt(query, grad_scores)
            dq = nn(keys, grad_scores)
            upper, lower = unrope(dq[:half], dq[half:], here)
            proj_grad[pl.ds(row, half), here] = upper.astype(BF16)
            proj_grad[pl.ds(row + half, half), here] = lower.astype(BF16)
        proj_grad[head, length:tokens] = jnp.zeros((HEAD, tokens - length), BF16)
        keys_grad = pltpu.roll(dk[head, :], tokens - HALF, 1)
        upper, lower = unrope(keys_grad[:half], keys_grad[half:], every)
        at = pl.multiple_of(columns + row, HEAD)
        proj_grad[pl.ds(at, half), :] = upper.astype(BF16)
        proj_grad[pl.ds(at + half, half), :] = lower.astype(BF16)
        at = pl.multiple_of(2 * columns + row, HEAD)
        proj_grad[pl.ds(at, HEAD), :] = pltpu.roll(dv[head, :], tokens - HALF, 1).astype(BF16)
        return carry

    lax.fori_loop(0, heads, one_head, 0)
    stack[0:columns, :] = nt(proj_grad[2 * columns : 3 * columns, :], fed[...])
    stack[columns : 2 * columns, :] = nt(mixed[...], low[...])
    stack[2 * columns : 4 * columns, :] = nt(proj_grad[0 : 2 * columns, :], fed[...])
    emit_units(stack, outs[3:], cuts)


def terms_kernel(
    proj_grad, w, gain, xall, stats, gout, product,
    keep, send, terms,
):
    width, tokens = xall.shape
    share = (keep.shape[0] - 16) // 2
    me = lax.axis_index("mp")
    core = me % 2
    terms[:, 0:tokens] = tn(w[...], proj_grad[...])
    mean = stats[0:1, :]
    inverse = stats[1:2, :]

    def add(r, acc):
        a, b = acc
        at = pl.ds(r, STEP)
        hat = terms[at, 0:tokens] * gain[at, 0:1]
        normed = (xall[at, :].astype(F32) - mean) * inverse
        return a + fold(hat), b + fold(hat * normed)

    zero = jnp.zeros((8, tokens), F32)
    a, b = row_loop(width, STEP, add, (zero, zero))
    one = jnp.sum(a, axis=0, keepdims=True) / width
    two = jnp.sum(b, axis=0, keepdims=True) / width
    terms[:, tokens:] = tn(gout[...], product[...])
    for x in range(2):
        mine = pl.multiple_of((2 * x + core) * share, share)
        other = pl.multiple_of((2 * x + 1 - core) * share, share)
        at = slice(x * share, (x + 1) * share)
        keep[at, :] = terms[pl.ds(mine, share), :]
        send[at, :] = terms[pl.ds(other, share), :].astype(BF16)
    rest = slice(2 * share, 2 * share + 16)
    row = lax.broadcasted_iota(jnp.int32, (16, tokens), 0)
    sums = jnp.where(row == 0, one, jnp.where(row == 1, two, 0.0))
    keep[rest, 0:tokens] = sums
    send[rest, 0:tokens] = sums.astype(BF16)
    keep[rest, tokens:] = jnp.zeros((16, terms.shape[1] - tokens), F32)
    send[rest, tokens:] = jnp.zeros((16, terms.shape[1] - tokens), BF16)


def own_rows_kernel(xall, stats, out):
    share = out.shape[0]
    own = pl.ds(pl.multiple_of(lax.axis_index("mp") * share, share), share)
    out[...] = (xall[own, :].astype(F32) - stats[0:1, :]) * stats[1:2, :]


def across_kernel(keep, got, own, away):
    share = (keep.shape[0] - 16) // 2
    x = lax.axis_index("mp") // 2
    for out, index in ((own, x), (away, 1 - x)):
        at = pl.ds(pl.multiple_of(index * share, share), share)
        out[0:share, :] = (keep[at, :] + got[at, :].astype(F32)).astype(out.dtype)
        last = slice(2 * share, 2 * share + 16)
        out[share : share + 16, :] = (keep[last, :] + got[last, :].astype(F32)).astype(out.dtype)


def finish_kernel(own, got, middle, normed, gain_lanes, layer_out, main, edges, gains):
    share, length = middle.shape
    tokens = normed.shape[1]
    layer_out[...] = middle[...] + own[0:share, tokens:] + got[0:share, tokens:].astype(F32)
    main[...] = own[:, 0:length] + got[:, 0:length].astype(F32)
    edges[...] = own[:, length:tokens] + got[:, length:tokens].astype(F32)
    weighted = gain_lanes[...], main[0:share, :] * normed[:, 0:length]
    last = edges[0:share, :] * normed[:, length:tokens]
    exact = functools.partial(
        lax.dot_general,
        dimension_numbers=(((1,), (1,)), ((), ())),
        precision=lax.Precision.HIGHEST,
        preferred_element_type=F32,
    )
    one = exact(jnp.ones((8, length), F32), weighted[1])
    gains[0:8, :] = one + exact(jnp.ones((8, tokens - length), F32), last)
    gains[8:16, :] = exact(jnp.ones((8, gain_lanes.shape[1]), F32), weighted[0])


def input_kernel(main, low, high, middle_grad, stats, normed, gain, out):
    share, length = out.shape
    own = pl.ds(pl.multiple_of(lax.axis_index("mp") * share, share), share)
    pad = jnp.zeros((main.shape[0], HALF), F32)
    ends = (
        jnp.concatenate([low[...], pad], axis=1),
        jnp.concatenate([pad, high[...]], axis=1),
    )
    for j in range(length // 128):
        at = slice(j * 128, (j + 1) * 128)
        both = main[:, at]
        if j == 0:
            both = both + ends[0]
        if j == length // 128 - 1:
            both = both + ends[1]
        hat = both[0:share] * gain[own, 0:1]
        one = both[share : share + 1]
        two = both[share + 1 : share + 2]
        out[:, at] = middle_grad[:, at] + stats[1:2, at] * (hat - one - normed[:, at] * two)


def halves_kernel(keep, got, out_keep, out_send, *, axis):
    rows = out_keep.shape[0]
    index = lax.axis_index(axis) % 2

    def one(r, carry):
        mine = pl.ds(pl.multiple_of(index * rows + r, 16), 16)
        other = pl.ds(pl.multiple_of((1 - index) * rows + r, 16), 16)
        at = pl.ds(r, 16)
        out_keep[at, :] = keep[mine, :] + got[mine, :].astype(F32)
        out_send[at, :] = (keep[other, :] + got[other, :].astype(F32)).astype(BF16)
        return carry

    row_loop(rows, 16, one, 0)


def join_kernel(mine, other, out, *, axis):
    rows = mine.shape[0]
    index = lax.axis_index(axis) % 2
    out[pl.ds(pl.multiple_of(index * rows, 16), rows), :] = mine[...]
    out[pl.ds(pl.multiple_of((1 - index) * rows, 16), rows), :] = other[...]


def place_kernel(*refs, cuts, outs):
    count = len(cuts)
    pieces, targets, stack = refs[: 2 * count], refs[2 * count : -1], refs[-1]
    start = 0
    for i, (rows, order) in enumerate(cuts):
        size = rows // 2
        index = lax.axis_index(order[0]) % 2
        for k, at in enumerate((index, 1 - index)):
            at = pl.multiple_of(start + at * size, 16)
            stack[pl.ds(at, size), :] = pieces[2 * i + k][...].astype(F32)
        start += rows
    for target, spans in zip(targets, outs):
        at = 0
        for begin, size in spans:
            target[at : at + size, :] = stack[begin : begin + size, :]
            at += size


def flip(x, axis, bit):
    count = lax.axis_size(axis)
    return lax.ppermute(x, axis, [(i, i ^ bit) for i in range(count)])


def gather_mp(shard):
    across = flip(shard, "mp", 2)
    return shard, flip(shard, "mp", 1), across, flip(across, "mp", 1)


def held(x, other):
    return lax.optimization_barrier((x, other))[0]


def sum_halves(keep, send):
    half = (keep + flip(send, "mp", 1).astype(F32)).astype(BF16)
    across = flip(half, "mp", 2)
    total = (half.astype(F32) + across.astype(F32)).astype(BF16)
    return total, flip(total, "mp", 1), half


def scatter_shards(keep, send):
    rows, lanes = keep.shape
    rows = (rows - 16) // 2 + 16
    got = flip(send, "mp", 1)
    own, away = call(across_kernel, [((rows, lanes), F32), ((rows, lanes), BF16)], [], keep, got)
    return own, flip(away, "mp", 2)


def to_neighbours(low, high):
    count = lax.axis_size("seq")
    if count == 2:
        last = lax.axis_index("seq") == 1
        got = flip(jnp.where(last, low, high), "seq", 1)
        zero = jnp.zeros_like(got)
        return jnp.where(last, zero, got), jnp.where(last, got, zero)
    after = lax.ppermute(low, "seq", [(i + 1, i) for i in range(count - 1)])
    before = lax.ppermute(high, "seq", [(i, i + 1) for i in range(count - 1)])
    return after, before


def staged():
    return lax.axis_size("seq") == 2 and lax.axis_size("dp") == 4


def sum_blocks(x):
    if not staged():
        return lax.psum(x, ("dp", "seq"))
    for axis, bit in (("seq", 1), ("dp", 1), ("dp", 2)):
        x = x + flip(x, axis, bit)
    return x


def reduce_unit(keep, send, order):
    one, two = order
    rows, width = keep.shape
    got = flip(send, one, 1)
    keep, send = call(
        functools.partial(halves_kernel, axis=two),
        [((rows // 2, width), F32), ((rows // 2, width), BF16)],
        [],
        keep,
        got,
    )
    got = flip(send, two, 1)
    part = (keep + got.astype(F32)).astype(BF16)
    got = flip(part, "dp", 2)
    total = (part.astype(F32) + got.astype(F32)).astype(BF16)
    beside = flip(total, two, 1)
    (half,) = call(
        functools.partial(join_kernel, axis=two),
        [((rows, width), BF16)],
        [],
        total,
        beside,
    )
    return half, flip(half, one, 1)


def reduce_stack(parts, cuts):
    if cuts is None:
        return [lax.psum(parts[0], ("dp", "seq"))]
    pieces = []
    for i, (_, order) in enumerate(cuts):
        pieces.extend(reduce_unit(parts[2 * i], parts[2 * i + 1], order))
    return pieces


def place_stack(pieces, cuts, spans, width):
    sizes = [(sum(size for _, size in span), width) for span in spans]
    if cuts is None:
        return [jnp.concatenate([pieces[0][b : b + n] for b, n in span]) for span in spans]
    kernel = functools.partial(place_kernel, cuts=cuts, outs=spans)
    scratch = [((sum(rows for rows, _ in cuts), width), F32)]
    return call(kernel, [(size, F32) for size in sizes], scratch, *pieces)


def unit_shapes(cuts, rows, width):
    if cuts is None:
        return [((rows, width), F32)]
    shapes = []
    for size, _ in cuts:
        shapes += [((size // 2, width), F32), ((size // 2, width), BF16)]
    return shapes


def body(
    hidden_in,
    cotangent,
    attention_gain,
    feedforward_gain,
    qkv_weight,
    attention_out,
    geglu_in,
    geglu_out,
):
    length, share = hidden_in.shape[1:]
    width = qkv_weight.shape[0]
    columns = qkv_weight.shape[2]
    units = geglu_out.shape[0]
    heads = columns // HEAD
    tokens = length + TILE
    half = width // 2
    orders = (("seq", "dp"), ("dp", "seq"))
    grain = 8 * 16
    x_own = hidden_in[0].T
    u_own = cotangent[0].T
    w = jnp.transpose(qkv_weight, (1, 2, 0)).reshape(3 * columns, width)
    win = jnp.transpose(geglu_in, (1, 2, 0)).reshape(2 * units, width)
    gains = jnp.stack([attention_gain, feedforward_gain], axis=1)

    x_parts = gather_mp(x_own)
    after, before = to_neighbours(x_own[:, :HALF], x_own[:, length - HALF :])
    halo = jnp.concatenate([after, before], axis=1)
    h_parts = gather_mp(halo)
    u_parts = gather_mp(u_own)

    base = (lax.axis_index("seq") * length).astype(jnp.int32)
    spot = jnp.arange(tokens, dtype=jnp.int32)
    spot = jnp.where(spot < length + HALF, spot, spot - tokens) + base
    rates = jnp.exp(jnp.arange(HEAD // 2).astype(F32) * (-2.0 * math.log(10000.0) / HEAD))
    angles = rates[:, None] * spot.astype(F32)[None, :]
    cos, sin = jnp.cos(angles), jnp.sin(angles)

    xall, stats, fed, q, kw, vw, totals, mixed, keep, send = call(
        attention_kernel,
        [
            ((width, tokens), BF16),
            ((8, tokens), F32),
            ((width, tokens), BF16),
            ((columns, length), BF16),
            ((columns, tokens), BF16),
            ((columns, tokens), BF16),
            ((heads, 8, length), F32),
            ((columns, length), BF16),
            ((half, length), F32),
            ((half, length), BF16),
        ],
        [
            ((3 * columns, tokens), F32),
            ((width, length), F32),
            ((share, length), BF16),
            ((3 * columns, width), BF16),
            ((columns, width), BF16),
        ],
        *x_parts[1:], *h_parts, gains, cos, sin, x_own, w, attention_out,
        loads=3,
    )
    mine, other, _ = sum_halves(keep, send)
    middle_own, normed, inverse, fed_two, upstream, product, lifted_grad, keep, send = call(
        geglu_kernel,
        [
            ((share, length), F32),
            ((width, length), F32),
            ((8, length), F32),
            ((width, length), BF16),
            ((width, length), BF16),
            ((units, length), BF16),
            ((2 * units, length), BF16),
            ((half, length), F32),
            ((half, length), BF16),
        ],
        [
            ((width, length), F32),
            ((2 * units, length), F32),
            ((units, length), F32),
            ((width, length), F32),
        ],
        xall, mine, other, *u_parts, gains, win, geglu_out,
    )
    mine, other, half_sent = sum_halves(keep, send)

    (normed_own,) = call(
        own_rows_kernel, [((share, tokens), F32)], [], xall, held(stats, half_sent)
    )
    rows = 3 * units
    padded = -(-rows // grain) * grain if staged() else rows
    geglu_cuts = tuple((padded // 2, order) for order in orders) if staged() else None
    geglu_parts = call(
        functools.partial(geglu_weights_kernel, cuts=geglu_cuts),
        unit_shapes(geglu_cuts, padded, width),
        [((padded, width), F32)],
        held(product, half_sent), lifted_grad, fed_two, upstream,
    )

    back_cuts = None
    if staged() and 4 * columns % grain == 0:
        back_cuts = tuple((2 * columns, order) for order in orders)
    outs = call(
        functools.partial(attention_back_kernel, cuts=back_cuts),
        [((share, length), F32), ((share, 128), F32), ((3 * columns, tokens), BF16)]
        + unit_shapes(back_cuts, 4 * columns, width),
        [
            ((width, length), F32),
            ((width, length), BF16),
            ((columns, length), BF16),
            ((columns, tokens), F32),
            ((columns, tokens), F32),
            ((4 * columns, width), F32),
        ],
        mine, other, normed, inverse, gains, upstream, attention_out,
        q, kw, vw, totals, mixed, cos, sin, fed,
    )
    middle_grad, gain_two_lanes, proj_grad = outs[:3]
    pieces = reduce_stack(geglu_parts, geglu_cuts)
    grad_in, grad_out = place_stack(
        pieces, geglu_cuts, (((0, 2 * units),), ((2 * units, units),)), width
    )
    back_pieces = reduce_stack(outs[3:], back_cuts)

    lanes = tokens + length
    keep, send = call(
        terms_kernel,
        [((2 * share + 16, lanes), F32), ((2 * share + 16, lanes), BF16)],
        [((width, lanes), F32)],
        proj_grad, w, gains, xall, stats, geglu_out, product,
    )
    own, got = scatter_shards(keep, send)
    layer_out, main, edges, gain_sums = call(
        finish_kernel,
        [
            ((share, length), F32),
            ((share + 16, length), F32),
            ((share + 16, TILE), F32),
            ((16, share), F32),
        ],
        [],
        own, got, middle_own, normed_own, gain_two_lanes,
    )
    high_add, low_add = to_neighbours(edges[:, HALF:], edges[:, :HALF])
    gain_sums = sum_blocks(gain_sums)
    (grad_input,) = call(
        input_kernel,
        [((share, length), F32)],
        [],
        main, low_add, high_add, middle_grad, stats, normed_own, gains,
    )
    grad_qkv, grad_attention_out = place_stack(
        held(back_pieces, (gain_sums, grad_input, layer_out)),
        back_cuts,
        (((2 * columns, 2 * columns), (0, columns)), ((columns, columns),)),
        width,
    )
    return (
        layer_out.T[None],
        grad_input.T[None],
        jnp.transpose(grad_qkv.reshape(3, columns, width), (2, 0, 1)),
        grad_attention_out,
        jnp.transpose(grad_in.reshape(2, units, width), (2, 0, 1)),
        grad_out,
        gain_sums[0],
        gain_sums[8],
    )


def solution(mesh):
    in_specs = (
        P("dp", "seq", "mp"),
        P("dp", "seq", "mp"),
        P(),
        P(),
        P(None, None, "mp"),
        P("mp", None),
        P(None, None, "mp"),
        P("mp", None),
    )
    out_specs = (
        P("dp", "seq", "mp"),
        P("dp", "seq", "mp"),
        P(None, None, "mp"),
        P("mp", None),
        P(None, None, "mp"),
        P("mp", None),
        P("mp"),
        P("mp"),
    )

    return jax.shard_map(body, mesh=mesh, in_specs=in_specs, out_specs=out_specs, check_vma=False)
```

```python
import functools
import math

import jax
import jax.numpy as jnp
from jax import lax
from jax.experimental import pallas as pl
from jax.experimental.pallas import tpu as pltpu
from jax.sharding import PartitionSpec as P


HEAD = 64
HALF = 64
TILE = 2 * HALF
STEP = 64
GRANT = 8 * 1024 * 1024
F32 = jnp.float32
BF16 = jnp.bfloat16


def room(shape, dtype):
    lanes = -(-shape[-1] // 128) * 128
    return math.prod(shape[:-1]) * lanes * jnp.dtype(dtype).itemsize


def call(kernel, outs, scratch, *args, loads=0):
    grant = sum(room(s, t) for s, t in scratch) + GRANT
    extra = [pltpu.SemaphoreType.DMA((loads,))] if loads else []
    spaces = [pltpu.VMEM] * (len(args) - loads) + [pltpu.HBM] * loads
    run = pl.pallas_call(
        kernel,
        out_shape=tuple(jax.ShapeDtypeStruct(s, t) for s, t in outs),
        in_specs=[pl.BlockSpec(memory_space=space) for space in spaces],
        scratch_shapes=[pltpu.VMEM(s, t) for s, t in scratch] + extra,
        compiler_params=pltpu.CompilerParams(vmem_limit_bytes=grant),
    )
    if loads:
        far = [pltpu.with_memory_space_constraint(a, pltpu.HBM) for a in args[-loads:]]
        args = args[:-loads] + tuple(far)
    return run(*args)


def nn(a, b):
    return lax.dot_general(a, b, (((1,), (0,)), ((), ())), preferred_element_type=F32)


def tn(a, b):
    return lax.dot_general(a, b, (((0,), (0,)), ((), ())), preferred_element_type=F32)


def nt(a, b):
    return lax.dot_general(a, b, (((1,), (1,)), ((), ())), preferred_element_type=F32)


def row_loop(rows, step, fn, init):
    def one(i, carry):
        return fn(pl.multiple_of(i * step, step), carry)

    return lax.fori_loop(0, rows // step, one, init)


def fold(x):
    return jnp.sum(x.reshape(x.shape[0] // 8, 8, x.shape[1]), axis=0)


def fill_bias(bias, first, length, total):
    shape = (2 * TILE, TILE)
    key = lax.broadcasted_iota(jnp.int32, shape, 0)
    gap = key - lax.broadcasted_iota(jnp.int32, shape, 1)
    near = (gap >= 0) & (gap <= TILE)
    low = key + (first - HALF) >= 0
    high = key + (first + length - TILE - HALF) < total
    if length == TILE:
        low = low & high
    for k, allowed in enumerate((near & low, near, near & high)):
        bias[k] = jnp.where(allowed, 0.0, -1e30)


def bias_of(bias, tile, count):
    if tile == 0:
        return bias[0]
    return bias[2] if tile == count - 1 else bias[1]


def gather_rows(pieces, target, lanes):
    me = lax.axis_index("mp")
    share = pieces[0].shape[0]
    for k, piece in enumerate(pieces):
        start = pl.multiple_of(jnp.bitwise_xor(me, k) * share, share)
        target[pl.ds(start, share), lanes] = piece[...]


def split_half(source, keep, send, index):
    rows = keep.shape[0]

    def one(r, carry):
        mine = pl.multiple_of(index * rows + r, 16)
        other = pl.multiple_of((1 - index) * rows + r, 16)
        keep[pl.ds(r, 16), :] = source[pl.ds(mine, 16), :]
        send[pl.ds(r, 16), :] = source[pl.ds(other, 16), :].astype(send.dtype)
        return carry

    row_loop(rows, 16, one, 0)


def attention_kernel(
    p1, p2, p3, h0, h1, h2, h3, gain, cos, sin, p0_far, w_far, wo_far,
    xall, stats, fed, q, kw, kt, vt, totals, mixed, keep, send,
    proj, terms, p0, w, wo, bias, sems,
):
    copies = [
        pltpu.make_async_copy(p0_far, p0, sems.at[0]),
        pltpu.make_async_copy(w_far, w, sems.at[1]),
        pltpu.make_async_copy(wo_far, wo, sems.at[2]),
    ]
    for copy in copies:
        copy.start()
    width, tokens = xall.shape
    length = q.shape[1]
    columns = q.shape[0]
    heads = columns // HEAD
    core = lax.axis_index("mp") % 2
    first = lax.axis_index("seq") * length
    total = lax.axis_size("seq") * length
    fill_bias(bias, first, length, total)
    gather_rows((h0, h1, h2, h3), xall, slice(length, tokens))
    copies[0].wait()
    gather_rows((p0, p1, p2, p3), xall, slice(0, length))

    def add(r, acc):
        return acc + fold(xall[pl.ds(r, STEP), :].astype(F32))

    zero = jnp.zeros((8, tokens), F32)
    mean = jnp.sum(row_loop(width, STEP, add, zero), axis=0, keepdims=True) / width

    def add_square(r, acc):
        center = xall[pl.ds(r, STEP), :].astype(F32) - mean
        return acc + fold(center * center)

    var = jnp.sum(row_loop(width, STEP, add_square, zero), axis=0, keepdims=True) / width
    inverse = lax.rsqrt(var + 1e-05)
    stats[0:1, :] = mean
    stats[1:2, :] = inverse
    stats[2:8, :] = jnp.zeros((6, tokens), F32)

    def feed(r, carry):
        normed = (xall[pl.ds(r, STEP), :].astype(F32) - mean) * inverse
        fed[pl.ds(r, STEP), :] = (normed * gain[pl.ds(r, STEP), 0:1]).astype(BF16)
        return carry

    row_loop(width, STEP, feed, 0)
    copies[1].wait()
    proj[...] = nn(w[...], fed[...])
    half = HEAD // 2

    def rope(row, lanes):
        a = proj[pl.ds(row, half), lanes]
        b = proj[pl.ds(row + half, half), lanes]
        c = cos[:, lanes]
        s = sin[:, lanes]
        return a * c - b * s, b * c + a * s

    def one_head(h, carry):
        row = pl.multiple_of(h * HEAD, HEAD)
        own = slice(0, length)
        every = slice(0, tokens)
        upper, lower = rope(row, own)
        q[pl.ds(row, half), :] = upper.astype(BF16)
        q[pl.ds(row + half, half), :] = lower.astype(BF16)
        keys = jnp.concatenate(rope(columns + row, every), axis=0)
        keys = pltpu.roll(keys, HALF, 1)
        kw[pl.ds(row, HEAD), :] = keys.astype(BF16)
        kt[h] = keys.T.astype(BF16)
        value = pltpu.roll(proj[pl.ds(2 * columns + row, HEAD), :], HALF, 1)
        vt[h] = value.T.astype(BF16)
        value = value.astype(BF16)
        count = length // TILE
        for j in range(count):
            wide = slice(j * TILE, (j + 2) * TILE)
            mine = slice(j * TILE, (j + 1) * TILE)
            scores = nn(kt[h, wide, :], q[pl.ds(row, HEAD), mine]) * HEAD**-0.5
            scores = scores + bias_of(bias, j, count)
            top = jnp.max(scores, axis=0, keepdims=True)
            raised = jnp.exp(scores - top)
            amount = jnp.sum(raised, axis=0, keepdims=True)
            weights = (raised * (1.0 / amount)).astype(BF16)
            totals[h, 0:1, mine] = top + jnp.log(amount)
            mixed[pl.ds(row, HEAD), mine] = nn(value[:, wide], weights).astype(BF16)
        return carry

    lax.fori_loop(0, heads, one_head, 0)
    copies[2].wait()
    terms[...] = tn(wo[...], mixed[...])
    split_half(terms, keep, send, core)


def flip_weights_kernel(*refs):
    for source, target in zip(refs[:3], refs[3:]):
        target[...] = source[...].T


def geglu_kernel(
    xall, mine, other, u0, u1, u2, u3, gain, win, win_t, gout,
    middle_own, normed, inverse_out, fed, upstream, product, lifted_grad, keep, send,
    middle, lifted, grad_product, terms,
):
    width, length = normed.shape
    share = middle_own.shape[0]
    units = product.shape[0]
    rows = mine.shape[0]
    me = lax.axis_index("mp")
    core = me % 2
    gather_rows((u0, u1, u2, u3), upstream, slice(0, length))
    own = slice(0, length)

    def add(r, acc):
        for part, index in ((mine, core), (other, 1 - core)):
            at = pl.multiple_of(index * rows + r, STEP)
            value = xall[pl.ds(at, STEP), own].astype(F32) + part[pl.ds(r, STEP), :].astype(F32)
            middle[pl.ds(at, STEP), :] = value
            acc = acc + fold(value)
        return acc

    zero = jnp.zeros((8, length), F32)
    mean = jnp.sum(row_loop(rows, STEP, add, zero), axis=0, keepdims=True) / width

    def add_square(r, acc):
        center = middle[pl.ds(r, STEP), :] - mean
        return acc + fold(center * center)

    var = jnp.sum(row_loop(width, STEP, add_square, zero), axis=0, keepdims=True) / width
    inverse = lax.rsqrt(var + 1e-05)
    inverse_out[...] = jnp.broadcast_to(inverse, inverse_out.shape)

    def feed(r, carry):
        value = (middle[pl.ds(r, STEP), :] - mean) * inverse
        normed[pl.ds(r, STEP), :] = value
        fed[pl.ds(r, STEP), :] = (value * gain[pl.ds(r, STEP), 1:2]).astype(BF16)
        return carry

    row_loop(width, STEP, feed, 0)
    middle_own[...] = middle[pl.ds(pl.multiple_of(me * share, share), share), :]
    lifted[...] = nn(win[...], fed[...])
    grad_product[...] = nn(gout[...], upstream[...])

    def unit(r, carry):
        at = pl.ds(r, 32)
        gate = pl.ds(pl.multiple_of(units + r, 32), 32)
        linear = lifted[at, :]
        gating = lifted[gate, :]
        grad = grad_product[at, :]
        area = 0.5 * (1.0 + lax.erf(linear * 0.7071067811865476))
        activated = linear * area
        slope = area + linear * jnp.exp(-0.5 * linear * linear) * 0.3989422804014327
        product[at, :] = (activated * gating).astype(BF16)
        lifted_grad[at, :] = (grad * gating * slope).astype(BF16)
        lifted_grad[gate, :] = (grad * activated).astype(BF16)
        return carry

    row_loop(units, 32, unit, 0)
    terms[...] = nn(win_t[...], lifted_grad[...])
    split_half(terms, keep, send, core)


def geglu_weights_kernel(product, lifted_grad, fed, upstream, *rest, cuts):
    outs, stack = rest[:-1], rest[-1]
    count = lifted_grad.shape[0]
    units = product.shape[0]
    stack[0:count, :] = nt(lifted_grad[...], fed[...])
    stack[count : count + units, :] = nt(product[...], upstream[...])
    if stack.shape[0] > count + units:
        stack[count + units :, :] = jnp.zeros((stack.shape[0] - count - units, stack.shape[1]), F32)
    emit_units(stack, outs, cuts)


def emit_units(stack, outs, cuts):
    if cuts is None:
        outs[0][...] = stack[...]
        return
    start = 0
    for i, (rows, order) in enumerate(cuts):
        index = lax.axis_index(order[0]) % 2
        split_half(stack.at[pl.ds(start, rows), :], outs[2 * i], outs[2 * i + 1], index)
        start += rows


def attention_back_kernel(
    mine, other, normed, inverse, gain, upstream, wo, q, kw, kt, vt, totals, mixed, cos, sin, fed, *rest,
    cuts,
):
    outs, (full, low, mixed_grad, dk, dv, stack, bias) = rest[:-7], rest[-7:]
    middle_grad_own, gain_grad, proj_grad = outs[:3]
    width, length = normed.shape
    columns = q.shape[0]
    heads = columns // HEAD
    tokens = kw.shape[1]
    rows = mine.shape[0]
    share = middle_grad_own.shape[0]
    me = lax.axis_index("mp")
    core = me % 2
    first = lax.axis_index("seq") * length
    total = lax.axis_size("seq") * length
    inv = inverse[0:1, :]
    fill_bias(bias, first, length, total)

    def add(r, acc):
        a, b = acc
        for part, index in ((mine, core), (other, 1 - core)):
            at = pl.multiple_of(index * rows + r, STEP)
            grad = part[pl.ds(r, STEP), :].astype(F32)
            full[pl.ds(at, STEP), :] = grad
            hat = grad * gain[pl.ds(at, STEP), 1:2]
            a = a + fold(hat)
            b = b + fold(hat * normed[pl.ds(at, STEP), :])
        return a, b

    zero = jnp.zeros((8, length), F32)
    a, b = row_loop(rows, STEP, add, (zero, zero))
    one = jnp.sum(a, axis=0, keepdims=True) / width
    two = jnp.sum(b, axis=0, keepdims=True) / width
    start = pl.multiple_of(me * share, share)
    weighted = full[pl.ds(start, share), :] * normed[pl.ds(start, share), :]
    lanes = weighted[:, 0:128]
    for j in range(1, length // 128):
        lanes = lanes + weighted[:, j * 128 : (j + 1) * 128]
    gain_grad[...] = lanes

    def back(r, carry):
        at = pl.ds(r, STEP)
        hat = full[at, :] * gain[at, 1:2]
        value = upstream[at, :].astype(F32) + inv * (hat - one - normed[at, :] * two)
        full[at, :] = value
        low[at, :] = value.astype(BF16)
        return carry

    row_loop(width, STEP, back, 0)
    middle_grad_own[...] = full[pl.ds(start, share), :]
    mixed_grad[...] = nn(wo[...], low[...]).astype(BF16)
    dk[...] = jnp.zeros(dk.shape, F32)
    dv[...] = jnp.zeros(dv.shape, F32)
    half = HEAD // 2
    every = slice(0, tokens)

    def unrope(a, b, lanes):
        c = cos[:, lanes]
        s = sin[:, lanes]
        return a * c + b * s, b * c - a * s

    def one_head(h, carry):
        row = pl.multiple_of(h * HEAD, HEAD)
        head = pl.ds(row, HEAD)
        for j in range(length // TILE):
            wide = slice(j * TILE, (j + 2) * TILE)
            here = slice(j * TILE, (j + 1) * TILE)
            keys = kw[head, wide]
            query = q[head, here]
            grad = mixed_grad[head, here]
            scores = nn(kt[h, wide, :], query) * HEAD**-0.5
            scores = scores + bias_of(bias, j, length // TILE)
            probs = jnp.exp(scores - totals[h, 0:1, here])
            both = grad.astype(F32) * mixed[head, here].astype(F32)
            delta = jnp.sum(both, axis=0, keepdims=True)
            dv[head, wide] += nt(grad, probs.astype(BF16))
            grad_probs = nn(vt[h, wide, :], grad)
            grad_scores = (probs * (grad_probs - delta) * HEAD**-0.5).astype(BF16)
            dk[head, wide] += nt(query, grad_scores)
            dq = nn(keys, grad_scores)
            upper, lower = unrope(dq[:half], dq[half:], here)
            proj_grad[pl.ds(row, half), here] = upper.astype(BF16)
            proj_grad[pl.ds(row + half, half), here] = lower.astype(BF16)
        proj_grad[head, length:tokens] = jnp.zeros((HEAD, tokens - length), BF16)
        keys_grad = pltpu.roll(dk[head, :], tokens - HALF, 1)
        upper, lower = unrope(keys_grad[:half], keys_grad[half:], every)
        at = pl.multiple_of(columns + row, HEAD)
        proj_grad[pl.ds(at, half), :] = upper.astype(BF16)
        proj_grad[pl.ds(at + half, half), :] = lower.astype(BF16)
        at = pl.multiple_of(2 * columns + row, HEAD)
        proj_grad[pl.ds(at, HEAD), :] = pltpu.roll(dv[head, :], tokens - HALF, 1).astype(BF16)
        return carry

    lax.fori_loop(0, heads, one_head, 0)
    stack[0:columns, :] = nt(proj_grad[2 * columns : 3 * columns, :], fed[...])
    stack[columns : 2 * columns, :] = nt(mixed[...], low[...])
    stack[2 * columns : 4 * columns, :] = nt(proj_grad[0 : 2 * columns, :], fed[...])
    emit_units(stack, outs[3:], cuts)


def terms_kernel(
    proj_grad, w, gain, xall, stats, gout, product,
    keep, send, terms,
):
    width, tokens = xall.shape
    share = (keep.shape[0] - 16) // 2
    me = lax.axis_index("mp")
    core = me % 2
    terms[:, 0:tokens] = nn(w[...], proj_grad[...])
    mean = stats[0:1, :]
    inverse = stats[1:2, :]

    def add(r, acc):
        a, b = acc
        at = pl.ds(r, STEP)
        hat = terms[at, 0:tokens] * gain[at, 0:1]
        normed = (xall[at, :].astype(F32) - mean) * inverse
        return a + fold(hat), b + fold(hat * normed)

    zero = jnp.zeros((8, tokens), F32)
    a, b = row_loop(width, STEP, add, (zero, zero))
    one = jnp.sum(a, axis=0, keepdims=True) / width
    two = jnp.sum(b, axis=0, keepdims=True) / width
    terms[:, tokens:] = nn(gout[...], product[...])
    for x in range(2):
        mine = pl.multiple_of((2 * x + core) * share, share)
        other = pl.multiple_of((2 * x + 1 - core) * share, share)
        at = slice(x * share, (x + 1) * share)
        keep[at, :] = terms[pl.ds(mine, share), :]
        send[at, :] = terms[pl.ds(other, share), :].astype(BF16)
    rest = slice(2 * share, 2 * share + 16)
    row = lax.broadcasted_iota(jnp.int32, (16, tokens), 0)
    sums = jnp.where(row == 0, one, jnp.where(row == 1, two, 0.0))
    keep[rest, 0:tokens] = sums
    send[rest, 0:tokens] = sums.astype(BF16)
    keep[rest, tokens:] = jnp.zeros((16, terms.shape[1] - tokens), F32)
    send[rest, tokens:] = jnp.zeros((16, terms.shape[1] - tokens), BF16)


def own_rows_kernel(xall, stats, out):
    share = out.shape[0]
    own = pl.ds(pl.multiple_of(lax.axis_index("mp") * share, share), share)
    out[...] = (xall[own, :].astype(F32) - stats[0:1, :]) * stats[1:2, :]


def across_kernel(keep, got, own, away):
    share = (keep.shape[0] - 16) // 2
    x = lax.axis_index("mp") // 2
    for out, index in ((own, x), (away, 1 - x)):
        at = pl.ds(pl.multiple_of(index * share, share), share)
        out[0:share, :] = (keep[at, :] + got[at, :].astype(F32)).astype(out.dtype)
        last = slice(2 * share, 2 * share + 16)
        out[share : share + 16, :] = (keep[last, :] + got[last, :].astype(F32)).astype(out.dtype)


def finish_kernel(own, got, middle, normed, gain_lanes, layer_out, main, edges, gains):
    share, length = middle.shape
    tokens = normed.shape[1]
    layer_out[...] = middle[...] + own[0:share, tokens:] + got[0:share, tokens:].astype(F32)
    main[...] = own[:, 0:length] + got[:, 0:length].astype(F32)
    edges[...] = own[:, length:tokens] + got[:, length:tokens].astype(F32)
    weighted = gain_lanes[...], main[0:share, :] * normed[:, 0:length]
    last = edges[0:share, :] * normed[:, length:tokens]
    exact = functools.partial(
        lax.dot_general,
        dimension_numbers=(((1,), (1,)), ((), ())),
        precision=lax.Precision.HIGHEST,
        preferred_element_type=F32,
    )
    one = exact(jnp.ones((8, length), F32), weighted[1])
    gains[...] = jnp.zeros(gains.shape, F32)
    gains[0:8, 0:share] = one + exact(jnp.ones((8, tokens - length), F32), last)
    gains[8:16, 0:share] = exact(jnp.ones((8, gain_lanes.shape[1]), F32), weighted[0])


def input_kernel(main, low, high, middle_grad, stats, normed, gain, out):
    share, length = out.shape
    own = pl.ds(pl.multiple_of(lax.axis_index("mp") * share, share), share)
    pad = jnp.zeros((main.shape[0], HALF), F32)
    ends = (
        jnp.concatenate([low[...], pad], axis=1),
        jnp.concatenate([pad, high[...]], axis=1),
    )
    for j in range(length // 128):
        at = slice(j * 128, (j + 1) * 128)
        both = main[:, at]
        if j == 0:
            both = both + ends[0]
        if j == length // 128 - 1:
            both = both + ends[1]
        hat = both[0:share] * gain[own, 0:1]
        one = both[share : share + 1]
        two = both[share + 1 : share + 2]
        out[:, at] = middle_grad[:, at] + stats[1:2, at] * (hat - one - normed[:, at] * two)


def halves_kernel(keep, got, out_keep, out_send, *, axis):
    rows = out_keep.shape[0]
    index = lax.axis_index(axis) % 2

    def one(r, carry):
        mine = pl.ds(pl.multiple_of(index * rows + r, 16), 16)
        other = pl.ds(pl.multiple_of((1 - index) * rows + r, 16), 16)
        at = pl.ds(r, 16)
        out_keep[at, :] = keep[mine, :] + got[mine, :].astype(F32)
        out_send[at, :] = (keep[other, :] + got[other, :].astype(F32)).astype(BF16)
        return carry

    row_loop(rows, 16, one, 0)


def part_kernel(keep, got, rest, out):
    rows = keep.shape[0]
    out[0:rows, :] = (keep[...] + got[...].astype(F32)).astype(BF16)
    out[rows:, :] = rest[...].astype(BF16)


def join_kernel(mine, other, out, *, axis, rows):
    index = lax.axis_index(axis) % 2
    out[pl.ds(pl.multiple_of(index * rows, 16), rows), :] = mine[0:rows, :]
    out[pl.ds(pl.multiple_of((1 - index) * rows, 16), rows), :] = other[0:rows, :]
    if mine.shape[0] > rows:
        rest = mine[rows:, :].astype(F32) + other[rows:, :].astype(F32)
        out[2 * rows :, :] = rest.astype(BF16)


def place_kernel(*refs, cuts, outs):
    count = len(cuts)
    pieces, targets, stack = refs[: 2 * count], refs[2 * count : -1], refs[-1]
    start = 0
    for i, (rows, order) in enumerate(cuts):
        size = rows // 2
        index = lax.axis_index(order[0]) % 2
        for k, at in enumerate((index, 1 - index)):
            at = pl.multiple_of(start + at * size, 16)
            stack[pl.ds(at, size), :] = pieces[2 * i + k][0:size, :].astype(F32)
        start += rows
    for target, spans in zip(targets, outs):
        at = 0
        for begin, size in spans:
            target[at : at + size, :] = stack[begin : begin + size, :]
            at += size


def flip(x, axis, bit):
    count = lax.axis_size(axis)
    return lax.ppermute(x, axis, [(i, i ^ bit) for i in range(count)])


def gather_mp(shard):
    across = flip(shard, "mp", 2)
    beside = flip(shard, "mp", 1)
    return shard, beside, across, flip(across, "mp", 1)


def held(x, other):
    return lax.optimization_barrier((x, other))[0]


def sum_halves(keep, send):
    got = flip(send, "mp", 1)
    half = (keep + got.astype(F32)).astype(BF16)
    across = flip(half, "mp", 2)
    total = (half.astype(F32) + across.astype(F32)).astype(BF16)
    return total, flip(total, "mp", 1), half


def scatter_shards(keep, send):
    rows, lanes = keep.shape
    rows = (rows - 16) // 2 + 16
    got = flip(send, "mp", 1)
    own, away = call(across_kernel, [((rows, lanes), F32), ((rows, lanes), BF16)], [], keep, got)
    return own, flip(away, "mp", 2)


def to_neighbours(low, high):
    count = lax.axis_size("seq")
    if count == 2:
        last = lax.axis_index("seq") == 1
        got = flip(jnp.where(last, low, high), "seq", 1)
        zero = jnp.zeros_like(got)
        return jnp.where(last, zero, got), jnp.where(last, got, zero)
    after = lax.ppermute(low, "seq", [(i + 1, i) for i in range(count - 1)])
    before = lax.ppermute(high, "seq", [(i, i + 1) for i in range(count - 1)])
    return after, before


def staged():
    return lax.axis_size("seq") == 2 and lax.axis_size("dp") == 4


def reduce_unit(keep, send, order, rest=None):
    one, two = order
    rows, width = keep.shape
    got = flip(send, one, 1)
    keep, send = call(
        functools.partial(halves_kernel, axis=two),
        [((rows // 2, width), F32), ((rows // 2, width), BF16)],
        [],
        keep,
        got,
    )
    got = flip(send, two, 1)
    if rest is None:
        part = (keep + got.astype(F32)).astype(BF16)
    else:
        shape = (keep.shape[0] + rest.shape[0], width)
        (part,) = call(part_kernel, [(shape, BF16)], [], keep, got, rest)
    got = flip(part, "dp", 2)
    total = (part.astype(F32) + got.astype(F32)).astype(BF16)
    beside = flip(total, two, 1)
    (half,) = call(
        functools.partial(join_kernel, axis=two, rows=rows // 2),
        [((rows + (0 if rest is None else rest.shape[0]), width), BF16)],
        [],
        total,
        beside,
    )
    return half, flip(half, one, 1)


def reduce_stack(parts, cuts, rest=None):
    if cuts is None:
        return [lax.psum(parts[0], ("dp", "seq"))], rest if rest is None else lax.psum(rest, ("dp", "seq"))
    pieces = []
    for i, (_, order) in enumerate(cuts):
        more = rest if i == len(cuts) - 1 else None
        pieces.extend(reduce_unit(parts[2 * i], parts[2 * i + 1], order, more))
    if rest is not None:
        rest = sum(p[-rest.shape[0] :].astype(F32) for p in pieces[-2:])
    return pieces, rest


def place_stack(pieces, cuts, spans, width):
    sizes = [(sum(size for _, size in span), width) for span in spans]
    if cuts is None:
        return [jnp.concatenate([pieces[0][b : b + n] for b, n in span]) for span in spans]
    kernel = functools.partial(place_kernel, cuts=cuts, outs=spans)
    scratch = [((sum(rows for rows, _ in cuts), width), F32)]
    return call(kernel, [(size, F32) for size in sizes], scratch, *pieces)


def unit_shapes(cuts, rows, width):
    if cuts is None:
        return [((rows, width), F32)]
    shapes = []
    for size, _ in cuts:
        shapes += [((size // 2, width), F32), ((size // 2, width), BF16)]
    return shapes


def body(
    hidden_in,
    cotangent,
    attention_gain,
    feedforward_gain,
    qkv_weight,
    attention_out,
    geglu_in,
    geglu_out,
):
    length, share = hidden_in.shape[1:]
    width = qkv_weight.shape[0]
    columns = qkv_weight.shape[2]
    units = geglu_out.shape[0]
    heads = columns // HEAD
    tokens = length + TILE
    half = width // 2
    orders = (("seq", "dp"), ("dp", "seq"))
    grain = 8 * 16
    x_own = hidden_in[0].T
    u_own = cotangent[0].T
    w = jnp.transpose(qkv_weight, (1, 2, 0)).reshape(3 * columns, width)
    win = jnp.transpose(geglu_in, (1, 2, 0)).reshape(2 * units, width)
    gains = jnp.stack([attention_gain, feedforward_gain], axis=1)

    after, before = to_neighbours(x_own[:, :HALF], x_own[:, length - HALF :])
    x_parts = gather_mp(x_own)
    halo = jnp.concatenate([after, before], axis=1)
    h_parts = gather_mp(halo)
    u_parts = gather_mp(u_own)

    base = (lax.axis_index("seq") * length).astype(jnp.int32)
    spot = jnp.arange(tokens, dtype=jnp.int32)
    spot = jnp.where(spot < length + HALF, spot, spot - tokens) + base
    rates = jnp.exp(jnp.arange(HEAD // 2).astype(F32) * (-2.0 * math.log(10000.0) / HEAD))
    angles = rates[:, None] * spot.astype(F32)[None, :]
    cos, sin = jnp.cos(angles), jnp.sin(angles)

    xall, stats, fed, q, kw, kt, vt, totals, mixed, keep, send = call(
        attention_kernel,
        [
            ((width, tokens), BF16),
            ((8, tokens), F32),
            ((width, tokens), BF16),
            ((columns, length), BF16),
            ((columns, tokens), BF16),
            ((heads, tokens, HEAD), BF16),
            ((heads, tokens, HEAD), BF16),
            ((heads, 8, length), F32),
            ((columns, length), BF16),
            ((half, length), F32),
            ((half, length), BF16),
        ],
        [
            ((3 * columns, tokens), F32),
            ((width, length), F32),
            ((share, length), BF16),
            ((3 * columns, width), BF16),
            ((columns, width), BF16),
            ((3, 2 * TILE, TILE), F32),
        ],
        *x_parts[1:], *h_parts, gains, cos, sin, x_own, w, attention_out,
        loads=3,
    )
    mine, other, half_one = sum_halves(keep, send)
    win_t, w_t, gout_t = call(
        flip_weights_kernel,
        [((width, 2 * units), BF16), ((width, 3 * columns), BF16), ((width, units), BF16)],
        [],
        held(win, half_one), w, geglu_out,
    )
    middle_own, normed, inverse, fed_two, upstream, product, lifted_grad, keep, send = call(
        geglu_kernel,
        [
            ((share, length), F32),
            ((width, length), F32),
            ((8, length), F32),
            ((width, length), BF16),
            ((width, length), BF16),
            ((units, length), BF16),
            ((2 * units, length), BF16),
            ((half, length), F32),
            ((half, length), BF16),
        ],
        [
            ((width, length), F32),
            ((2 * units, length), F32),
            ((units, length), F32),
            ((width, length), F32),
        ],
        xall, mine, other, *u_parts, gains, win, win_t, geglu_out,
    )
    mine, other, half_sent = sum_halves(keep, send)

    (normed_own,) = call(
        own_rows_kernel, [((share, tokens), F32)], [], xall, held(stats, half_sent)
    )
    rows = 3 * units
    padded = -(-rows // grain) * grain if staged() else rows
    geglu_cuts = tuple((padded // 2, order) for order in orders) if staged() else None
    geglu_parts = call(
        functools.partial(geglu_weights_kernel, cuts=geglu_cuts),
        unit_shapes(geglu_cuts, padded, width),
        [((padded, width), F32)],
        held(product, half_sent), lifted_grad, fed_two, upstream,
    )

    back_cuts = None
    if staged() and 4 * columns % grain == 0:
        back_cuts = ((2 * columns, orders[0]),) * 2
    outs = call(
        functools.partial(attention_back_kernel, cuts=back_cuts),
        [((share, length), F32), ((share, 128), F32), ((3 * columns, tokens), BF16)]
        + unit_shapes(back_cuts, 4 * columns, width),
        [
            ((width, length), F32),
            ((width, length), BF16),
            ((columns, length), BF16),
            ((columns, tokens), F32),
            ((columns, tokens), F32),
            ((4 * columns, width), F32),
            ((3, 2 * TILE, TILE), F32),
        ],
        mine, other, normed, inverse, gains, upstream, attention_out,
        q, kw, kt, vt, totals, mixed, cos, sin, fed,
    )
    middle_grad, gain_two_lanes, proj_grad = outs[:3]
    pieces, _ = reduce_stack(geglu_parts, geglu_cuts)
    grad_in, grad_out = place_stack(
        pieces, geglu_cuts, (((0, 2 * units),), ((2 * units, units),)), width
    )
    back_parts = outs[3:]

    lanes = tokens + length
    keep, send = call(
        terms_kernel,
        [((2 * share + 16, lanes), F32), ((2 * share + 16, lanes), BF16)],
        [((width, lanes), F32)],
        proj_grad, w_t, gains, xall, stats, gout_t, product,
    )
    own, got = scatter_shards(keep, send)
    layer_out, main, edges, gain_sums = call(
        finish_kernel,
        [
            ((share, length), F32),
            ((share + 16, length), F32),
            ((share + 16, TILE), F32),
            ((16, width), F32),
        ],
        [],
        own, got, middle_own, normed_own, gain_two_lanes,
    )
    high_add, low_add = to_neighbours(edges[:, HALF:], edges[:, :HALF])
    back_pieces, gain_sums = reduce_stack(back_parts, back_cuts, gain_sums)
    (grad_input,) = call(
        input_kernel,
        [((share, length), F32)],
        [],
        main, low_add, high_add, middle_grad, stats, normed_own, gains,
    )
    grad_qkv, grad_attention_out = place_stack(
        held(back_pieces, (grad_input, layer_out)),
        back_cuts,
        (((2 * columns, 2 * columns), (0, columns)), ((columns, columns),)),
        width,
    )
    return (
        layer_out.T[None],
        grad_input.T[None],
        jnp.transpose(grad_qkv.reshape(3, columns, width), (2, 0, 1)),
        grad_attention_out,
        jnp.transpose(grad_in.reshape(2, units, width), (2, 0, 1)),
        grad_out,
        gain_sums[0, :share],
        gain_sums[8, :share],
    )


def solution(mesh):
    in_specs = (
        P("dp", "seq", "mp"),
        P("dp", "seq", "mp"),
        P(),
        P(),
        P(None, None, "mp"),
        P("mp", None),
        P(None, None, "mp"),
        P("mp", None),
    )
    out_specs = (
        P("dp", "seq", "mp"),
        P("dp", "seq", "mp"),
        P(None, None, "mp"),
        P("mp", None),
        P(None, None, "mp"),
        P("mp", None),
        P("mp"),
        P("mp"),
    )

    return jax.shard_map(body, mesh=mesh, in_specs=in_specs, out_specs=out_specs, check_vma=False)
```

```python
import functools
import math

import jax
import jax.numpy as jnp
from jax import lax
from jax.experimental import pallas as pl
from jax.experimental.pallas import tpu as pltpu
from jax.sharding import PartitionSpec as P


HEAD = 64
HALF = 64
TILE = 2 * HALF
STEP = 64
GRANT = 8 * 1024 * 1024
F32 = jnp.float32
BF16 = jnp.bfloat16


def room(shape, dtype):
    lanes = -(-shape[-1] // 128) * 128
    return math.prod(shape[:-1]) * lanes * jnp.dtype(dtype).itemsize


def call(kernel, outs, scratch, *args, loads=0):
    grant = sum(room(s, t) for s, t in scratch) + GRANT
    extra = [pltpu.SemaphoreType.DMA((loads,))] if loads else []
    spaces = [pltpu.VMEM] * (len(args) - loads) + [pltpu.HBM] * loads
    run = pl.pallas_call(
        kernel,
        out_shape=tuple(jax.ShapeDtypeStruct(s, t) for s, t in outs),
        in_specs=[pl.BlockSpec(memory_space=space) for space in spaces],
        scratch_shapes=[pltpu.VMEM(s, t) for s, t in scratch] + extra,
        compiler_params=pltpu.CompilerParams(vmem_limit_bytes=grant),
    )
    if loads:
        far = [pltpu.with_memory_space_constraint(a, pltpu.HBM) for a in args[-loads:]]
        args = args[:-loads] + tuple(far)
    return run(*args)


def nn(a, b):
    return lax.dot_general(a, b, (((1,), (0,)), ((), ())), preferred_element_type=F32)


def tn(a, b):
    return lax.dot_general(a, b, (((0,), (0,)), ((), ())), preferred_element_type=F32)


def nt(a, b):
    return lax.dot_general(a, b, (((1,), (1,)), ((), ())), preferred_element_type=F32)


def row_loop(rows, step, fn, init):
    def one(i, carry):
        return fn(pl.multiple_of(i * step, step), carry)

    return lax.fori_loop(0, rows // step, one, init)


def fold(x):
    return jnp.sum(x.reshape(x.shape[0] // 8, 8, x.shape[1]), axis=0)


def fill_bias(bias, first, length, total):
    shape = (2 * TILE, TILE)
    key = lax.broadcasted_iota(jnp.int32, shape, 0)
    gap = key - lax.broadcasted_iota(jnp.int32, shape, 1)
    near = (gap >= 0) & (gap <= TILE)
    low = key + (first - HALF) >= 0
    high = key + (first + length - TILE - HALF) < total
    if length == TILE:
        low = low & high
    for k, allowed in enumerate((near & low, near, near & high)):
        bias[k] = jnp.where(allowed, 0.0, -1e30)


def bias_of(bias, tile, count):
    if tile == 0:
        return bias[0]
    return bias[2] if tile == count - 1 else bias[1]


def gather_rows(pieces, target, lanes):
    me = lax.axis_index("mp")
    share = pieces[0].shape[0]
    for k, piece in enumerate(pieces):
        start = pl.multiple_of(jnp.bitwise_xor(me, k) * share, share)
        target[pl.ds(start, share), lanes] = piece[...]


def split_half(source, keep, send, index):
    rows = keep.shape[0]

    def one(r, carry):
        mine = pl.multiple_of(index * rows + r, 16)
        other = pl.multiple_of((1 - index) * rows + r, 16)
        keep[pl.ds(r, 16), :] = source[pl.ds(mine, 16), :]
        send[pl.ds(r, 16), :] = source[pl.ds(other, 16), :].astype(send.dtype)
        return carry

    row_loop(rows, 16, one, 0)


def attention_kernel(
    p1, p2, p3, h0, h1, h2, h3, gain, cos, sin, p0_far, w_far, wo_far,
    xall, stats, fed, q, kw, kt, vt, totals, mixed, keep, send,
    proj, terms, p0, w, wo, bias, sems,
):
    copies = [
        pltpu.make_async_copy(p0_far, p0, sems.at[0]),
        pltpu.make_async_copy(w_far, w, sems.at[1]),
        pltpu.make_async_copy(wo_far, wo, sems.at[2]),
    ]
    for copy in copies:
        copy.start()
    width, tokens = xall.shape
    length = q.shape[1]
    columns = q.shape[0]
    heads = columns // HEAD
    core = lax.axis_index("mp") % 2
    first = lax.axis_index("seq") * length
    total = lax.axis_size("seq") * length
    fill_bias(bias, first, length, total)
    gather_rows((h0, h1, h2, h3), xall, slice(length, tokens))
    copies[0].wait()
    gather_rows((p0, p1, p2, p3), xall, slice(0, length))

    def add(r, acc):
        return acc + fold(xall[pl.ds(r, STEP), :].astype(F32))

    zero = jnp.zeros((8, tokens), F32)
    mean = jnp.sum(row_loop(width, STEP, add, zero), axis=0, keepdims=True) / width

    def add_square(r, acc):
        center = xall[pl.ds(r, STEP), :].astype(F32) - mean
        return acc + fold(center * center)

    var = jnp.sum(row_loop(width, STEP, add_square, zero), axis=0, keepdims=True) / width
    inverse = lax.rsqrt(var + 1e-05)
    stats[0:1, :] = mean
    stats[1:2, :] = inverse
    stats[2:8, :] = jnp.zeros((6, tokens), F32)

    def feed(r, carry):
        normed = (xall[pl.ds(r, STEP), :].astype(F32) - mean) * inverse
        fed[pl.ds(r, STEP), :] = (normed * gain[pl.ds(r, STEP), 0:1]).astype(BF16)
        return carry

    row_loop(width, STEP, feed, 0)
    copies[1].wait()
    proj[...] = nn(w[...], fed[...])
    half = HEAD // 2

    def rope(row, lanes):
        a = proj[pl.ds(row, half), lanes]
        b = proj[pl.ds(row + half, half), lanes]
        c = cos[:, lanes]
        s = sin[:, lanes]
        return a * c - b * s, b * c + a * s

    def one_head(h, carry):
        row = h * HEAD
        own = slice(0, length)
        every = slice(0, tokens)
        upper, lower = rope(row, own)
        q[pl.ds(row, half), :] = upper.astype(BF16)
        q[pl.ds(row + half, half), :] = lower.astype(BF16)
        keys = jnp.concatenate(rope(columns + row, every), axis=0)
        keys = pltpu.roll(keys, HALF, 1)
        kw[pl.ds(row, HEAD), :] = keys.astype(BF16)
        kt[h] = keys.T.astype(BF16)
        value = pltpu.roll(proj[pl.ds(2 * columns + row, HEAD), :], HALF, 1)
        vt[h] = value.T.astype(BF16)
        value = value.astype(BF16)
        count = length // TILE
        for j in range(count):
            wide = slice(j * TILE, (j + 2) * TILE)
            mine = slice(j * TILE, (j + 1) * TILE)
            scores = nn(kt[h, wide, :], q[pl.ds(row, HEAD), mine]) * HEAD**-0.5
            scores = scores + bias_of(bias, j, count)
            top = jnp.max(scores, axis=0, keepdims=True)
            raised = jnp.exp(scores - top)
            amount = jnp.sum(raised, axis=0, keepdims=True)
            weights = (raised * (1.0 / amount)).astype(BF16)
            totals[h, 0:1, mine] = top + jnp.log(amount)
            mixed[pl.ds(row, HEAD), mine] = nn(value[:, wide], weights).astype(BF16)
        return carry

    for h in range(heads):
        one_head(h, 0)
    copies[2].wait()
    terms[...] = tn(wo[...], mixed[...])
    split_half(terms, keep, send, core)


def flip_weights_kernel(*refs):
    for source, target in zip(refs[:3], refs[3:]):
        target[...] = source[...].T


def geglu_kernel(
    xall, mine, other, u0, u1, u2, u3, gain, win, win_t, gout,
    middle_own, normed, inverse_out, fed, upstream, product, lifted_grad, keep, send,
    middle, lifted, grad_product, terms,
):
    width, length = normed.shape
    share = middle_own.shape[0]
    units = product.shape[0]
    rows = mine.shape[0]
    me = lax.axis_index("mp")
    core = me % 2
    gather_rows((u0, u1, u2, u3), upstream, slice(0, length))
    own = slice(0, length)

    def add(r, acc):
        for part, index in ((mine, core), (other, 1 - core)):
            at = pl.multiple_of(index * rows + r, STEP)
            value = xall[pl.ds(at, STEP), own].astype(F32) + part[pl.ds(r, STEP), :].astype(F32)
            middle[pl.ds(at, STEP), :] = value
            acc = acc + fold(value)
        return acc

    zero = jnp.zeros((8, length), F32)
    mean = jnp.sum(row_loop(rows, STEP, add, zero), axis=0, keepdims=True) / width

    def add_square(r, acc):
        center = middle[pl.ds(r, STEP), :] - mean
        return acc + fold(center * center)

    var = jnp.sum(row_loop(width, STEP, add_square, zero), axis=0, keepdims=True) / width
    inverse = lax.rsqrt(var + 1e-05)
    inverse_out[...] = jnp.broadcast_to(inverse, inverse_out.shape)

    def feed(r, carry):
        value = (middle[pl.ds(r, STEP), :] - mean) * inverse
        normed[pl.ds(r, STEP), :] = value
        fed[pl.ds(r, STEP), :] = (value * gain[pl.ds(r, STEP), 1:2]).astype(BF16)
        return carry

    row_loop(width, STEP, feed, 0)
    middle_own[...] = middle[pl.ds(pl.multiple_of(me * share, share), share), :]
    lifted[...] = nn(win[...], fed[...])
    grad_product[...] = nn(gout[...], upstream[...])

    def unit(r, carry):
        at = pl.ds(r, 32)
        gate = pl.ds(pl.multiple_of(units + r, 32), 32)
        linear = lifted[at, :]
        gating = lifted[gate, :]
        grad = grad_product[at, :]
        area = 0.5 * (1.0 + lax.erf(linear * 0.7071067811865476))
        activated = linear * area
        slope = area + linear * jnp.exp(-0.5 * linear * linear) * 0.3989422804014327
        product[at, :] = (activated * gating).astype(BF16)
        lifted_grad[at, :] = (grad * gating * slope).astype(BF16)
        lifted_grad[gate, :] = (grad * activated).astype(BF16)
        return carry

    row_loop(units, 32, unit, 0)
    terms[...] = nn(win_t[...], lifted_grad[...])
    split_half(terms, keep, send, core)


def geglu_weights_kernel(product, lifted_grad, fed, upstream, *rest, cuts):
    outs, stack = rest[:-1], rest[-1]
    count = lifted_grad.shape[0]
    units = product.shape[0]
    stack[0:count, :] = nt(lifted_grad[...], fed[...])
    stack[count : count + units, :] = nt(product[...], upstream[...])
    if stack.shape[0] > count + units:
        stack[count + units :, :] = jnp.zeros((stack.shape[0] - count - units, stack.shape[1]), F32)
    emit_units(stack, outs, cuts)


def emit_units(stack, outs, cuts):
    if cuts is None:
        outs[0][...] = stack[...]
        return
    start = 0
    for i, (rows, order) in enumerate(cuts):
        index = lax.axis_index(order[0]) % 2
        split_half(stack.at[pl.ds(start, rows), :], outs[2 * i], outs[2 * i + 1], index)
        start += rows


def attention_back_kernel(
    mine, other, normed, inverse, gain, upstream, wo, q, kw, kt, vt, totals, mixed, cos, sin, fed, *rest,
    cuts,
):
    outs, (full, low, mixed_grad, dk, dv, stack, bias) = rest[:-7], rest[-7:]
    middle_grad_own, gain_grad, proj_grad = outs[:3]
    width, length = normed.shape
    columns = q.shape[0]
    heads = columns // HEAD
    tokens = kw.shape[1]
    rows = mine.shape[0]
    share = middle_grad_own.shape[0]
    me = lax.axis_index("mp")
    core = me % 2
    first = lax.axis_index("seq") * length
    total = lax.axis_size("seq") * length
    inv = inverse[0:1, :]
    fill_bias(bias, first, length, total)

    def add(r, acc):
        a, b = acc
        for part, index in ((mine, core), (other, 1 - core)):
            at = pl.multiple_of(index * rows + r, STEP)
            grad = part[pl.ds(r, STEP), :].astype(F32)
            full[pl.ds(at, STEP), :] = grad
            hat = grad * gain[pl.ds(at, STEP), 1:2]
            a = a + fold(hat)
            b = b + fold(hat * normed[pl.ds(at, STEP), :])
        return a, b

    zero = jnp.zeros((8, length), F32)
    a, b = row_loop(rows, STEP, add, (zero, zero))
    one = jnp.sum(a, axis=0, keepdims=True) / width
    two = jnp.sum(b, axis=0, keepdims=True) / width
    start = pl.multiple_of(me * share, share)
    weighted = full[pl.ds(start, share), :] * normed[pl.ds(start, share), :]
    lanes = weighted[:, 0:128]
    for j in range(1, length // 128):
        lanes = lanes + weighted[:, j * 128 : (j + 1) * 128]
    gain_grad[...] = lanes

    def back(r, carry):
        at = pl.ds(r, STEP)
        hat = full[at, :] * gain[at, 1:2]
        value = upstream[at, :].astype(F32) + inv * (hat - one - normed[at, :] * two)
        full[at, :] = value
        low[at, :] = value.astype(BF16)
        return carry

    row_loop(width, STEP, back, 0)
    middle_grad_own[...] = full[pl.ds(start, share), :]
    mixed_grad[...] = nn(wo[...], low[...]).astype(BF16)
    dk[...] = jnp.zeros(dk.shape, F32)
    dv[...] = jnp.zeros(dv.shape, F32)
    half = HEAD // 2
    every = slice(0, tokens)

    def unrope(a, b, lanes):
        c = cos[:, lanes]
        s = sin[:, lanes]
        return a * c + b * s, b * c - a * s

    def one_head(h, carry):
        row = h * HEAD
        head = pl.ds(row, HEAD)
        for j in range(length // TILE):
            wide = slice(j * TILE, (j + 2) * TILE)
            here = slice(j * TILE, (j + 1) * TILE)
            keys = kw[head, wide]
            query = q[head, here]
            grad = mixed_grad[head, here]
            scores = nn(kt[h, wide, :], query) * HEAD**-0.5
            scores = scores + bias_of(bias, j, length // TILE)
            probs = jnp.exp(scores - totals[h, 0:1, here])
            both = grad.astype(F32) * mixed[head, here].astype(F32)
            delta = jnp.sum(both, axis=0, keepdims=True)
            dv[head, wide] += nt(grad, probs.astype(BF16))
            grad_probs = nn(vt[h, wide, :], grad)
            grad_scores = (probs * (grad_probs - delta) * HEAD**-0.5).astype(BF16)
            dk[head, wide] += nt(query, grad_scores)
            dq = nn(keys, grad_scores)
            upper, lower = unrope(dq[:half], dq[half:], here)
            proj_grad[pl.ds(row, half), here] = upper.astype(BF16)
            proj_grad[pl.ds(row + half, half), here] = lower.astype(BF16)
        proj_grad[head, length:tokens] = jnp.zeros((HEAD, tokens - length), BF16)
        keys_grad = pltpu.roll(dk[head, :], tokens - HALF, 1)
        upper, lower = unrope(keys_grad[:half], keys_grad[half:], every)
        at = columns + row
        proj_grad[pl.ds(at, half), :] = upper.astype(BF16)
        proj_grad[pl.ds(at + half, half), :] = lower.astype(BF16)
        at = 2 * columns + row
        proj_grad[pl.ds(at, HEAD), :] = pltpu.roll(dv[head, :], tokens - HALF, 1).astype(BF16)
        return carry

    for h in range(heads):
        one_head(h, 0)
    stack[0:columns, :] = nt(proj_grad[2 * columns : 3 * columns, :], fed[...])
    stack[columns : 2 * columns, :] = nt(mixed[...], low[...])
    stack[2 * columns : 4 * columns, :] = nt(proj_grad[0 : 2 * columns, :], fed[...])
    emit_units(stack, outs[3:], cuts)


def terms_kernel(
    proj_grad, w, gain, xall, stats, gout, product,
    keep, send, terms,
):
    width, tokens = xall.shape
    share = (keep.shape[0] - 16) // 2
    me = lax.axis_index("mp")
    core = me % 2
    terms[:, 0:tokens] = nn(w[...], proj_grad[...])
    mean = stats[0:1, :]
    inverse = stats[1:2, :]

    def add(r, acc):
        a, b = acc
        at = pl.ds(r, STEP)
        hat = terms[at, 0:tokens] * gain[at, 0:1]
        normed = (xall[at, :].astype(F32) - mean) * inverse
        return a + fold(hat), b + fold(hat * normed)

    zero = jnp.zeros((8, tokens), F32)
    a, b = row_loop(width, STEP, add, (zero, zero))
    one = jnp.sum(a, axis=0, keepdims=True) / width
    two = jnp.sum(b, axis=0, keepdims=True) / width
    terms[:, tokens:] = nn(gout[...], product[...])
    for x in range(2):
        mine = pl.multiple_of((2 * x + core) * share, share)
        other = pl.multiple_of((2 * x + 1 - core) * share, share)
        at = slice(x * share, (x + 1) * share)
        keep[at, :] = terms[pl.ds(mine, share), :]
        send[at, :] = terms[pl.ds(other, share), :].astype(BF16)
    rest = slice(2 * share, 2 * share + 16)
    row = lax.broadcasted_iota(jnp.int32, (16, tokens), 0)
    sums = jnp.where(row == 0, one, jnp.where(row == 1, two, 0.0))
    keep[rest, 0:tokens] = sums
    send[rest, 0:tokens] = sums.astype(BF16)
    keep[rest, tokens:] = jnp.zeros((16, terms.shape[1] - tokens), F32)
    send[rest, tokens:] = jnp.zeros((16, terms.shape[1] - tokens), BF16)


def own_rows_kernel(xall, stats, out):
    share = out.shape[0]
    own = pl.ds(pl.multiple_of(lax.axis_index("mp") * share, share), share)
    out[...] = (xall[own, :].astype(F32) - stats[0:1, :]) * stats[1:2, :]


def across_kernel(keep, got, own, away):
    share = (keep.shape[0] - 16) // 2
    x = lax.axis_index("mp") // 2
    for out, index in ((own, x), (away, 1 - x)):
        at = pl.ds(pl.multiple_of(index * share, share), share)
        out[0:share, :] = (keep[at, :] + got[at, :].astype(F32)).astype(out.dtype)
        last = slice(2 * share, 2 * share + 16)
        out[share : share + 16, :] = (keep[last, :] + got[last, :].astype(F32)).astype(out.dtype)


def finish_kernel(own, got, middle, normed, gain_lanes, layer_out, main, edges, gains):
    share, length = middle.shape
    tokens = normed.shape[1]
    layer_out[...] = middle[...] + own[0:share, tokens:] + got[0:share, tokens:].astype(F32)
    main[...] = own[:, 0:length] + got[:, 0:length].astype(F32)
    edges[...] = own[:, length:tokens] + got[:, length:tokens].astype(F32)
    weighted = gain_lanes[...], main[0:share, :] * normed[:, 0:length]
    last = edges[0:share, :] * normed[:, length:tokens]
    exact = functools.partial(
        lax.dot_general,
        dimension_numbers=(((1,), (1,)), ((), ())),
        precision=lax.Precision.HIGHEST,
        preferred_element_type=F32,
    )
    one = exact(jnp.ones((8, length), F32), weighted[1])
    gains[...] = jnp.zeros(gains.shape, F32)
    gains[0:8, 0:share] = one + exact(jnp.ones((8, tokens - length), F32), last)
    gains[8:16, 0:share] = exact(jnp.ones((8, gain_lanes.shape[1]), F32), weighted[0])


def input_kernel(main, low, high, middle_grad, stats, normed, gain, out):
    share, length = out.shape
    own = pl.ds(pl.multiple_of(lax.axis_index("mp") * share, share), share)
    pad = jnp.zeros((main.shape[0], HALF), F32)
    ends = (
        jnp.concatenate([low[...], pad], axis=1),
        jnp.concatenate([pad, high[...]], axis=1),
    )
    for j in range(length // 128):
        at = slice(j * 128, (j + 1) * 128)
        both = main[:, at]
        if j == 0:
            both = both + ends[0]
        if j == length // 128 - 1:
            both = both + ends[1]
        hat = both[0:share] * gain[own, 0:1]
        one = both[share : share + 1]
        two = both[share + 1 : share + 2]
        out[:, at] = middle_grad[:, at] + stats[1:2, at] * (hat - one - normed[:, at] * two)


def halves_kernel(keep, got, out_keep, out_send, *, axis):
    rows = out_keep.shape[0]
    index = lax.axis_index(axis) % 2

    def one(r, carry):
        mine = pl.ds(pl.multiple_of(index * rows + r, 16), 16)
        other = pl.ds(pl.multiple_of((1 - index) * rows + r, 16), 16)
        at = pl.ds(r, 16)
        out_keep[at, :] = keep[mine, :] + got[mine, :].astype(F32)
        out_send[at, :] = (keep[other, :] + got[other, :].astype(F32)).astype(BF16)
        return carry

    row_loop(rows, 16, one, 0)


def part_kernel(keep, got, rest, out):
    rows = keep.shape[0]
    out[0:rows, :] = (keep[...] + got[...].astype(F32)).astype(BF16)
    out[rows:, :] = rest[...].astype(BF16)


def join_kernel(mine, other, out, *, axis, rows):
    index = lax.axis_index(axis) % 2
    out[pl.ds(pl.multiple_of(index * rows, 16), rows), :] = mine[0:rows, :]
    out[pl.ds(pl.multiple_of((1 - index) * rows, 16), rows), :] = other[0:rows, :]
    if mine.shape[0] > rows:
        rest = mine[rows:, :].astype(F32) + other[rows:, :].astype(F32)
        out[2 * rows :, :] = rest.astype(BF16)


def place_kernel(*refs, cuts, outs):
    count = len(cuts)
    pieces, targets, stack = refs[: 2 * count], refs[2 * count : -1], refs[-1]
    start = 0
    for i, (rows, order) in enumerate(cuts):
        size = rows // 2
        index = lax.axis_index(order[0]) % 2
        for k, at in enumerate((index, 1 - index)):
            at = pl.multiple_of(start + at * size, 16)
            stack[pl.ds(at, size), :] = pieces[2 * i + k][0:size, :].astype(F32)
        start += rows
    for target, spans in zip(targets, outs):
        at = 0
        for begin, size in spans:
            target[at : at + size, :] = stack[begin : begin + size, :]
            at += size


def flip(x, axis, bit):
    count = lax.axis_size(axis)
    return lax.ppermute(x, axis, [(i, i ^ bit) for i in range(count)])


def gather_mp(shard):
    across = flip(shard, "mp", 2)
    beside = flip(shard, "mp", 1)
    return shard, beside, across, flip(across, "mp", 1)


def held(x, other):
    return lax.optimization_barrier((x, other))[0]


def sum_halves(keep, send):
    got = flip(send, "mp", 1)
    half = (keep + got.astype(F32)).astype(BF16)
    across = flip(half, "mp", 2)
    total = (half.astype(F32) + across.astype(F32)).astype(BF16)
    return total, flip(total, "mp", 1), half


def scatter_shards(keep, send):
    rows, lanes = keep.shape
    rows = (rows - 16) // 2 + 16
    got = flip(send, "mp", 1)
    own, away = call(across_kernel, [((rows, lanes), F32), ((rows, lanes), BF16)], [], keep, got)
    return own, flip(away, "mp", 2)


def to_neighbours(low, high):
    count = lax.axis_size("seq")
    if count == 2:
        last = lax.axis_index("seq") == 1
        got = flip(jnp.where(last, low, high), "seq", 1)
        zero = jnp.zeros_like(got)
        return jnp.where(last, zero, got), jnp.where(last, got, zero)
    after = lax.ppermute(low, "seq", [(i + 1, i) for i in range(count - 1)])
    before = lax.ppermute(high, "seq", [(i, i + 1) for i in range(count - 1)])
    return after, before


def staged():
    return lax.axis_size("seq") == 2 and lax.axis_size("dp") == 4


def reduce_unit(keep, send, order, rest=None):
    one, two = order
    rows, width = keep.shape
    got = flip(send, one, 1)
    keep, send = call(
        functools.partial(halves_kernel, axis=two),
        [((rows // 2, width), F32), ((rows // 2, width), BF16)],
        [],
        keep,
        got,
    )
    got = flip(send, two, 1)
    if rest is None:
        part = (keep + got.astype(F32)).astype(BF16)
    else:
        shape = (keep.shape[0] + rest.shape[0], width)
        (part,) = call(part_kernel, [(shape, BF16)], [], keep, got, rest)
    got = flip(part, "dp", 2)
    total = (part.astype(F32) + got.astype(F32)).astype(BF16)
    beside = flip(total, two, 1)
    (half,) = call(
        functools.partial(join_kernel, axis=two, rows=rows // 2),
        [((rows + (0 if rest is None else rest.shape[0]), width), BF16)],
        [],
        total,
        beside,
    )
    return half, flip(half, one, 1)


def reduce_stack(parts, cuts, rest=None):
    if cuts is None:
        return [lax.psum(parts[0], ("dp", "seq"))], rest if rest is None else lax.psum(rest, ("dp", "seq"))
    pieces = []
    for i, (_, order) in enumerate(cuts):
        more = rest if i == len(cuts) - 1 else None
        pieces.extend(reduce_unit(parts[2 * i], parts[2 * i + 1], order, more))
    if rest is not None:
        rest = sum(p[-rest.shape[0] :].astype(F32) for p in pieces[-2:])
    return pieces, rest


def place_stack(pieces, cuts, spans, width):
    sizes = [(sum(size for _, size in span), width) for span in spans]
    if cuts is None:
        return [jnp.concatenate([pieces[0][b : b + n] for b, n in span]) for span in spans]
    kernel = functools.partial(place_kernel, cuts=cuts, outs=spans)
    scratch = [((sum(rows for rows, _ in cuts), width), F32)]
    return call(kernel, [(size, F32) for size in sizes], scratch, *pieces)


def unit_shapes(cuts, rows, width):
    if cuts is None:
        return [((rows, width), F32)]
    shapes = []
    for size, _ in cuts:
        shapes += [((size // 2, width), F32), ((size // 2, width), BF16)]
    return shapes


def body(
    hidden_in,
    cotangent,
    attention_gain,
    feedforward_gain,
    qkv_weight,
    attention_out,
    geglu_in,
    geglu_out,
):
    length, share = hidden_in.shape[1:]
    width = qkv_weight.shape[0]
    columns = qkv_weight.shape[2]
    units = geglu_out.shape[0]
    heads = columns // HEAD
    tokens = length + TILE
    half = width // 2
    orders = (("seq", "dp"), ("dp", "seq"))
    grain = 8 * 16
    x_own = hidden_in[0].T
    u_own = cotangent[0].T
    w = jnp.transpose(qkv_weight, (1, 2, 0)).reshape(3 * columns, width)
    win = jnp.transpose(geglu_in, (1, 2, 0)).reshape(2 * units, width)
    gains = jnp.stack([attention_gain, feedforward_gain], axis=1)

    after, before = to_neighbours(x_own[:, :HALF], x_own[:, length - HALF :])
    x_parts = gather_mp(x_own)
    halo = jnp.concatenate([after, before], axis=1)
    h_parts = gather_mp(halo)
    u_parts = gather_mp(u_own)

    base = (lax.axis_index("seq") * length).astype(jnp.int32)
    spot = jnp.arange(tokens, dtype=jnp.int32)
    spot = jnp.where(spot < length + HALF, spot, spot - tokens) + base
    rates = jnp.exp(jnp.arange(HEAD // 2).astype(F32) * (-2.0 * math.log(10000.0) / HEAD))
    angles = rates[:, None] * spot.astype(F32)[None, :]
    cos, sin = jnp.cos(angles), jnp.sin(angles)

    xall, stats, fed, q, kw, kt, vt, totals, mixed, keep, send = call(
        attention_kernel,
        [
            ((width, tokens), BF16),
            ((8, tokens), F32),
            ((width, tokens), BF16),
            ((columns, length), BF16),
            ((columns, tokens), BF16),
            ((heads, tokens, HEAD), BF16),
            ((heads, tokens, HEAD), BF16),
            ((heads, 8, length), F32),
            ((columns, length), BF16),
            ((half, length), F32),
            ((half, length), BF16),
        ],
        [
            ((3 * columns, tokens), F32),
            ((width, length), F32),
            ((share, length), BF16),
            ((3 * columns, width), BF16),
            ((columns, width), BF16),
            ((3, 2 * TILE, TILE), F32),
        ],
        *x_parts[1:], *h_parts, gains, cos, sin, x_own, w, attention_out,
        loads=3,
    )
    mine, other, half_one = sum_halves(keep, send)
    win_t, w_t, gout_t = call(
        flip_weights_kernel,
        [((width, 2 * units), BF16), ((width, 3 * columns), BF16), ((width, units), BF16)],
        [],
        held(win, half_one), w, geglu_out,
    )
    middle_own, normed, inverse, fed_two, upstream, product, lifted_grad, keep, send = call(
        geglu_kernel,
        [
            ((share, length), F32),
            ((width, length), F32),
            ((8, length), F32),
            ((width, length), BF16),
            ((width, length), BF16),
            ((units, length), BF16),
            ((2 * units, length), BF16),
            ((half, length), F32),
            ((half, length), BF16),
        ],
        [
            ((width, length), F32),
            ((2 * units, length), F32),
            ((units, length), F32),
            ((width, length), F32),
        ],
        xall, mine, other, *u_parts, gains, win, win_t, geglu_out,
    )
    mine, other, half_sent = sum_halves(keep, send)

    (normed_own,) = call(
        own_rows_kernel, [((share, tokens), F32)], [], xall, held(stats, half_sent)
    )
    rows = 3 * units
    padded = -(-rows // grain) * grain if staged() else rows
    geglu_cuts = tuple((padded // 2, order) for order in orders) if staged() else None
    geglu_parts = call(
        functools.partial(geglu_weights_kernel, cuts=geglu_cuts),
        unit_shapes(geglu_cuts, padded, width),
        [((padded, width), F32)],
        held(product, half_sent), lifted_grad, fed_two, upstream,
    )

    back_cuts = None
    if staged() and 4 * columns % grain == 0:
        back_cuts = ((2 * columns, orders[0]),) * 2
    outs = call(
        functools.partial(attention_back_kernel, cuts=back_cuts),
        [((share, length), F32), ((share, 128), F32), ((3 * columns, tokens), BF16)]
        + unit_shapes(back_cuts, 4 * columns, width),
        [
            ((width, length), F32),
            ((width, length), BF16),
            ((columns, length), BF16),
            ((columns, tokens), F32),
            ((columns, tokens), F32),
            ((4 * columns, width), F32),
            ((3, 2 * TILE, TILE), F32),
        ],
        mine, other, normed, inverse, gains, upstream, attention_out,
        q, kw, kt, vt, totals, mixed, cos, sin, fed,
    )
    middle_grad, gain_two_lanes, proj_grad = outs[:3]
    pieces, _ = reduce_stack(geglu_parts, geglu_cuts)
    grad_in, grad_out = place_stack(
        pieces, geglu_cuts, (((0, 2 * units),), ((2 * units, units),)), width
    )
    back_parts = outs[3:]

    lanes = tokens + length
    keep, send = call(
        terms_kernel,
        [((2 * share + 16, lanes), F32), ((2 * share + 16, lanes), BF16)],
        [((width, lanes), F32)],
        proj_grad, w_t, gains, xall, stats, gout_t, product,
    )
    own, got = scatter_shards(keep, send)
    layer_out, main, edges, gain_sums = call(
        finish_kernel,
        [
            ((share, length), F32),
            ((share + 16, length), F32),
            ((share + 16, TILE), F32),
            ((16, width), F32),
        ],
        [],
        own, got, middle_own, normed_own, gain_two_lanes,
    )
    high_add, low_add = to_neighbours(edges[:, HALF:], edges[:, :HALF])
    back_pieces, gain_sums = reduce_stack(back_parts, back_cuts, gain_sums)
    (grad_input,) = call(
        input_kernel,
        [((share, length), F32)],
        [],
        main, low_add, high_add, middle_grad, stats, normed_own, gains,
    )
    grad_qkv, grad_attention_out = place_stack(
        held(back_pieces, (grad_input, layer_out)),
        back_cuts,
        (((2 * columns, 2 * columns), (0, columns)), ((columns, columns),)),
        width,
    )
    return (
        layer_out.T[None],
        grad_input.T[None],
        jnp.transpose(grad_qkv.reshape(3, columns, width), (2, 0, 1)),
        grad_attention_out,
        jnp.transpose(grad_in.reshape(2, units, width), (2, 0, 1)),
        grad_out,
        gain_sums[0, :share],
        gain_sums[8, :share],
    )


def solution(mesh):
    in_specs = (
        P("dp", "seq", "mp"),
        P("dp", "seq", "mp"),
        P(),
        P(),
        P(None, None, "mp"),
        P("mp", None),
        P(None, None, "mp"),
        P("mp", None),
    )
    out_specs = (
        P("dp", "seq", "mp"),
        P("dp", "seq", "mp"),
        P(None, None, "mp"),
        P("mp", None),
        P(None, None, "mp"),
        P("mp", None),
        P("mp"),
        P("mp"),
    )

    return jax.shard_map(body, mesh=mesh, in_specs=in_specs, out_specs=out_specs, check_vma=False)
```

```python
import functools
import math

import jax
import jax.numpy as jnp
from jax import lax
from jax.experimental import pallas as pl
from jax.experimental.pallas import tpu as pltpu
from jax.sharding import PartitionSpec as P


HEAD = 64
HALF = 64
TILE = 2 * HALF
STEP = 64
GRANT = 8 * 1024 * 1024
F32 = jnp.float32
BF16 = jnp.bfloat16


def room(shape, dtype):
    lanes = -(-shape[-1] // 128) * 128
    return math.prod(shape[:-1]) * lanes * jnp.dtype(dtype).itemsize


def call(kernel, outs, scratch, *args, loads=0):
    grant = sum(room(s, t) for s, t in scratch) + GRANT
    extra = [pltpu.SemaphoreType.DMA((loads,))] if loads else []
    spaces = [pltpu.VMEM] * (len(args) - loads) + [pltpu.HBM] * loads
    run = pl.pallas_call(
        kernel,
        out_shape=tuple(jax.ShapeDtypeStruct(s, t) for s, t in outs),
        in_specs=[pl.BlockSpec(memory_space=space) for space in spaces],
        scratch_shapes=[pltpu.VMEM(s, t) for s, t in scratch] + extra,
        compiler_params=pltpu.CompilerParams(vmem_limit_bytes=grant),
    )
    if loads:
        far = [pltpu.with_memory_space_constraint(a, pltpu.HBM) for a in args[-loads:]]
        args = args[:-loads] + tuple(far)
    return run(*args)


def nn(a, b):
    return lax.dot_general(a, b, (((1,), (0,)), ((), ())), preferred_element_type=F32)


def tn(a, b):
    return lax.dot_general(a, b, (((0,), (0,)), ((), ())), preferred_element_type=F32)


def nt(a, b):
    return lax.dot_general(a, b, (((1,), (1,)), ((), ())), preferred_element_type=F32)


def row_loop(rows, step, fn, init):
    def one(i, carry):
        return fn(pl.multiple_of(i * step, step), carry)

    return lax.fori_loop(0, rows // step, one, init)


def step_of(rows):
    return next(step for step in (64, 48, 32, 16) if rows % step == 0)


def fold(x):
    return jnp.sum(x.reshape(x.shape[0] // 8, 8, x.shape[1]), axis=0)


def fill_bias(bias, first, length, total):
    shape = (2 * TILE, TILE)
    key = lax.broadcasted_iota(jnp.int32, shape, 0)
    gap = key - lax.broadcasted_iota(jnp.int32, shape, 1)
    near = (gap >= 0) & (gap <= TILE)
    low = key + (first - HALF) >= 0
    high = key + (first + length - TILE - HALF) < total
    if length == TILE:
        low = low & high
    for k, allowed in enumerate((near & low, near, near & high)):
        bias[k] = jnp.where(allowed, 0.0, -1e30)


def bias_of(bias, tile, count):
    if tile == 0:
        return bias[0]
    return bias[2] if tile == count - 1 else bias[1]


def gather_rows(pieces, target, lanes):
    me = lax.axis_index("mp")
    share = pieces[0].shape[0]
    for k, piece in enumerate(pieces):
        start = pl.multiple_of(jnp.bitwise_xor(me, k) * share, share)
        target[pl.ds(start, share), lanes] = piece[...]


def split_half(source, keep, send, index):
    rows = keep.shape[0]
    step = step_of(rows)

    def one(r, carry):
        mine = pl.multiple_of(index * rows + r, 16)
        other = pl.multiple_of((1 - index) * rows + r, 16)
        keep[pl.ds(r, step), :] = source[pl.ds(mine, step), :]
        send[pl.ds(r, step), :] = source[pl.ds(other, step), :].astype(send.dtype)
        return carry

    row_loop(rows, step, one, 0)


def attention_kernel(
    p1, p2, p3, h0, h1, h2, h3, gain, cos, sin, p0_far, w_far, wo_far,
    xall, stats, fed, q, kw, kt, vt, totals, mixed, keep, send,
    proj, terms, p0, w, wo, bias, sems,
):
    copies = [
        pltpu.make_async_copy(p0_far, p0, sems.at[0]),
        pltpu.make_async_copy(w_far, w, sems.at[1]),
        pltpu.make_async_copy(wo_far, wo, sems.at[2]),
    ]
    for copy in copies:
        copy.start()
    width, tokens = xall.shape
    length = q.shape[1]
    columns = q.shape[0]
    heads = columns // HEAD
    core = lax.axis_index("mp") % 2
    first = lax.axis_index("seq") * length
    total = lax.axis_size("seq") * length
    fill_bias(bias, first, length, total)
    gather_rows((h0, h1, h2, h3), xall, slice(length, tokens))
    copies[0].wait()
    gather_rows((p0, p1, p2, p3), xall, slice(0, length))

    def add(r, acc):
        return acc + fold(xall[pl.ds(r, STEP), :].astype(F32))

    zero = jnp.zeros((8, tokens), F32)
    mean = jnp.sum(row_loop(width, STEP, add, zero), axis=0, keepdims=True) / width

    def add_square(r, acc):
        center = xall[pl.ds(r, STEP), :].astype(F32) - mean
        return acc + fold(center * center)

    var = jnp.sum(row_loop(width, STEP, add_square, zero), axis=0, keepdims=True) / width
    inverse = lax.rsqrt(var + 1e-05)
    stats[0:1, :] = mean
    stats[1:2, :] = inverse
    stats[2:8, :] = jnp.zeros((6, tokens), F32)

    def feed(r, carry):
        normed = (xall[pl.ds(r, STEP), :].astype(F32) - mean) * inverse
        fed[pl.ds(r, STEP), :] = (normed * gain[pl.ds(r, STEP), 0:1]).astype(BF16)
        return carry

    row_loop(width, STEP, feed, 0)
    copies[1].wait()
    proj[...] = nn(w[...], fed[...])
    half = HEAD // 2

    def rope(row, lanes):
        a = proj[pl.ds(row, half), lanes]
        b = proj[pl.ds(row + half, half), lanes]
        c = cos[:, lanes]
        s = sin[:, lanes]
        return a * c - b * s, b * c + a * s

    def one_head(h, carry):
        row = h * HEAD
        own = slice(0, length)
        every = slice(0, tokens)
        upper, lower = rope(row, own)
        q[pl.ds(row, half), :] = upper.astype(BF16)
        q[pl.ds(row + half, half), :] = lower.astype(BF16)
        keys = jnp.concatenate(rope(columns + row, every), axis=0)
        keys = pltpu.roll(keys, HALF, 1)
        kw[pl.ds(row, HEAD), :] = keys.astype(BF16)
        kt[h] = keys.T.astype(BF16)
        value = pltpu.roll(proj[pl.ds(2 * columns + row, HEAD), :], HALF, 1)
        vt[h] = value.T.astype(BF16)
        value = value.astype(BF16)
        count = length // TILE
        for j in range(count):
            wide = slice(j * TILE, (j + 2) * TILE)
            mine = slice(j * TILE, (j + 1) * TILE)
            scores = nn(kt[h, wide, :], q[pl.ds(row, HEAD), mine]) * HEAD**-0.5
            scores = scores + bias_of(bias, j, count)
            top = jnp.max(scores, axis=0, keepdims=True)
            raised = jnp.exp(scores - top)
            amount = jnp.sum(raised, axis=0, keepdims=True)
            weights = (raised * (1.0 / amount)).astype(BF16)
            totals[h, 0:1, mine] = top + jnp.log(amount)
            mixed[pl.ds(row, HEAD), mine] = nn(value[:, wide], weights).astype(BF16)
        return carry

    for h in range(heads):
        one_head(h, 0)
    copies[2].wait()
    terms[...] = tn(wo[...], mixed[...])
    split_half(terms, keep, send, core)


def flip_weights_kernel(*refs):
    for source, target in zip(refs[:3], refs[3:]):
        target[...] = source[...].T


def geglu_kernel(
    xall, mine, other, u0, u1, u2, u3, gain, win, win_t, gout,
    middle_own, normed, inverse_out, fed, upstream, product, lifted_grad, keep, send,
    middle, lifted, grad_product, terms,
):
    width, length = normed.shape
    share = middle_own.shape[0]
    units = product.shape[0]
    rows = mine.shape[0]
    me = lax.axis_index("mp")
    core = me % 2
    gather_rows((u0, u1, u2, u3), upstream, slice(0, length))
    own = slice(0, length)

    def add(r, acc):
        for part, index in ((mine, core), (other, 1 - core)):
            at = pl.multiple_of(index * rows + r, STEP)
            value = xall[pl.ds(at, STEP), own].astype(F32) + part[pl.ds(r, STEP), :].astype(F32)
            middle[pl.ds(at, STEP), :] = value
            acc = acc + fold(value)
        return acc

    zero = jnp.zeros((8, length), F32)
    mean = jnp.sum(row_loop(rows, STEP, add, zero), axis=0, keepdims=True) / width

    def add_square(r, acc):
        center = middle[pl.ds(r, STEP), :] - mean
        return acc + fold(center * center)

    var = jnp.sum(row_loop(width, STEP, add_square, zero), axis=0, keepdims=True) / width
    inverse = lax.rsqrt(var + 1e-05)
    inverse_out[...] = jnp.broadcast_to(inverse, inverse_out.shape)

    def feed(r, carry):
        value = (middle[pl.ds(r, STEP), :] - mean) * inverse
        normed[pl.ds(r, STEP), :] = value
        fed[pl.ds(r, STEP), :] = (value * gain[pl.ds(r, STEP), 1:2]).astype(BF16)
        return carry

    row_loop(width, STEP, feed, 0)
    middle_own[...] = middle[pl.ds(pl.multiple_of(me * share, share), share), :]
    lifted[...] = nn(win[...], fed[...])
    grad_product[...] = nn(gout[...], upstream[...])

    def unit(r, carry):
        at = pl.ds(r, 32)
        gate = pl.ds(pl.multiple_of(units + r, 32), 32)
        linear = lifted[at, :]
        gating = lifted[gate, :]
        grad = grad_product[at, :]
        area = 0.5 * (1.0 + lax.erf(linear * 0.7071067811865476))
        activated = linear * area
        slope = area + linear * jnp.exp(-0.5 * linear * linear) * 0.3989422804014327
        product[at, :] = (activated * gating).astype(BF16)
        lifted_grad[at, :] = (grad * gating * slope).astype(BF16)
        lifted_grad[gate, :] = (grad * activated).astype(BF16)
        return carry

    row_loop(units, 32, unit, 0)
    terms[...] = nn(win_t[...], lifted_grad[...])
    split_half(terms, keep, send, core)


def geglu_weights_kernel(product, lifted_grad, fed, upstream, *rest, cuts):
    outs, stack = rest[:-1], rest[-1]
    count = lifted_grad.shape[0]
    units = product.shape[0]
    stack[0:count, :] = nt(lifted_grad[...], fed[...])
    stack[count : count + units, :] = nt(product[...], upstream[...])
    if stack.shape[0] > count + units:
        stack[count + units :, :] = jnp.zeros((stack.shape[0] - count - units, stack.shape[1]), F32)
    emit_units(stack, outs, cuts)


def emit_units(stack, outs, cuts):
    if cuts is None:
        outs[0][...] = stack[...]
        return
    start = 0
    for i, (rows, order) in enumerate(cuts):
        index = lax.axis_index(order[0]) % 2
        split_half(stack.at[pl.ds(start, rows), :], outs[2 * i], outs[2 * i + 1], index)
        start += rows


def attention_back_kernel(
    mine, other, normed, inverse, gain, upstream, wo, q, kw, kt, vt, totals, mixed, cos, sin, fed, *rest,
    cuts,
):
    outs, (full, low, mixed_grad, dk, dv, stack, bias) = rest[:-7], rest[-7:]
    middle_grad_own, gain_grad, proj_grad = outs[:3]
    width, length = normed.shape
    columns = q.shape[0]
    heads = columns // HEAD
    tokens = kw.shape[1]
    rows = mine.shape[0]
    share = middle_grad_own.shape[0]
    me = lax.axis_index("mp")
    core = me % 2
    first = lax.axis_index("seq") * length
    total = lax.axis_size("seq") * length
    inv = inverse[0:1, :]
    fill_bias(bias, first, length, total)

    def add(r, acc):
        a, b = acc
        for part, index in ((mine, core), (other, 1 - core)):
            at = pl.multiple_of(index * rows + r, STEP)
            grad = part[pl.ds(r, STEP), :].astype(F32)
            full[pl.ds(at, STEP), :] = grad
            hat = grad * gain[pl.ds(at, STEP), 1:2]
            a = a + fold(hat)
            b = b + fold(hat * normed[pl.ds(at, STEP), :])
        return a, b

    zero = jnp.zeros((8, length), F32)
    a, b = row_loop(rows, STEP, add, (zero, zero))
    one = jnp.sum(a, axis=0, keepdims=True) / width
    two = jnp.sum(b, axis=0, keepdims=True) / width
    start = pl.multiple_of(me * share, share)
    weighted = full[pl.ds(start, share), :] * normed[pl.ds(start, share), :]
    lanes = weighted[:, 0:128]
    for j in range(1, length // 128):
        lanes = lanes + weighted[:, j * 128 : (j + 1) * 128]
    gain_grad[...] = lanes

    def back(r, carry):
        at = pl.ds(r, STEP)
        hat = full[at, :] * gain[at, 1:2]
        value = upstream[at, :].astype(F32) + inv * (hat - one - normed[at, :] * two)
        full[at, :] = value
        low[at, :] = value.astype(BF16)
        return carry

    row_loop(width, STEP, back, 0)
    middle_grad_own[...] = full[pl.ds(start, share), :]
    mixed_grad[...] = nn(wo[...], low[...]).astype(BF16)
    dk[...] = jnp.zeros(dk.shape, F32)
    dv[...] = jnp.zeros(dv.shape, F32)
    half = HEAD // 2
    every = slice(0, tokens)

    def unrope(a, b, lanes):
        c = cos[:, lanes]
        s = sin[:, lanes]
        return a * c + b * s, b * c - a * s

    def one_head(h, carry):
        row = h * HEAD
        head = pl.ds(row, HEAD)
        for j in range(length // TILE):
            wide = slice(j * TILE, (j + 2) * TILE)
            here = slice(j * TILE, (j + 1) * TILE)
            keys = kw[head, wide]
            query = q[head, here]
            grad = mixed_grad[head, here]
            scores = nn(kt[h, wide, :], query) * HEAD**-0.5
            scores = scores + bias_of(bias, j, length // TILE)
            probs = jnp.exp(scores - totals[h, 0:1, here])
            both = grad.astype(F32) * mixed[head, here].astype(F32)
            delta = jnp.sum(both, axis=0, keepdims=True)
            dv[head, wide] += nt(grad, probs.astype(BF16))
            grad_probs = nn(vt[h, wide, :], grad)
            grad_scores = (probs * (grad_probs - delta) * HEAD**-0.5).astype(BF16)
            dk[head, wide] += nt(query, grad_scores)
            dq = nn(keys, grad_scores)
            upper, lower = unrope(dq[:half], dq[half:], here)
            proj_grad[pl.ds(row, half), here] = upper.astype(BF16)
            proj_grad[pl.ds(row + half, half), here] = lower.astype(BF16)
        proj_grad[head, length:tokens] = jnp.zeros((HEAD, tokens - length), BF16)
        keys_grad = pltpu.roll(dk[head, :], tokens - HALF, 1)
        upper, lower = unrope(keys_grad[:half], keys_grad[half:], every)
        at = columns + row
        proj_grad[pl.ds(at, half), :] = upper.astype(BF16)
        proj_grad[pl.ds(at + half, half), :] = lower.astype(BF16)
        at = 2 * columns + row
        proj_grad[pl.ds(at, HEAD), :] = pltpu.roll(dv[head, :], tokens - HALF, 1).astype(BF16)
        return carry

    for h in range(heads):
        one_head(h, 0)
    stack[0:columns, :] = nt(proj_grad[2 * columns : 3 * columns, :], fed[...])
    stack[columns : 2 * columns, :] = nt(mixed[...], low[...])
    stack[2 * columns : 4 * columns, :] = nt(proj_grad[0 : 2 * columns, :], fed[...])
    emit_units(stack, outs[3:], cuts)


def terms_kernel(
    proj_grad, w, gain, xall, stats, gout, product,
    keep, send, terms,
):
    width, tokens = xall.shape
    share = (keep.shape[0] - 16) // 2
    me = lax.axis_index("mp")
    core = me % 2
    terms[:, 0:tokens] = nn(w[...], proj_grad[...])
    mean = stats[0:1, :]
    inverse = stats[1:2, :]

    def add(r, acc):
        a, b = acc
        at = pl.ds(r, STEP)
        hat = terms[at, 0:tokens] * gain[at, 0:1]
        normed = (xall[at, :].astype(F32) - mean) * inverse
        return a + fold(hat), b + fold(hat * normed)

    zero = jnp.zeros((8, tokens), F32)
    a, b = row_loop(width, STEP, add, (zero, zero))
    one = jnp.sum(a, axis=0, keepdims=True) / width
    two = jnp.sum(b, axis=0, keepdims=True) / width
    terms[:, tokens:] = nn(gout[...], product[...])
    for x in range(2):
        mine = pl.multiple_of((2 * x + core) * share, share)
        other = pl.multiple_of((2 * x + 1 - core) * share, share)
        at = slice(x * share, (x + 1) * share)
        keep[at, :] = terms[pl.ds(mine, share), :]
        send[at, :] = terms[pl.ds(other, share), :].astype(BF16)
    rest = slice(2 * share, 2 * share + 16)
    row = lax.broadcasted_iota(jnp.int32, (16, tokens), 0)
    sums = jnp.where(row == 0, one, jnp.where(row == 1, two, 0.0))
    keep[rest, 0:tokens] = sums
    send[rest, 0:tokens] = sums.astype(BF16)
    keep[rest, tokens:] = jnp.zeros((16, terms.shape[1] - tokens), F32)
    send[rest, tokens:] = jnp.zeros((16, terms.shape[1] - tokens), BF16)


def own_rows_kernel(xall, stats, out):
    share = out.shape[0]
    own = pl.ds(pl.multiple_of(lax.axis_index("mp") * share, share), share)
    out[...] = (xall[own, :].astype(F32) - stats[0:1, :]) * stats[1:2, :]


def across_kernel(keep, got, own, away):
    share = (keep.shape[0] - 16) // 2
    x = lax.axis_index("mp") // 2
    for out, index in ((own, x), (away, 1 - x)):
        at = pl.ds(pl.multiple_of(index * share, share), share)
        out[0:share, :] = (keep[at, :] + got[at, :].astype(F32)).astype(out.dtype)
        last = slice(2 * share, 2 * share + 16)
        out[share : share + 16, :] = (keep[last, :] + got[last, :].astype(F32)).astype(out.dtype)


def finish_kernel(own, got, middle, normed, gain_lanes, layer_out, main, edges, gains):
    share, length = middle.shape
    tokens = normed.shape[1]
    layer_out[...] = middle[...] + own[0:share, tokens:] + got[0:share, tokens:].astype(F32)
    main[...] = own[:, 0:length] + got[:, 0:length].astype(F32)
    edges[...] = own[:, length:tokens] + got[:, length:tokens].astype(F32)
    weighted = gain_lanes[...], main[0:share, :] * normed[:, 0:length]
    last = edges[0:share, :] * normed[:, length:tokens]
    exact = functools.partial(
        lax.dot_general,
        dimension_numbers=(((1,), (1,)), ((), ())),
        precision=lax.Precision.HIGHEST,
        preferred_element_type=F32,
    )
    one = exact(jnp.ones((8, length), F32), weighted[1])
    gains[...] = jnp.zeros(gains.shape, F32)
    gains[0:8, 0:share] = one + exact(jnp.ones((8, tokens - length), F32), last)
    gains[8:16, 0:share] = exact(jnp.ones((8, gain_lanes.shape[1]), F32), weighted[0])


def input_kernel(main, low, high, middle_grad, stats, normed, gain, out):
    share, length = out.shape
    own = pl.ds(pl.multiple_of(lax.axis_index("mp") * share, share), share)
    pad = jnp.zeros((main.shape[0], HALF), F32)
    ends = (
        jnp.concatenate([low[...], pad], axis=1),
        jnp.concatenate([pad, high[...]], axis=1),
    )
    for j in range(length // 128):
        at = slice(j * 128, (j + 1) * 128)
        both = main[:, at]
        if j == 0:
            both = both + ends[0]
        if j == length // 128 - 1:
            both = both + ends[1]
        hat = both[0:share] * gain[own, 0:1]
        one = both[share : share + 1]
        two = both[share + 1 : share + 2]
        out[:, at] = middle_grad[:, at] + stats[1:2, at] * (hat - one - normed[:, at] * two)


def halves_kernel(keep, got, out_keep, out_send, *, axis):
    rows = out_keep.shape[0]
    index = lax.axis_index(axis) % 2

    def one(r, carry):
        mine = pl.ds(pl.multiple_of(index * rows + r, 16), 16)
        other = pl.ds(pl.multiple_of((1 - index) * rows + r, 16), 16)
        at = pl.ds(r, 16)
        out_keep[at, :] = keep[mine, :] + got[mine, :].astype(F32)
        out_send[at, :] = (keep[other, :] + got[other, :].astype(F32)).astype(BF16)
        return carry

    row_loop(rows, 16, one, 0)


def part_kernel(keep, got, rest, out):
    rows = keep.shape[0]
    out[0:rows, :] = (keep[...] + got[...].astype(F32)).astype(BF16)
    out[rows:, :] = rest[...].astype(BF16)


def join_kernel(mine, other, out, *, axis, rows):
    index = lax.axis_index(axis) % 2
    out[pl.ds(pl.multiple_of(index * rows, 16), rows), :] = mine[0:rows, :]
    out[pl.ds(pl.multiple_of((1 - index) * rows, 16), rows), :] = other[0:rows, :]
    if mine.shape[0] > rows:
        rest = mine[rows:, :].astype(F32) + other[rows:, :].astype(F32)
        out[2 * rows :, :] = rest.astype(BF16)


def place_kernel(*refs, cuts, outs):
    count = len(cuts)
    pieces, targets = refs[: 2 * count], refs[2 * count :]

    def copy(piece, begin, size):
        for target, spans in zip(targets, outs):
            at = 0
            for low, rows in spans:
                start, stop = max(begin, low), min(begin + size, low + rows)
                if start < stop:
                    rows_here = piece[start - begin : stop - begin, :].astype(F32)
                    target[at + start - low : at + stop - low, :] = rows_here
                at += rows

    start = 0
    for i, (rows, order) in enumerate(cuts):
        size = rows // 2
        index = lax.axis_index(order[0]) % 2
        for value in range(2):

            @pl.when(index == value)
            def _(mine=start + value * size, other=start + (1 - value) * size, i=i, size=size):
                copy(pieces[2 * i], mine, size)
                copy(pieces[2 * i + 1], other, size)

        start += rows


def flip(x, axis, bit):
    count = lax.axis_size(axis)
    return lax.ppermute(x, axis, [(i, i ^ bit) for i in range(count)])


def gather_mp(shard):
    across = flip(shard, "mp", 2)
    beside = flip(shard, "mp", 1)
    return shard, beside, across, flip(across, "mp", 1)


def held(x, other):
    return lax.optimization_barrier((x, other))[0]


def sum_halves(keep, send):
    got = flip(send, "mp", 1)
    half = (keep + got.astype(F32)).astype(BF16)
    across = flip(half, "mp", 2)
    total = (half.astype(F32) + across.astype(F32)).astype(BF16)
    return total, flip(total, "mp", 1), half


def scatter_shards(keep, send):
    rows, lanes = keep.shape
    rows = (rows - 16) // 2 + 16
    got = flip(send, "mp", 1)
    own, away = call(across_kernel, [((rows, lanes), F32), ((rows, lanes), BF16)], [], keep, got)
    return own, flip(away, "mp", 2)


def to_neighbours(low, high):
    count = lax.axis_size("seq")
    if count == 2:
        last = lax.axis_index("seq") == 1
        got = flip(jnp.where(last, low, high), "seq", 1)
        zero = jnp.zeros_like(got)
        return jnp.where(last, zero, got), jnp.where(last, got, zero)
    after = lax.ppermute(low, "seq", [(i + 1, i) for i in range(count - 1)])
    before = lax.ppermute(high, "seq", [(i, i + 1) for i in range(count - 1)])
    return after, before


def staged():
    return lax.axis_size("seq") == 2 and lax.axis_size("dp") == 4


def reduce_unit(keep, send, order, rest=None):
    one, two = order
    rows, width = keep.shape
    got = flip(send, one, 1)
    keep, send = call(
        functools.partial(halves_kernel, axis=two),
        [((rows // 2, width), F32), ((rows // 2, width), BF16)],
        [],
        keep,
        got,
    )
    got = flip(send, two, 1)
    if rest is None:
        part = (keep + got.astype(F32)).astype(BF16)
    else:
        shape = (keep.shape[0] + rest.shape[0], width)
        (part,) = call(part_kernel, [(shape, BF16)], [], keep, got, rest)
    got = flip(part, "dp", 2)
    total = (part.astype(F32) + got.astype(F32)).astype(BF16)
    beside = flip(total, two, 1)
    (half,) = call(
        functools.partial(join_kernel, axis=two, rows=rows // 2),
        [((rows + (0 if rest is None else rest.shape[0]), width), BF16)],
        [],
        total,
        beside,
    )
    return half, flip(half, one, 1)


def reduce_stack(parts, cuts, rest=None):
    if cuts is None:
        return [lax.psum(parts[0], ("dp", "seq"))], rest if rest is None else lax.psum(rest, ("dp", "seq"))
    pieces = []
    for i, (_, order) in enumerate(cuts):
        more = rest if i == len(cuts) - 1 else None
        pieces.extend(reduce_unit(parts[2 * i], parts[2 * i + 1], order, more))
    if rest is not None:
        rest = sum(p[-rest.shape[0] :].astype(F32) for p in pieces[-2:])
    return pieces, rest


def place_stack(pieces, cuts, spans, width):
    sizes = [(sum(size for _, size in span), width) for span in spans]
    if cuts is None:
        return [jnp.concatenate([pieces[0][b : b + n] for b, n in span]) for span in spans]
    kernel = functools.partial(place_kernel, cuts=cuts, outs=spans)
    return call(kernel, [(size, F32) for size in sizes], [], *pieces)


def gather_edges(shard):
    low, high = shard[:, :HALF], shard[:, -HALF:]
    if lax.axis_size("seq") != 2:
        after, before = to_neighbours(low, high)
        return gather_mp(jnp.concatenate([after, before], axis=1))
    last = lax.axis_index("seq") == 1
    edge = jnp.where(last, low, high)
    near = flip(edge, "seq", 1)
    count = lax.axis_size("mp")
    pairs = [(i, (i + count) % (2 * count) ^ 2) for i in range(2 * count)]
    far = lax.ppermute(edge, ("seq", "mp"), pairs)
    own, across = (
        jnp.concatenate([jnp.where(last, 0, got), jnp.where(last, got, 0)], axis=1)
        for got in (near, far)
    )
    beside = flip(own, "mp", 1)
    return own, beside, across, flip(across, "mp", 1)


def unit_shapes(cuts, rows, width):
    if cuts is None:
        return [((rows, width), F32)]
    shapes = []
    for size, _ in cuts:
        shapes += [((size // 2, width), F32), ((size // 2, width), BF16)]
    return shapes


def body(
    hidden_in,
    cotangent,
    attention_gain,
    feedforward_gain,
    qkv_weight,
    attention_out,
    geglu_in,
    geglu_out,
):
    length, share = hidden_in.shape[1:]
    width = qkv_weight.shape[0]
    columns = qkv_weight.shape[2]
    units = geglu_out.shape[0]
    heads = columns // HEAD
    tokens = length + TILE
    half = width // 2
    orders = (("seq", "dp"), ("dp", "seq"))
    grain = 8 * 16
    x_own = hidden_in[0].T
    u_own = cotangent[0].T
    w = jnp.transpose(qkv_weight, (1, 2, 0)).reshape(3 * columns, width)
    win = jnp.transpose(geglu_in, (1, 2, 0)).reshape(2 * units, width)
    gains = jnp.stack([attention_gain, feedforward_gain], axis=1)

    h_parts = gather_edges(x_own)
    x_parts = gather_mp(x_own)
    u_parts = gather_mp(u_own)

    base = (lax.axis_index("seq") * length).astype(jnp.int32)
    spot = jnp.arange(tokens, dtype=jnp.int32)
    spot = jnp.where(spot < length + HALF, spot, spot - tokens) + base
    rates = jnp.exp(jnp.arange(HEAD // 2).astype(F32) * (-2.0 * math.log(10000.0) / HEAD))
    angles = rates[:, None] * spot.astype(F32)[None, :]
    cos, sin = jnp.cos(angles), jnp.sin(angles)

    xall, stats, fed, q, kw, kt, vt, totals, mixed, keep, send = call(
        attention_kernel,
        [
            ((width, tokens), BF16),
            ((8, tokens), F32),
            ((width, tokens), BF16),
            ((columns, length), BF16),
            ((columns, tokens), BF16),
            ((heads, tokens, HEAD), BF16),
            ((heads, tokens, HEAD), BF16),
            ((heads, 8, length), F32),
            ((columns, length), BF16),
            ((half, length), F32),
            ((half, length), BF16),
        ],
        [
            ((3 * columns, tokens), F32),
            ((width, length), F32),
            ((share, length), BF16),
            ((3 * columns, width), BF16),
            ((columns, width), BF16),
            ((3, 2 * TILE, TILE), F32),
        ],
        *x_parts[1:], *h_parts, gains, cos, sin, x_own, w, attention_out,
        loads=3,
    )
    mine, other, half_one = sum_halves(keep, send)
    win_t, w_t, gout_t = call(
        flip_weights_kernel,
        [((width, 2 * units), BF16), ((width, 3 * columns), BF16), ((width, units), BF16)],
        [],
        held(win, half_one), w, geglu_out,
    )
    middle_own, normed, inverse, fed_two, upstream, product, lifted_grad, keep, send = call(
        geglu_kernel,
        [
            ((share, length), F32),
            ((width, length), F32),
            ((8, length), F32),
            ((width, length), BF16),
            ((width, length), BF16),
            ((units, length), BF16),
            ((2 * units, length), BF16),
            ((half, length), F32),
            ((half, length), BF16),
        ],
        [
            ((width, length), F32),
            ((2 * units, length), F32),
            ((units, length), F32),
            ((width, length), F32),
        ],
        xall, mine, other, *u_parts, gains, win, win_t, geglu_out,
    )
    mine, other, half_sent = sum_halves(keep, send)

    (normed_own,) = call(
        own_rows_kernel, [((share, tokens), F32)], [], xall, held(stats, half_sent)
    )
    rows = 3 * units
    padded = -(-rows // grain) * grain if staged() else rows
    geglu_cuts = tuple((padded // 2, order) for order in orders) if staged() else None
    geglu_parts = call(
        functools.partial(geglu_weights_kernel, cuts=geglu_cuts),
        unit_shapes(geglu_cuts, padded, width),
        [((padded, width), F32)],
        held(product, half_sent), lifted_grad, fed_two, upstream,
    )

    back_cuts = None
    if staged() and 4 * columns % grain == 0:
        back_cuts = ((2 * columns, orders[0]),) * 2
    outs = call(
        functools.partial(attention_back_kernel, cuts=back_cuts),
        [((share, length), F32), ((share, 128), F32), ((3 * columns, tokens), BF16)]
        + unit_shapes(back_cuts, 4 * columns, width),
        [
            ((width, length), F32),
            ((width, length), BF16),
            ((columns, length), BF16),
            ((columns, tokens), F32),
            ((columns, tokens), F32),
            ((4 * columns, width), F32),
            ((3, 2 * TILE, TILE), F32),
        ],
        mine, other, normed, inverse, gains, upstream, attention_out,
        q, kw, kt, vt, totals, mixed, cos, sin, fed,
    )
    middle_grad, gain_two_lanes, proj_grad = outs[:3]
    pieces, _ = reduce_stack(geglu_parts, geglu_cuts)
    grad_in, grad_out = place_stack(
        pieces, geglu_cuts, (((0, 2 * units),), ((2 * units, units),)), width
    )
    back_parts = outs[3:]

    lanes = tokens + length
    keep, send = call(
        terms_kernel,
        [((2 * share + 16, lanes), F32), ((2 * share + 16, lanes), BF16)],
        [((width, lanes), F32)],
        proj_grad, w_t, gains, xall, stats, gout_t, product,
    )
    own, got = scatter_shards(keep, send)
    layer_out, main, edges, gain_sums = call(
        finish_kernel,
        [
            ((share, length), F32),
            ((share + 16, length), F32),
            ((share + 16, TILE), F32),
            ((16, width), F32),
        ],
        [],
        own, got, middle_own, normed_own, gain_two_lanes,
    )
    high_add, low_add = to_neighbours(edges[:, HALF:], edges[:, :HALF])
    back_pieces, gain_sums = reduce_stack(back_parts, back_cuts, gain_sums)
    (grad_input,) = call(
        input_kernel,
        [((share, length), F32)],
        [],
        main, low_add, high_add, middle_grad, stats, normed_own, gains,
    )
    grad_qkv, grad_attention_out = place_stack(
        held(back_pieces, (grad_input, layer_out)),
        back_cuts,
        (((2 * columns, 2 * columns), (0, columns)), ((columns, columns),)),
        width,
    )
    return (
        layer_out.T[None],
        grad_input.T[None],
        jnp.transpose(grad_qkv.reshape(3, columns, width), (2, 0, 1)),
        grad_attention_out,
        jnp.transpose(grad_in.reshape(2, units, width), (2, 0, 1)),
        grad_out,
        gain_sums[0, :share],
        gain_sums[8, :share],
    )


def solution(mesh):
    in_specs = (
        P("dp", "seq", "mp"),
        P("dp", "seq", "mp"),
        P(),
        P(),
        P(None, None, "mp"),
        P("mp", None),
        P(None, None, "mp"),
        P("mp", None),
    )
    out_specs = (
        P("dp", "seq", "mp"),
        P("dp", "seq", "mp"),
        P(None, None, "mp"),
        P("mp", None),
        P(None, None, "mp"),
        P("mp", None),
        P("mp"),
        P("mp"),
    )

    return jax.shard_map(body, mesh=mesh, in_specs=in_specs, out_specs=out_specs, check_vma=False)
```

```python
import functools
import math

import jax
import jax.numpy as jnp
from jax import lax
from jax.experimental import pallas as pl
from jax.experimental.pallas import tpu as pltpu
from jax.sharding import PartitionSpec as P


HEAD = 64
HALF = 64
TILE = 2 * HALF
STEP = 64
GRANT = 8 * 1024 * 1024
F32 = jnp.float32
BF16 = jnp.bfloat16


def room(shape, dtype):
    lanes = -(-shape[-1] // 128) * 128
    return math.prod(shape[:-1]) * lanes * jnp.dtype(dtype).itemsize


def call(kernel, outs, scratch, *args, loads=0):
    grant = sum(room(s, t) for s, t in scratch) + GRANT
    extra = [pltpu.SemaphoreType.DMA((loads,))] if loads else []
    spaces = [pltpu.VMEM] * (len(args) - loads) + [pltpu.HBM] * loads
    run = pl.pallas_call(
        kernel,
        out_shape=tuple(jax.ShapeDtypeStruct(s, t) for s, t in outs),
        in_specs=[pl.BlockSpec(memory_space=space) for space in spaces],
        scratch_shapes=[pltpu.VMEM(s, t) for s, t in scratch] + extra,
        compiler_params=pltpu.CompilerParams(vmem_limit_bytes=grant),
    )
    if loads:
        far = [pltpu.with_memory_space_constraint(a, pltpu.HBM) for a in args[-loads:]]
        args = args[:-loads] + tuple(far)
    return run(*args)


def nn(a, b):
    return lax.dot_general(a, b, (((1,), (0,)), ((), ())), preferred_element_type=F32)


def tn(a, b):
    return lax.dot_general(a, b, (((0,), (0,)), ((), ())), preferred_element_type=F32)


def nt(a, b):
    return lax.dot_general(a, b, (((1,), (1,)), ((), ())), preferred_element_type=F32)


def row_loop(rows, step, fn, init):
    def one(i, carry):
        return fn(pl.multiple_of(i * step, step), carry)

    return lax.fori_loop(0, rows // step, one, init)


def step_of(rows):
    return next(step for step in (64, 48, 32, 16) if rows % step == 0)


def fold(x):
    return jnp.sum(x.reshape(x.shape[0] // 8, 8, x.shape[1]), axis=0)


def fill_bias(bias, first, length, total):
    shape = (2 * TILE, TILE)
    key = lax.broadcasted_iota(jnp.int32, shape, 0)
    gap = key - lax.broadcasted_iota(jnp.int32, shape, 1)
    near = (gap >= 0) & (gap <= TILE)
    low = key + (first - HALF) >= 0
    high = key + (first + length - TILE - HALF) < total
    if length == TILE:
        low = low & high
    for k, allowed in enumerate((near & low, near, near & high)):
        bias[k] = jnp.where(allowed, 0.0, -1e30)


def bias_of(bias, tile, count):
    if tile == 0:
        return bias[0]
    return bias[2] if tile == count - 1 else bias[1]


def gather_rows(pieces, target, lanes):
    me = lax.axis_index("mp")
    share = pieces[0].shape[0]
    for k, piece in enumerate(pieces):
        start = pl.multiple_of(jnp.bitwise_xor(me, k) * share, share)
        target[pl.ds(start, share), lanes] = piece[...]


def split_half(source, keep, send, index):
    rows = keep.shape[0]
    step = step_of(rows)

    def one(r, carry):
        mine = pl.multiple_of(index * rows + r, 16)
        other = pl.multiple_of((1 - index) * rows + r, 16)
        keep[pl.ds(r, step), :] = source[pl.ds(mine, step), :]
        send[pl.ds(r, step), :] = source[pl.ds(other, step), :].astype(send.dtype)
        return carry

    row_loop(rows, step, one, 0)


def attention_kernel(
    p1, p2, p3, h0, h1, h2, h3, gain, cos, sin, p0_far, w_far, wo_far,
    xall, stats, fed, q, kw, kt, vt, totals, mixed, keep, send,
    proj, terms, p0, w, wo, bias, sems,
):
    copies = [
        pltpu.make_async_copy(p0_far, p0, sems.at[0]),
        pltpu.make_async_copy(w_far, w, sems.at[1]),
        pltpu.make_async_copy(wo_far, wo, sems.at[2]),
    ]
    for copy in copies:
        copy.start()
    width, tokens = xall.shape
    length = q.shape[1]
    columns = q.shape[0]
    heads = columns // HEAD
    core = lax.axis_index("mp") % 2
    first = lax.axis_index("seq") * length
    total = lax.axis_size("seq") * length
    fill_bias(bias, first, length, total)
    gather_rows((h0, h1, h2, h3), xall, slice(length, tokens))
    copies[0].wait()
    gather_rows((p0, p1, p2, p3), xall, slice(0, length))

    def add(r, acc):
        return acc + fold(xall[pl.ds(r, STEP), :].astype(F32))

    zero = jnp.zeros((8, tokens), F32)
    mean = jnp.sum(row_loop(width, STEP, add, zero), axis=0, keepdims=True) / width

    def add_square(r, acc):
        center = xall[pl.ds(r, STEP), :].astype(F32) - mean
        return acc + fold(center * center)

    var = jnp.sum(row_loop(width, STEP, add_square, zero), axis=0, keepdims=True) / width
    inverse = lax.rsqrt(var + 1e-05)
    stats[0:1, :] = mean
    stats[1:2, :] = inverse
    stats[2:8, :] = jnp.zeros((6, tokens), F32)

    def feed(r, carry):
        normed = (xall[pl.ds(r, STEP), :].astype(F32) - mean) * inverse
        fed[pl.ds(r, STEP), :] = (normed * gain[pl.ds(r, STEP), 0:1]).astype(BF16)
        return carry

    row_loop(width, STEP, feed, 0)
    copies[1].wait()
    proj[...] = nn(w[...], fed[...])
    half = HEAD // 2

    def rope(row, lanes):
        a = proj[pl.ds(row, half), lanes]
        b = proj[pl.ds(row + half, half), lanes]
        c = cos[:, lanes]
        s = sin[:, lanes]
        return a * c - b * s, b * c + a * s

    def one_head(h, carry):
        row = h * HEAD
        own = slice(0, length)
        every = slice(0, tokens)
        upper, lower = rope(row, own)
        q[pl.ds(row, half), :] = upper.astype(BF16)
        q[pl.ds(row + half, half), :] = lower.astype(BF16)
        keys = jnp.concatenate(rope(columns + row, every), axis=0)
        keys = pltpu.roll(keys, HALF, 1)
        kw[pl.ds(row, HEAD), :] = keys.astype(BF16)
        kt[h] = keys.T.astype(BF16)
        value = pltpu.roll(proj[pl.ds(2 * columns + row, HEAD), :], HALF, 1)
        vt[h] = value.T.astype(BF16)
        value = value.astype(BF16)
        count = length // TILE
        for j in range(count):
            wide = slice(j * TILE, (j + 2) * TILE)
            mine = slice(j * TILE, (j + 1) * TILE)
            scores = nn(kt[h, wide, :], q[pl.ds(row, HEAD), mine]) * HEAD**-0.5
            scores = scores + bias_of(bias, j, count)
            top = jnp.max(scores, axis=0, keepdims=True)
            raised = jnp.exp(scores - top)
            amount = jnp.sum(raised, axis=0, keepdims=True)
            weights = (raised * (1.0 / amount)).astype(BF16)
            totals[h, 0:1, mine] = top + jnp.log(amount)
            mixed[pl.ds(row, HEAD), mine] = nn(value[:, wide], weights).astype(BF16)
        return carry

    for h in range(heads):
        one_head(h, 0)
    copies[2].wait()
    terms[...] = tn(wo[...], mixed[...])
    split_half(terms, keep, send, core)


def flip_weights_kernel(*refs):
    for source, target in zip(refs[:3], refs[3:]):
        target[...] = source[...].T


def geglu_kernel(
    xall, mine, other, u0, u1, u2, u3, gain, win, win_t, gout,
    middle_own, normed, inverse_out, fed, upstream, product, lifted_grad, keep, send,
    middle, lifted, grad_product, terms,
):
    width, length = normed.shape
    share = middle_own.shape[0]
    units = product.shape[0]
    rows = mine.shape[0]
    me = lax.axis_index("mp")
    core = me % 2
    gather_rows((u0, u1, u2, u3), upstream, slice(0, length))
    own = slice(0, length)

    def add(r, acc):
        for part, index in ((mine, core), (other, 1 - core)):
            at = pl.multiple_of(index * rows + r, STEP)
            value = xall[pl.ds(at, STEP), own].astype(F32) + part[pl.ds(r, STEP), :].astype(F32)
            middle[pl.ds(at, STEP), :] = value
            acc = acc + fold(value)
        return acc

    zero = jnp.zeros((8, length), F32)
    mean = jnp.sum(row_loop(rows, STEP, add, zero), axis=0, keepdims=True) / width

    def add_square(r, acc):
        center = middle[pl.ds(r, STEP), :] - mean
        return acc + fold(center * center)

    var = jnp.sum(row_loop(width, STEP, add_square, zero), axis=0, keepdims=True) / width
    inverse = lax.rsqrt(var + 1e-05)
    inverse_out[...] = jnp.broadcast_to(inverse, inverse_out.shape)

    def feed(r, carry):
        value = (middle[pl.ds(r, STEP), :] - mean) * inverse
        normed[pl.ds(r, STEP), :] = value
        fed[pl.ds(r, STEP), :] = (value * gain[pl.ds(r, STEP), 1:2]).astype(BF16)
        return carry

    row_loop(width, STEP, feed, 0)
    middle_own[...] = middle[pl.ds(pl.multiple_of(me * share, share), share), :]
    lifted[...] = nn(win[...], fed[...])
    grad_product[...] = nn(gout[...], upstream[...])

    def unit(r, carry):
        at = pl.ds(r, 32)
        gate = pl.ds(pl.multiple_of(units + r, 32), 32)
        linear = lifted[at, :]
        gating = lifted[gate, :]
        grad = grad_product[at, :]
        area = 0.5 * (1.0 + lax.erf(linear * 0.7071067811865476))
        activated = linear * area
        slope = area + linear * jnp.exp(-0.5 * linear * linear) * 0.3989422804014327
        product[at, :] = (activated * gating).astype(BF16)
        lifted_grad[at, :] = (grad * gating * slope).astype(BF16)
        lifted_grad[gate, :] = (grad * activated).astype(BF16)
        return carry

    row_loop(units, 32, unit, 0)
    terms[...] = nn(win_t[...], lifted_grad[...])
    split_half(terms, keep, send, core)


def geglu_weights_kernel(product, lifted_grad, fed, upstream, *rest, cuts):
    outs, stack = rest[:-1], rest[-1]
    count = lifted_grad.shape[0]
    units = product.shape[0]
    stack[0:count, :] = nt(lifted_grad[...], fed[...])
    stack[count : count + units, :] = nt(product[...], upstream[...])
    if stack.shape[0] > count + units:
        stack[count + units :, :] = jnp.zeros((stack.shape[0] - count - units, stack.shape[1]), F32)
    emit_units(stack, outs, cuts)


def emit_units(stack, outs, cuts):
    if cuts is None:
        outs[0][...] = stack[...]
        return
    start = 0
    for i, (rows, order) in enumerate(cuts):
        index = lax.axis_index(order[0]) % 2
        split_half(stack.at[pl.ds(start, rows), :], outs[2 * i], outs[2 * i + 1], index)
        start += rows


def attention_back_kernel(
    mine, other, normed, inverse, gain, upstream, wo, q, kw, kt, vt, totals, mixed, cos, sin, fed, *rest,
    cuts,
):
    outs, (full, low, mixed_grad, dk, dv, stack, bias) = rest[:-7], rest[-7:]
    middle_grad_own, gain_grad, proj_grad = outs[:3]
    width, length = normed.shape
    columns = q.shape[0]
    heads = columns // HEAD
    tokens = kw.shape[1]
    rows = mine.shape[0]
    share = middle_grad_own.shape[0]
    me = lax.axis_index("mp")
    core = me % 2
    first = lax.axis_index("seq") * length
    total = lax.axis_size("seq") * length
    inv = inverse[0:1, :]
    fill_bias(bias, first, length, total)

    def add(r, acc):
        a, b = acc
        for part, index in ((mine, core), (other, 1 - core)):
            at = pl.multiple_of(index * rows + r, STEP)
            grad = part[pl.ds(r, STEP), :].astype(F32)
            full[pl.ds(at, STEP), :] = grad
            hat = grad * gain[pl.ds(at, STEP), 1:2]
            a = a + fold(hat)
            b = b + fold(hat * normed[pl.ds(at, STEP), :])
        return a, b

    zero = jnp.zeros((8, length), F32)
    a, b = row_loop(rows, STEP, add, (zero, zero))
    one = jnp.sum(a, axis=0, keepdims=True) / width
    two = jnp.sum(b, axis=0, keepdims=True) / width
    start = pl.multiple_of(me * share, share)
    weighted = full[pl.ds(start, share), :] * normed[pl.ds(start, share), :]
    lanes = weighted[:, 0:128]
    for j in range(1, length // 128):
        lanes = lanes + weighted[:, j * 128 : (j + 1) * 128]
    gain_grad[...] = lanes

    def back(r, carry):
        at = pl.ds(r, STEP)
        hat = full[at, :] * gain[at, 1:2]
        value = upstream[at, :].astype(F32) + inv * (hat - one - normed[at, :] * two)
        full[at, :] = value
        low[at, :] = value.astype(BF16)
        return carry

    row_loop(width, STEP, back, 0)
    middle_grad_own[...] = full[pl.ds(start, share), :]
    mixed_grad[...] = nn(wo[...], low[...]).astype(BF16)
    dk[...] = jnp.zeros(dk.shape, F32)
    dv[...] = jnp.zeros(dv.shape, F32)
    half = HEAD // 2
    every = slice(0, tokens)

    def unrope(a, b, lanes):
        c = cos[:, lanes]
        s = sin[:, lanes]
        return a * c + b * s, b * c - a * s

    def one_head(h, carry):
        row = h * HEAD
        head = pl.ds(row, HEAD)
        for j in range(length // TILE):
            wide = slice(j * TILE, (j + 2) * TILE)
            here = slice(j * TILE, (j + 1) * TILE)
            keys = kw[head, wide]
            query = q[head, here]
            grad = mixed_grad[head, here]
            scores = nn(kt[h, wide, :], query) * HEAD**-0.5
            scores = scores + bias_of(bias, j, length // TILE)
            probs = jnp.exp(scores - totals[h, 0:1, here])
            both = grad.astype(F32) * mixed[head, here].astype(F32)
            delta = jnp.sum(both, axis=0, keepdims=True)
            dv[head, wide] += nt(grad, probs.astype(BF16))
            grad_probs = nn(vt[h, wide, :], grad)
            grad_scores = (probs * (grad_probs - delta) * HEAD**-0.5).astype(BF16)
            dk[head, wide] += nt(query, grad_scores)
            dq = nn(keys, grad_scores)
            upper, lower = unrope(dq[:half], dq[half:], here)
            proj_grad[pl.ds(row, half), here] = upper.astype(BF16)
            proj_grad[pl.ds(row + half, half), here] = lower.astype(BF16)
        proj_grad[head, length:tokens] = jnp.zeros((HEAD, tokens - length), BF16)
        keys_grad = pltpu.roll(dk[head, :], tokens - HALF, 1)
        upper, lower = unrope(keys_grad[:half], keys_grad[half:], every)
        at = columns + row
        proj_grad[pl.ds(at, half), :] = upper.astype(BF16)
        proj_grad[pl.ds(at + half, half), :] = lower.astype(BF16)
        at = 2 * columns + row
        proj_grad[pl.ds(at, HEAD), :] = pltpu.roll(dv[head, :], tokens - HALF, 1).astype(BF16)
        return carry

    for h in range(heads):
        one_head(h, 0)
    stack[0:columns, :] = nt(proj_grad[2 * columns : 3 * columns, :], fed[...])
    stack[columns : 2 * columns, :] = nt(mixed[...], low[...])
    stack[2 * columns : 4 * columns, :] = nt(proj_grad[0 : 2 * columns, :], fed[...])
    emit_units(stack, outs[3:], cuts)


def terms_kernel(
    proj_grad, w, gain, xall, stats, gout, product,
    keep, send, terms,
):
    width, tokens = xall.shape
    share = (keep.shape[0] - 16) // 2
    me = lax.axis_index("mp")
    core = me % 2
    terms[:, 0:tokens] = nn(w[...], proj_grad[...])
    mean = stats[0:1, :]
    inverse = stats[1:2, :]

    def add(r, acc):
        a, b = acc
        at = pl.ds(r, STEP)
        hat = terms[at, 0:tokens] * gain[at, 0:1]
        normed = (xall[at, :].astype(F32) - mean) * inverse
        return a + fold(hat), b + fold(hat * normed)

    zero = jnp.zeros((8, tokens), F32)
    a, b = row_loop(width, STEP, add, (zero, zero))
    one = jnp.sum(a, axis=0, keepdims=True) / width
    two = jnp.sum(b, axis=0, keepdims=True) / width
    terms[:, tokens:] = nn(gout[...], product[...])
    for x in range(2):
        mine = pl.multiple_of((2 * x + core) * share, share)
        other = pl.multiple_of((2 * x + 1 - core) * share, share)
        at = slice(x * share, (x + 1) * share)
        keep[at, :] = terms[pl.ds(mine, share), :]
        send[at, :] = terms[pl.ds(other, share), :].astype(BF16)
    rest = slice(2 * share, 2 * share + 16)
    row = lax.broadcasted_iota(jnp.int32, (16, tokens), 0)
    sums = jnp.where(row == 0, one, jnp.where(row == 1, two, 0.0))
    keep[rest, 0:tokens] = sums
    send[rest, 0:tokens] = sums.astype(BF16)
    keep[rest, tokens:] = jnp.zeros((16, terms.shape[1] - tokens), F32)
    send[rest, tokens:] = jnp.zeros((16, terms.shape[1] - tokens), BF16)


def own_rows_kernel(xall, stats, out):
    share = out.shape[0]
    own = pl.ds(pl.multiple_of(lax.axis_index("mp") * share, share), share)
    out[...] = (xall[own, :].astype(F32) - stats[0:1, :]) * stats[1:2, :]


def across_kernel(keep, got, own, away):
    share = (keep.shape[0] - 16) // 2
    x = lax.axis_index("mp") // 2
    for out, index in ((own, x), (away, 1 - x)):
        at = pl.ds(pl.multiple_of(index * share, share), share)
        out[0:share, :] = (keep[at, :] + got[at, :].astype(F32)).astype(out.dtype)
        last = slice(2 * share, 2 * share + 16)
        out[share : share + 16, :] = (keep[last, :] + got[last, :].astype(F32)).astype(out.dtype)


def finish_kernel(own, got, middle, normed, gain_lanes, layer_out, main, edges, gains):
    share, length = middle.shape
    tokens = normed.shape[1]
    layer_out[...] = middle[...] + own[0:share, tokens:] + got[0:share, tokens:].astype(F32)
    main[...] = own[:, 0:length] + got[:, 0:length].astype(F32)
    edges[...] = own[:, length:tokens] + got[:, length:tokens].astype(F32)
    weighted = gain_lanes[...], main[0:share, :] * normed[:, 0:length]
    last = edges[0:share, :] * normed[:, length:tokens]
    rows_of = functools.partial(
        lax.dot_general,
        dimension_numbers=(((1,), (1,)), ((), ())),
        preferred_element_type=F32,
    )
    one = rows_of(jnp.ones((8, length), F32), weighted[1])
    gains[...] = jnp.zeros(gains.shape, F32)
    gains[0:8, 0:share] = one + rows_of(jnp.ones((8, tokens - length), F32), last)
    gains[8:16, 0:share] = rows_of(jnp.ones((8, gain_lanes.shape[1]), F32), weighted[0])


def input_kernel(main, low, high, middle_grad, stats, normed, gain, out):
    share, length = out.shape
    own = pl.ds(pl.multiple_of(lax.axis_index("mp") * share, share), share)
    pad = jnp.zeros((main.shape[0], HALF), F32)
    ends = (
        jnp.concatenate([low[...], pad], axis=1),
        jnp.concatenate([pad, high[...]], axis=1),
    )
    for j in range(length // 128):
        at = slice(j * 128, (j + 1) * 128)
        both = main[:, at]
        if j == 0:
            both = both + ends[0]
        if j == length // 128 - 1:
            both = both + ends[1]
        hat = both[0:share] * gain[own, 0:1]
        one = both[share : share + 1]
        two = both[share + 1 : share + 2]
        out[:, at] = middle_grad[:, at] + stats[1:2, at] * (hat - one - normed[:, at] * two)


def halves_kernel(keep, got, out_keep, out_send, *, axis):
    rows = out_keep.shape[0]
    index = lax.axis_index(axis) % 2

    def one(r, carry):
        mine = pl.ds(pl.multiple_of(index * rows + r, 16), 16)
        other = pl.ds(pl.multiple_of((1 - index) * rows + r, 16), 16)
        at = pl.ds(r, 16)
        out_keep[at, :] = keep[mine, :] + got[mine, :].astype(F32)
        out_send[at, :] = (keep[other, :] + got[other, :].astype(F32)).astype(BF16)
        return carry

    row_loop(rows, 16, one, 0)


def part_kernel(keep, got, rest, out):
    rows = keep.shape[0]
    out[0:rows, :] = (keep[...] + got[...].astype(F32)).astype(BF16)
    out[rows:, :] = rest[...].astype(BF16)


def join_kernel(mine, other, out, *, axis, rows):
    index = lax.axis_index(axis) % 2
    out[pl.ds(pl.multiple_of(index * rows, 16), rows), :] = mine[0:rows, :]
    out[pl.ds(pl.multiple_of((1 - index) * rows, 16), rows), :] = other[0:rows, :]
    if mine.shape[0] > rows:
        rest = mine[rows:, :].astype(F32) + other[rows:, :].astype(F32)
        out[2 * rows :, :] = rest.astype(BF16)


def place_kernel(*refs, cuts, outs):
    count = len(cuts)
    pieces, targets = refs[: 2 * count], refs[2 * count :]

    def copy(piece, begin, size):
        for target, spans in zip(targets, outs):
            at = 0
            for low, rows in spans:
                start, stop = max(begin, low), min(begin + size, low + rows)
                if start < stop:
                    rows_here = piece[start - begin : stop - begin, :].astype(F32)
                    target[at + start - low : at + stop - low, :] = rows_here
                at += rows

    start = 0
    for i, (rows, order) in enumerate(cuts):
        size = rows // 2
        index = lax.axis_index(order[0]) % 2
        for value in range(2):

            @pl.when(index == value)
            def _(mine=start + value * size, other=start + (1 - value) * size, i=i, size=size):
                copy(pieces[2 * i], mine, size)
                copy(pieces[2 * i + 1], other, size)

        start += rows


def flip(x, axis, bit):
    count = lax.axis_size(axis)
    return lax.ppermute(x, axis, [(i, i ^ bit) for i in range(count)])


def gather_mp(shard):
    across = flip(shard, "mp", 2)
    beside = flip(shard, "mp", 1)
    return shard, beside, across, flip(across, "mp", 1)


def held(x, other):
    return lax.optimization_barrier((x, other))[0]


def sum_halves(keep, send):
    got = flip(send, "mp", 1)
    half = (keep + got.astype(F32)).astype(BF16)
    across = flip(half, "mp", 2)
    total = (half.astype(F32) + across.astype(F32)).astype(BF16)
    return total, flip(total, "mp", 1), half


def scatter_shards(keep, send):
    rows, lanes = keep.shape
    rows = (rows - 16) // 2 + 16
    got = flip(send, "mp", 1)
    own, away = call(across_kernel, [((rows, lanes), F32), ((rows, lanes), BF16)], [], keep, got)
    return own, flip(away, "mp", 2)


def to_neighbours(low, high):
    count = lax.axis_size("seq")
    if count == 2:
        last = lax.axis_index("seq") == 1
        got = flip(jnp.where(last, low, high), "seq", 1)
        zero = jnp.zeros_like(got)
        return jnp.where(last, zero, got), jnp.where(last, got, zero)
    after = lax.ppermute(low, "seq", [(i + 1, i) for i in range(count - 1)])
    before = lax.ppermute(high, "seq", [(i, i + 1) for i in range(count - 1)])
    return after, before


def staged():
    return lax.axis_size("seq") == 2 and lax.axis_size("dp") == 4


def reduce_unit(keep, send, order, rest=None):
    one, two = order
    rows, width = keep.shape
    got = flip(send, one, 1)
    keep, send = call(
        functools.partial(halves_kernel, axis=two),
        [((rows // 2, width), F32), ((rows // 2, width), BF16)],
        [],
        keep,
        got,
    )
    got = flip(send, two, 1)
    if rest is None:
        part = (keep + got.astype(F32)).astype(BF16)
    else:
        shape = (keep.shape[0] + rest.shape[0], width)
        (part,) = call(part_kernel, [(shape, BF16)], [], keep, got, rest)
    got = flip(part, "dp", 2)
    total = (part.astype(F32) + got.astype(F32)).astype(BF16)
    beside = flip(total, two, 1)
    (half,) = call(
        functools.partial(join_kernel, axis=two, rows=rows // 2),
        [((rows + (0 if rest is None else rest.shape[0]), width), BF16)],
        [],
        total,
        beside,
    )
    return half, flip(half, one, 1)


def reduce_stack(parts, cuts, rest=None):
    if cuts is None:
        return [lax.psum(parts[0], ("dp", "seq"))], rest if rest is None else lax.psum(rest, ("dp", "seq"))
    pieces = []
    for i, (_, order) in enumerate(cuts):
        more = rest if i == len(cuts) - 1 else None
        pieces.extend(reduce_unit(parts[2 * i], parts[2 * i + 1], order, more))
    if rest is not None:
        rest = sum(p[-rest.shape[0] :].astype(F32) for p in pieces[-2:])
    return pieces, rest


def place_stack(pieces, cuts, spans, width):
    sizes = [(sum(size for _, size in span), width) for span in spans]
    if cuts is None:
        return [jnp.concatenate([pieces[0][b : b + n] for b, n in span]) for span in spans]
    kernel = functools.partial(place_kernel, cuts=cuts, outs=spans)
    return call(kernel, [(size, F32) for size in sizes], [], *pieces)


def gather_edges(shard):
    low, high = shard[:, :HALF], shard[:, -HALF:]
    if lax.axis_size("seq") != 2:
        after, before = to_neighbours(low, high)
        return gather_mp(jnp.concatenate([after, before], axis=1))
    last = lax.axis_index("seq") == 1
    edge = jnp.where(last, low, high)
    near = flip(edge, "seq", 1)
    count = lax.axis_size("mp")
    pairs = [(i, (i + count) % (2 * count) ^ 2) for i in range(2 * count)]
    far = lax.ppermute(edge, ("seq", "mp"), pairs)
    own, across = (
        jnp.concatenate([jnp.where(last, 0, got), jnp.where(last, got, 0)], axis=1)
        for got in (near, far)
    )
    beside = flip(own, "mp", 1)
    return own, beside, across, flip(across, "mp", 1)


def unit_shapes(cuts, rows, width):
    if cuts is None:
        return [((rows, width), F32)]
    shapes = []
    for size, _ in cuts:
        shapes += [((size // 2, width), F32), ((size // 2, width), BF16)]
    return shapes


def body(
    hidden_in,
    cotangent,
    attention_gain,
    feedforward_gain,
    qkv_weight,
    attention_out,
    geglu_in,
    geglu_out,
):
    length, share = hidden_in.shape[1:]
    width = qkv_weight.shape[0]
    columns = qkv_weight.shape[2]
    units = geglu_out.shape[0]
    heads = columns // HEAD
    tokens = length + TILE
    half = width // 2
    orders = (("seq", "dp"), ("dp", "seq"))
    grain = 8 * 16
    x_own = hidden_in[0].T
    u_own = cotangent[0].T
    w = jnp.transpose(qkv_weight, (1, 2, 0)).reshape(3 * columns, width)
    win = jnp.transpose(geglu_in, (1, 2, 0)).reshape(2 * units, width)
    gains = jnp.stack([attention_gain, feedforward_gain], axis=1)

    h_parts = gather_edges(x_own)
    x_parts = gather_mp(x_own)
    u_parts = gather_mp(u_own)

    base = (lax.axis_index("seq") * length).astype(jnp.int32)
    spot = jnp.arange(tokens, dtype=jnp.int32)
    spot = jnp.where(spot < length + HALF, spot, spot - tokens) + base
    rates = jnp.exp(jnp.arange(HEAD // 2).astype(F32) * (-2.0 * math.log(10000.0) / HEAD))
    angles = rates[:, None] * spot.astype(F32)[None, :]
    cos, sin = jnp.cos(angles), jnp.sin(angles)

    xall, stats, fed, q, kw, kt, vt, totals, mixed, keep, send = call(
        attention_kernel,
        [
            ((width, tokens), BF16),
            ((8, tokens), F32),
            ((width, tokens), BF16),
            ((columns, length), BF16),
            ((columns, tokens), BF16),
            ((heads, tokens, HEAD), BF16),
            ((heads, tokens, HEAD), BF16),
            ((heads, 8, length), F32),
            ((columns, length), BF16),
            ((half, length), F32),
            ((half, length), BF16),
        ],
        [
            ((3 * columns, tokens), F32),
            ((width, length), F32),
            ((share, length), BF16),
            ((3 * columns, width), BF16),
            ((columns, width), BF16),
            ((3, 2 * TILE, TILE), F32),
        ],
        *x_parts[1:], *h_parts, gains, cos, sin, x_own, w, attention_out,
        loads=3,
    )
    mine, other, half_one = sum_halves(keep, send)
    win_t, w_t, gout_t = call(
        flip_weights_kernel,
        [((width, 2 * units), BF16), ((width, 3 * columns), BF16), ((width, units), BF16)],
        [],
        held(win, half_one), w, geglu_out,
    )
    middle_own, normed, inverse, fed_two, upstream, product, lifted_grad, keep, send = call(
        geglu_kernel,
        [
            ((share, length), F32),
            ((width, length), F32),
            ((8, length), F32),
            ((width, length), BF16),
            ((width, length), BF16),
            ((units, length), BF16),
            ((2 * units, length), BF16),
            ((half, length), F32),
            ((half, length), BF16),
        ],
        [
            ((width, length), F32),
            ((2 * units, length), F32),
            ((units, length), F32),
            ((width, length), F32),
        ],
        xall, mine, other, *u_parts, gains, win, win_t, geglu_out,
    )
    mine, other, half_sent = sum_halves(keep, send)

    (normed_own,) = call(
        own_rows_kernel, [((share, tokens), F32)], [], xall, held(stats, half_sent)
    )
    rows = 3 * units
    padded = -(-rows // grain) * grain if staged() else rows
    geglu_cuts = tuple((padded // 2, order) for order in orders) if staged() else None
    geglu_parts = call(
        functools.partial(geglu_weights_kernel, cuts=geglu_cuts),
        unit_shapes(geglu_cuts, padded, width),
        [((padded, width), F32)],
        held(product, half_sent), lifted_grad, fed_two, upstream,
    )

    back_cuts = None
    if staged() and 4 * columns % grain == 0:
        back_cuts = ((2 * columns, orders[0]),) * 2
    outs = call(
        functools.partial(attention_back_kernel, cuts=back_cuts),
        [((share, length), F32), ((share, 128), F32), ((3 * columns, tokens), BF16)]
        + unit_shapes(back_cuts, 4 * columns, width),
        [
            ((width, length), F32),
            ((width, length), BF16),
            ((columns, length), BF16),
            ((columns, tokens), F32),
            ((columns, tokens), F32),
            ((4 * columns, width), F32),
            ((3, 2 * TILE, TILE), F32),
        ],
        mine, other, normed, inverse, gains, upstream, attention_out,
        q, kw, kt, vt, totals, mixed, cos, sin, fed,
    )
    middle_grad, gain_two_lanes, proj_grad = outs[:3]
    pieces, _ = reduce_stack(geglu_parts, geglu_cuts)
    grad_in, grad_out = place_stack(
        pieces, geglu_cuts, (((0, 2 * units),), ((2 * units, units),)), width
    )
    back_parts = outs[3:]

    lanes = tokens + length
    keep, send = call(
        terms_kernel,
        [((2 * share + 16, lanes), F32), ((2 * share + 16, lanes), BF16)],
        [((width, lanes), F32)],
        proj_grad, w_t, gains, xall, stats, gout_t, product,
    )
    own, got = scatter_shards(keep, send)
    layer_out, main, edges, gain_sums = call(
        finish_kernel,
        [
            ((share, length), F32),
            ((share + 16, length), F32),
            ((share + 16, TILE), F32),
            ((16, width), F32),
        ],
        [],
        own, got, middle_own, normed_own, gain_two_lanes,
    )
    high_add, low_add = to_neighbours(edges[:, HALF:], edges[:, :HALF])
    back_pieces, gain_sums = reduce_stack(back_parts, back_cuts, gain_sums)
    (grad_input,) = call(
        input_kernel,
        [((share, length), F32)],
        [],
        main, low_add, high_add, middle_grad, stats, normed_own, gains,
    )
    grad_qkv, grad_attention_out = place_stack(
        held(back_pieces, (grad_input, layer_out)),
        back_cuts,
        (((2 * columns, 2 * columns), (0, columns)), ((columns, columns),)),
        width,
    )
    return (
        layer_out.T[None],
        grad_input.T[None],
        jnp.transpose(grad_qkv.reshape(3, columns, width), (2, 0, 1)),
        grad_attention_out,
        jnp.transpose(grad_in.reshape(2, units, width), (2, 0, 1)),
        grad_out,
        gain_sums[0, :share],
        gain_sums[8, :share],
    )


def solution(mesh):
    in_specs = (
        P("dp", "seq", "mp"),
        P("dp", "seq", "mp"),
        P(),
        P(),
        P(None, None, "mp"),
        P("mp", None),
        P(None, None, "mp"),
        P("mp", None),
    )
    out_specs = (
        P("dp", "seq", "mp"),
        P("dp", "seq", "mp"),
        P(None, None, "mp"),
        P("mp", None),
        P(None, None, "mp"),
        P("mp", None),
        P("mp"),
        P("mp"),
    )

    return jax.shard_map(body, mesh=mesh, in_specs=in_specs, out_specs=out_specs, check_vma=False)
```
